32 devices in a mesh: bx: 4 (over z), by: 8 (over y, x, core).
Axes of the slice: x: 2, y: 2, z: 4, core: 2. Of those that a mesh axis runs over, the one named last changes fastest.
Arguments:
- flow: float32 [5, 32, 128, 128], P(None, 'bx', 'by'), as said below
- adjoint: float32 [5, 32, 128, 128], P(None, 'bx', 'by'), may hold values from -6 to 6
- faces: float32 [6, 3, 32, 128, 128], P(None, None, 'bx', 'by'), may hold values from -6 to 6
- decay: float32 [32, 128, 128], P('bx', 'by'), may hold values from 0.2 to 1
- surface_mask: int32 [32, 128, 128], P('bx', 'by'), may hold values 0 or 1
Outputs:
- adjoint_product: float32 [5, 32, 128, 128], P(None, 'bx', 'by')
- warp_adjoint: float32 [3, 32, 128, 128], P(None, 'bx', 'by')
The draws below stay inside these ranges and needn't reach their ends.
Inputs may be any that keep to these rules, and one draw needn't show every extreme that they name: `flow`: density between 0.5 and 2 and pressure between 0.5 and 2, up to rounding.
All inputs are finite; a program needn't handle non-finite values. No bound on the sum of `surface_mask` on one device may be relied on, other than what follows from the above.
Results may differ from the reference program's by a relative error of at most 0.00019.
Values sent between devices are 32-bit elements; how exact they have to be, the bound alone decides.
No kernel may reach another device: no remote copies, remote signals or barrier semaphores. Data moves between devices by JAX's collectives and lax.ppermute only.
A program may use at most 64 MiB of HBM per device.

```python
import math
import jax
import jax.numpy as jnp
from jax import lax

CJ = 16
SWEEPS = 4
NX = 32
SECOND_AXIS_SIZE = 128
NZ = 128


def draw_flow(key, part):
    lattice_extents = (NX, SECOND_AXIS_SIZE, NZ)
    key_density = jax.random.fold_in(key, 11)
    speed_sampling_seed = jax.random.fold_in(key, 12)
    key_pressure = jax.random.fold_in(key, 13)
    density = jnp.exp(jax.random.uniform(key_density, lattice_extents, jnp.float32, math.log(0.5), math.log(2.0)))
    velocity = 0.5 * jax.random.normal(speed_sampling_seed, (3,) + lattice_extents, jnp.float32)
    pressure = jnp.exp(jax.random.uniform(key_pressure, lattice_extents, jnp.float32, math.log(0.5), math.log(2.0)))
    momentum_field = density[None] * velocity
    energy = pressure / 0.4 + 0.5 * jnp.sum(momentum_field * momentum_field, axis=0) / density
    return jnp.concatenate([density[None], momentum_field, energy[None]], axis=0)


def draw_decay(key, part):
    lattice_extents = (NX, SECOND_AXIS_SIZE, NZ)
    key_column = jax.random.fold_in(key, 21)
    key_coin = jax.random.fold_in(key, 22)
    key_jitter = jax.random.fold_in(key, 23)
    spike_sampling_seed = jax.random.fold_in(key, 24)
    dropout_random_key = jax.random.fold_in(key, 25)
    column_draw = jax.random.uniform(key_column, (NX, 1, NZ), jnp.float32)
    coin_value = jax.random.randint(key_coin, (NX, 1, NZ), 0, 10)
    slow_column = coin_value < 5
    slow_scale = 2.0 * SECOND_AXIS_SIZE * jnp.exp(column_draw * math.log(8.0))
    fast_scale = 0.5 * CJ * jnp.exp(column_draw * math.log(6.0))
    jitter = jnp.exp(jax.random.uniform(key_jitter, lattice_extents, jnp.float32, math.log(0.7), math.log(1.4)))
    scale_length = jnp.where(slow_column, slow_scale, fast_scale) * jitter
    surviving_volumes = jnp.exp(-1.0 / scale_length)
    spike_occurrence_flags = jax.random.randint(spike_sampling_seed, lattice_extents, 0, SECOND_AXIS_SIZE) < 3
    discarded_volumes = jax.random.uniform(dropout_random_key, lattice_extents, jnp.float32, 0.5, 0.8)
    return jnp.where(spike_occurrence_flags, discarded_volumes, surviving_volumes)


def place_ends(entries, rng, least, top_value):
    longest = entries.shape.index(max(entries.shape))
    spots = []
    for shift in (0, 1):
        where = [jax.random.randint(jax.random.fold_in(rng, axis), (), 0, length) for axis, length in enumerate(entries.shape)]
        where[longest] = (where[longest] + shift) % entries.shape[longest]
        spots.append(tuple(where))
    return entries.at[spots[0]].set(least).at[spots[1]].set(top_value)


def block_levels(own_key, dims, split, least, top_value):
    def one(dim, blocks):
        draws = jax.random.uniform(jax.random.fold_in(jax.random.fold_in(own_key, 6), dim), (blocks,), jnp.float32, least / len(split), top_value / len(split))
        return jnp.repeat(jnp.exp(draws), dims[dim] // blocks).reshape((-1,) + (1,) * (len(dims) - dim - 1))

    factor_of = one(*split[0])
    for cut in split[1:]:
        factor_of = factor_of * one(*cut)
    return factor_of


def gaussian(own_key, shape, spread, bound, split=(), dtype=jnp.bfloat16):
    drawn = jax.random.normal(own_key, shape, jnp.float32) * spread
    if len(split) > 0:
        drawn = block_levels(own_key, shape, split, -0.22, 0.18) * drawn
    return jnp.clip(drawn, min=-bound, max=bound).astype(dtype)


def setup_inputs(seed: int = 0) -> dict:
    seeds = jax.random.split(jax.random.key(seed), 6)
    return {
        "flow": draw_flow(jax.random.fold_in(seeds[5], 71), 0),
        "adjoint": gaussian(seeds[1], (5, NX, SECOND_AXIS_SIZE, NZ), 1.0, 6.0, ((1, 4), (2, 8)), jnp.float32),
        "faces": gaussian(seeds[2], (6, 3, NX, SECOND_AXIS_SIZE, NZ), 1.0, 6.0, ((2, 4), (3, 8)), jnp.float32),
        "decay": draw_decay(jax.random.fold_in(seeds[5], 71), 0),
        "surface_mask": place_ends((jax.random.randint(seeds[4], (NX, SECOND_AXIS_SIZE, NZ), 0, 4096) < 1).astype(jnp.int32), jax.random.fold_in(seeds[4], 1), 0, 1),
    }


KAPPA = 0.15

def face_flux(flow_state, vector):
    density = flow_state[0]
    momentum_field = flow_state[1:4]
    normal_speed = lax.optimization_barrier(jnp.sum(momentum_field * vector, axis=0)) / density
    pressure = 0.4 * (flow_state[4] - 0.5 * lax.optimization_barrier(jnp.sum(momentum_field * momentum_field, axis=0)) / density)
    return jnp.concatenate([(density * normal_speed)[None], momentum_field * normal_speed[None] + pressure[None] * vector, ((flow_state[4] + pressure) * normal_speed)[None]], axis=0)

def face_term(flow_state, vector, weight):
    unused, pullback = jax.vjp(face_flux, flow_state, vector)
    grad_state, grad_vector = pullback(0.5 * weight)
    density = flow_state[0]
    momentum_field = flow_state[1:4]
    pressure = 0.4 * (flow_state[4] - 0.5 * lax.optimization_barrier(jnp.sum(momentum_field * momentum_field, axis=0)) / density)
    signal_celerity = jnp.abs(lax.optimization_barrier(jnp.sum(momentum_field * vector, axis=0))) / density + jnp.sqrt(1.4 * pressure / density) * jnp.sqrt(lax.optimization_barrier(jnp.sum(vector * vector, axis=0)))
    return (grad_state + 0.5 * signal_celerity[None] * weight, grad_vector)

def face_sums(flow, adjoint, faces, padded):
    beside_list = [padded[:, 2:, 1:-1, 1:-1], padded[:, :-2, 1:-1, 1:-1], padded[:, 1:-1, 2:, 1:-1], padded[:, 1:-1, :-2, 1:-1], padded[:, 1:-1, 1:-1, 2:], padded[:, 1:-1, 1:-1, :-2]]
    orients = (1.0, -1.0, 1.0, -1.0, 1.0, -1.0)
    product = None
    volume = None
    for face_index in range(6):
        weight = adjoint - beside_list[face_index]
        grad_state, grad_vector = face_term(flow, faces[face_index], weight)
        if face_index == 0:
            product = grad_state
            volume = orients[face_index] * grad_vector
        else:
            product = product + grad_state
            volume = volume + orients[face_index] * grad_vector
    return (product, volume)

def couple(warp_field):
    padded = jnp.pad(warp_field, ((0, 0), (1, 1), (0, 0), (1, 1)))
    return padded[:, 2:, :, 1:-1] + padded[:, :-2, :, 1:-1] + padded[:, 1:-1, :, 2:] + padded[:, 1:-1, :, :-2]

def reference(flow, adjoint, faces, decay, surface_mask):
    padded = jnp.pad(adjoint, ((0, 0), (1, 1), (1, 1), (1, 1)))
    product, volume = face_sums(flow, adjoint, faces, padded)
    retention = (1 - surface_mask).astype(jnp.float32) * decay
    rate_rows = jnp.moveaxis(retention, 1, 0)
    warp_field = volume

    def advance(carried, inputs):
        rate_row, source_row = inputs
        updated = rate_row[None] * carried + (1.0 - rate_row[None]) * source_row
        return (updated, updated)
    for sweep_index in range(SWEEPS):
        source_term = volume + KAPPA * couple(warp_field)
        source_rows = jnp.moveaxis(source_term, 2, 0)
        start = jnp.zeros((3, NX, NZ), jnp.float32)
        unused, outputs = lax.scan(advance, start, (rate_rows, source_rows), reverse=True)
        warp_field = jnp.moveaxis(outputs, 0, 2)
    return (product, warp_field)
```

```python
import functools

import jax
import jax.numpy as jnp
from jax import lax
from jax.experimental import pallas as pl
from jax.experimental.pallas import tpu as pltpu
from jax.sharding import PartitionSpec as P

SWEEPS = 4
KAPPA = 0.15
GAS = 0.4

F32 = jnp.float32

REACH = [[(0, 0)]]
for _ in range(SWEEPS - 1):
    REACH.append(
        sorted({(i + a, k + b) for i, k in REACH[-1] for a, b in ((1, 0), (-1, 0), (0, 1), (0, -1))})
    )


def matching(axis, first):
    count = lax.axis_size(axis)
    pairs = [(i, i + 1) for i in range(first, count - 1, 2)]
    return pairs + [(b, a) for a, b in pairs]


def swap(x, axis, first):
    return lax.ppermute(x, axis, matching(axis, first))


def ends(x, dim, width, even):
    size = x.shape[dim]
    to_first = lax.dynamic_slice_in_dim(x, jnp.where(even, size - width, 0), width, dim)
    to_second = lax.dynamic_slice_in_dim(x, jnp.where(even, 0, size - width), width, dim)
    return to_first, to_second


def flip(x, axis, mask):
    count = lax.axis_size(axis)
    return lax.ppermute(x, axis, [(i, i ^ mask) for i in range(count)])


def collect(x, axis):
    count = lax.axis_size(axis)
    if count not in (2, 4, 8):
        return [lax.all_gather(x, axis)]
    far = {m: flip(x, axis, m) for m in range(2, count, 2)}
    peers = {1: flip(x, axis, 1)}
    for m, value in far.items():
        peers[m] = value
        peers[m + 1] = flip(value, axis, 1)
    return [peers[m] for m in sorted(peers)]


def shift_i(x, step):
    rows = x.shape[0]
    return pltpu.roll(x, (-step) % rows, 0)


def shift_k(x, step):
    lanes = x.shape[1]
    return pltpu.roll(x, (-step) % lanes, 1)


def edge_k(x, step):
    lane = lax.broadcasted_iota(jnp.int32, x.shape, 1)
    edge = x.shape[1] - 1 if step > 0 else 0
    return jnp.where(lane == edge, 0.0, shift_k(x, step))


def move(x, step):
    return shift_i(x, step[0]) if step[0] else edge_k(x, step[1])


def couple(x):
    return (shift_i(x, 1) + shift_i(x, -1)) + (edge_k(x, 1) + edge_k(x, -1))


def row_valid(rows, lanes):
    own = rows - 2 * SWEEPS
    place = lax.axis_index("bx")
    above = jnp.where(place < lax.axis_size("bx") - 1, SWEEPS - 1, 0)
    below = jnp.where(place > 0, SWEEPS - 1, 0)
    row = lax.broadcasted_iota(jnp.int32, (rows, lanes), 0)
    inside = (row < own + above) | (row >= rows - below)
    return jnp.where(inside, 1.0, 0.0).astype(F32)


def fill_rows(dst, at, up, low, even):
    pass


def maps_kernel(decay_ref, mask_ref, first_ref, second_ref, rate_ref, map_ref, *, rows, nj):
    lanes = decay_ref.shape[-1]
    own = rows - 2 * SWEEPS
    wide = SWEEPS - 1
    rate_ref[0 : own * nj, :] = (
        (1 - mask_ref[...]).astype(F32) * decay_ref[...]
    ).reshape(own * nj, lanes)
    even = lax.axis_index("bx") % 2 == 0
    first = first_ref[...].reshape(wide * nj, lanes)
    second = second_ref[...].reshape(wide * nj, lanes)
    rate_ref[own * nj : (own + wide) * nj, :] = jnp.where(even, first, second)
    rate_ref[(own + wide) * nj : (rows - wide) * nj, :] = jnp.zeros((2 * nj, lanes), F32)
    rate_ref[(rows - wide) * nj : rows * nj, :] = jnp.where(even, second, first)

    valid = row_valid(rows, lanes)
    coef = [{o: None for o in REACH[d]} for d in range(SWEEPS)]
    for j in range(nj - 1, -1, -1):
        rate = rate_ref[pl.ds(j, rows, stride=nj), :]
        gain = KAPPA * (valid - rate)
        old = coef[0][(0, 0)]
        coef[0][(0, 0)] = rate if old is None else rate * old
        for d in range(1, SWEEPS):
            n = own if d == SWEEPS - 1 else rows
            total = {o: None for o in REACH[d]}
            for o, c in coef[d - 1].items():
                for step in ((1, 0), (-1, 0), (0, 1), (0, -1)):
                    moved = move(c, step)[:n]
                    goal = (o[0] + step[0], o[1] + step[1])
                    total[goal] = moved if total[goal] is None else total[goal] + moved
            for o in REACH[d]:
                fresh = gain[:n] * total[o]
                old = coef[d][o]
                coef[d][o] = fresh if old is None else rate[:n] * old + fresh
    at = 0
    for d in range(SWEEPS):
        for o in REACH[d]:
            c = coef[d][o]
            for part in range(c.shape[0] // own):
                map_ref[at] = c[part * own : (part + 1) * own]
                at += 1


def map_slots(rows, own):
    slots, at = {}, 0
    for d in range(SWEEPS):
        n = 1 if d == SWEEPS - 1 else rows // own
        for o in REACH[d]:
            slots[d, o] = (at, n)
            at += n
    return slots, at


def sweeps(v_ref, rate_ref, valid, state, rows, own, nj, emit):
    comps = v_ref.shape[0]
    for j in range(nj - 1, -1, -1):
        rate = rate_ref[pl.ds(j, rows, stride=nj), :]
        rest = valid - rate
        base = [v_ref[c, pl.ds(j, rows, stride=nj), :] for c in range(comps)]
        before = base
        for s in range(SWEEPS):
            n = own if s == SWEEPS - 1 else rows
            now = []
            for c in range(comps):
                source = base[c][:n] + KAPPA * couple(before[c])[:n]
                new = rest[:n] * source
                if state[s][c] is not None:
                    new = new + rate[:n] * state[s][c]
                now.append(new)
            state[s] = now
            before = now
        if emit is not None:
            emit(j, state[SWEEPS - 1])
    return state


def offsets_kernel(
    flow_ref, adj_ref, first_ref, second_ref, jfirst_ref, jsecond_ref, cfirst_ref, csecond_ref,
    rate_ref, v_ref, off_ref, halo_ref, line_ref, *, rows, nj,
):
    lanes = flow_ref.shape[-1]
    own = rows - 2 * SWEEPS
    w = SWEEPS
    even = lax.axis_index("bx") % 2 == 0
    jeven = lax.axis_index("by") % 2 == 0
    place, count = lax.axis_index("bx"), lax.axis_size("bx")
    one, two = first_ref[...], second_ref[...]
    halo_ref[0] = jnp.where(even, one, two)
    halo_ref[1] = jnp.where(even, two, one)
    a, b = jfirst_ref[...], jsecond_ref[...]
    c, d = cfirst_ref[...], csecond_ref[...]
    line_ref[0, :, 0:own, :] = jnp.where(jeven, b, a)
    line_ref[1, :, 0:own, :] = jnp.where(jeven, a, b)
    line_ref[:, :, own : own + w, :] = jnp.where(even, c, d)
    line_ref[:, :, own + w : rows, :] = jnp.where(even, d, c)

    sub = lax.broadcasted_iota(jnp.int32, (nj, lanes), 0)

    def adjoint_at(comp, i):
        if 0 <= i < own:
            return adj_ref[comp, i]
        if i >= own:
            return halo_ref[0, comp * (w + 1) + i - own]
        return halo_ref[1, comp * (w + 1) + (w + 1) + i]

    def flow_at(comp, i):
        if 0 <= i < own:
            return flow_ref[comp, i]
        base = 5 * (w + 1) + comp * w
        if i >= own:
            return halo_ref[0, base + i - own]
        return halo_ref[1, base + w + i]

    for row in range(rows):
        i = row if row < own + w else row - rows
        jump = []
        for comp in range(5):
            here = adjoint_at(comp, i)
            diff = adjoint_at(comp, i - 1) - adjoint_at(comp, i + 1)
            back = jnp.where(sub == 0, line_ref[0, comp, row : row + 1, :], pltpu.roll(here, 1, 0))
            ahead = jnp.where(
                sub == nj - 1, line_ref[1, comp, row : row + 1, :], pltpu.roll(here, nj - 1, 0)
            )
            jump.append(diff + (back - ahead) + (edge_k(here, -1) - edge_k(here, 1)))
        rho = flow_at(0, i)
        m = [flow_at(comp, i) for comp in (1, 2, 3)]
        energy = flow_at(4, i)
        inv = 1.0 / rho
        u = [x * inv for x in m]
        mu = m[0] * u[0] + m[1] * u[1] + m[2] * u[2]
        pressure = GAS * (energy - 0.5 * mu)
        q = (
            rho * jump[0]
            + (m[0] * jump[1] + m[1] * jump[2] + m[2] * jump[3])
            + (energy + pressure) * jump[4]
        )
        for comp in range(3):
            value = 0.5 * (u[comp] * q + pressure * jump[comp + 1])
            if i >= own:
                value = jnp.where(place < count - 1, value, 0.0)
            elif i < 0:
                value = jnp.where(place > 0, value, 0.0)
            v_ref[comp, row * nj : (row + 1) * nj, :] = value

    valid = row_valid(rows, lanes)
    state = [[None] * 3 for _ in range(SWEEPS)]
    state = sweeps(v_ref, rate_ref, valid, state, rows, own, nj, None)
    at = 0
    for s in range(SWEEPS):
        for comp in range(3):
            x = state[s][comp]
            for part in range(x.shape[0] // own):
                off_ref[at] = x[part * own : (part + 1) * own]
                at += 1


def finish_kernel(*refs, rows, nj, count, stacked):
    own = rows - 2 * SWEEPS
    if stacked:
        v_ref, rate_ref, map_ref, off_ref, out_ref, x_ref = refs
    else:
        v_ref, rate_ref = refs[:2]
        maps = refs[2 : 2 + count - 1]
        offs = refs[1 + count : 2 * count]
        out_ref, x_ref, map_ref, off_ref = refs[2 * count :]
    lanes = v_ref.shape[-1]
    me = lax.axis_index("by")
    if not stacked:
        for mask in range(1, count):
            map_ref[me ^ mask] = maps[mask - 1][...]
            off_ref[me ^ mask] = offs[mask - 1][...]
    slots, _ = map_slots(rows, own)

    def load(ref, block, at, n):
        if n == 1:
            return ref[block, at]
        return jnp.concatenate([ref[block, at + part] for part in range(n)], axis=0)

    sizes = [rows // own] * (SWEEPS - 1) + [1]
    starts, at = {}, 0
    for s in range(SWEEPS):
        for comp in range(3):
            starts[s, comp] = at
            at += sizes[s]
    x_ref[...] = jnp.zeros(x_ref.shape, F32)

    def get(s, comp):
        a = starts[s, comp]
        return jnp.concatenate([x_ref[a + part] for part in range(sizes[s])], axis=0)

    def put(s, comp, value):
        for part in range(sizes[s]):
            x_ref[starts[s, comp] + part] = value[part * own : (part + 1) * own]

    def through(hop, carry):
        block = count - 1 - hop
        coef = {key: load(map_ref, block, *slot) for key, slot in slots.items()}
        fresh = {}
        for comp in range(3):
            x = [get(s, comp) for s in range(SWEEPS)]
            total = [load(off_ref, block, starts[s, comp], sizes[s]) for s in range(SWEEPS)]
            for s in range(SWEEPS):
                for o in sorted({o for d in range(SWEEPS - s) for o in REACH[d]}):
                    moved = x[s]
                    if o[0]:
                        moved = shift_i(moved, o[0])
                    if o[1]:
                        moved = shift_k(moved, o[1])
                    for d in range(SWEEPS - s):
                        if o in REACH[d]:
                            n = sizes[s + d] * own
                            total[s + d] = total[s + d] + coef[d, o][:n] * moved[:n]
            for s in range(SWEEPS):
                fresh[s, comp] = total[s]
        for (s, comp), value in fresh.items():
            put(s, comp, value)
        return carry

    lax.fori_loop(0, count - 1 - me, through, 0)

    valid = row_valid(rows, lanes)
    state = [[get(s, comp) for comp in range(3)] for s in range(SWEEPS)]

    def emit(j, values):
        for comp in range(3):
            out_ref[comp, pl.ds(j, own, stride=nj), :] = values[comp]

    sweeps(v_ref, rate_ref, valid, state, rows, own, nj, emit)


def product_kernel(
    flow_ref, adj_ref, faces_ref, first_ref, second_ref, jfirst_ref, jsecond_ref, out_ref, *, nj,
):
    own, lanes = flow_ref.shape[1], flow_ref.shape[-1]
    w = SWEEPS
    even = lax.axis_index("bx") % 2 == 0
    jeven = lax.axis_index("by") % 2 == 0
    sub = lax.broadcasted_iota(jnp.int32, (nj, lanes), 0)
    for i in range(own):
        here = [adj_ref[comp, i] for comp in range(5)]

        def beside(comp, face):
            if face == 0:
                if i + 1 < own:
                    return adj_ref[comp, i + 1]
                at = comp * (w + 1)
                return jnp.where(even, first_ref[at], second_ref[at])
            if face == 1:
                if i > 0:
                    return adj_ref[comp, i - 1]
                at = comp * (w + 1) + w
                return jnp.where(even, second_ref[at], first_ref[at])
            if face in (2, 3):
                one = jfirst_ref[comp, i : i + 1, :]
                two = jsecond_ref[comp, i : i + 1, :]
                if face == 2:
                    line = jnp.where(jeven, one, two)
                    return jnp.where(sub == nj - 1, line, pltpu.roll(here[comp], nj - 1, 0))
                line = jnp.where(jeven, two, one)
                return jnp.where(sub == 0, line, pltpu.roll(here[comp], 1, 0))
            return edge_k(here[comp], 1 if face == 4 else -1)

        rho = flow_ref[0, i]
        m = [flow_ref[comp, i] for comp in (1, 2, 3)]
        energy = flow_ref[4, i]
        inv = 1.0 / rho
        u = [x * inv for x in m]
        uu = u[0] * u[0] + u[1] * u[1] + u[2] * u[2]
        pressure = GAS * (energy - 0.5 * (rho * uu))
        enthalpy = (energy + pressure) * inv
        sound = jnp.sqrt((1.0 + GAS) * pressure * inv)
        total = None
        for face in range(6):
            s = [faces_ref[face, axis, i] for axis in range(3)]
            h = [0.5 * (here[comp] - beside(comp, face)) for comp in range(5)]
            speed = u[0] * s[0] + u[1] * s[1] + u[2] * s[2]
            area = jnp.sqrt(s[0] * s[0] + s[1] * s[1] + s[2] * s[2])
            wave = jnp.abs(speed) + sound * area
            bulk = (u[0] * h[1] + u[1] * h[2] + u[2] * h[3]) + enthalpy * h[4]
            press = (s[0] * h[1] + s[1] * h[2] + s[2] * h[3]) + speed * h[4]
            full = h[0] + bulk
            term = [
                0.5 * GAS * (uu * press) - speed * bulk + wave * h[0],
                s[0] * full - GAS * (u[0] * press) + (speed + wave) * h[1],
                s[1] * full - GAS * (u[1] * press) + (speed + wave) * h[2],
                s[2] * full - GAS * (u[2] * press) + (speed + wave) * h[3],
                GAS * press + (speed + wave) * h[4],
            ]
            total = term if total is None else [a + b for a, b in zip(total, term)]
        for comp in range(5):
            out_ref[comp, i] = total[comp]


def call(kernel, out_shape, args, scratch=(), interpret=False):
    vmem = pl.BlockSpec(memory_space=pltpu.VMEM)
    single = not isinstance(out_shape, (list, tuple))
    return pl.pallas_call(
        kernel,
        out_shape=out_shape,
        in_specs=[vmem] * len(args),
        out_specs=vmem if single else [vmem] * len(out_shape),
        scratch_shapes=list(scratch),
        interpret=interpret,
        compiler_params=pltpu.CompilerParams(vmem_limit_bytes=60 * 1024 * 1024),
    )(*args)


INTERPRET = False


def on_device(flow, adjoint, faces, decay, surface_mask):
    own, nj, lanes = decay.shape
    w = SWEEPS
    rows = own + 2 * w
    nby = lax.axis_size("by")
    bx, by = lax.axis_index("bx"), lax.axis_index("by")
    even, jeven = bx % 2 == 0, by % 2 == 0
    run = functools.partial(call, interpret=INTERPRET)

    retention = (1 - surface_mask).astype(F32) * decay
    r1, r2 = ends(retention, 0, w - 1, even)
    r1, r2 = swap(r1, "bx", 0), swap(r2, "bx", 1)
    a1, a2 = ends(adjoint, 1, w + 1, even)
    f1, f2 = ends(flow, 1, w, even)

    def pack(a, f):
        return jnp.concatenate(
            [a.reshape(5 * (w + 1), nj, lanes), f.reshape(5 * w, nj, lanes)], axis=0
        )

    m1, m2 = swap(pack(a1, f1), "bx", 0), swap(pack(a2, f2), "bx", 1)
    l1, l2 = ends(adjoint, 2, 1, jeven)
    l1 = swap(l1.reshape(5, own, lanes), "by", 0)
    l2 = swap(l2.reshape(5, own, lanes), "by", 1)
    below, above = jnp.where(jeven, l2, l1), jnp.where(jeven, l1, l2)
    c1, c2 = ends(jnp.stack([below, above]), 2, w, even)
    c1, c2 = swap(c1, "bx", 0), swap(c2, "bx", 1)

    _, n_map = map_slots(rows, own)
    rate, maps = run(
        functools.partial(maps_kernel, rows=rows, nj=nj),
        [
            jax.ShapeDtypeStruct((rows * nj, lanes), F32),
            jax.ShapeDtypeStruct((n_map, own, lanes), F32),
        ],
        [decay, surface_mask, r1, r2],
    )
    all_maps = collect(maps, "by")

    n_off = 3 * ((SWEEPS - 1) * (rows // own) + 1)
    v, offs = run(
        functools.partial(offsets_kernel, rows=rows, nj=nj),
        [
            jax.ShapeDtypeStruct((3, rows * nj, lanes), F32),
            jax.ShapeDtypeStruct((n_off, own, lanes), F32),
        ],
        [flow, adjoint, m1, m2, l1, l2, c1, c2, rate],
        [
            pltpu.VMEM((2, 5 * (2 * w + 1), nj, lanes), F32),
            pltpu.VMEM((2, 5, rows, lanes), F32),
        ],
    )
    all_offs = collect(offs, "by")

    product = run(
        functools.partial(product_kernel, nj=nj),
        jax.ShapeDtypeStruct(flow.shape, F32),
        [flow, adjoint, faces, m1, m2, l1, l2],
    )

    stacked = len(all_maps) == 1 and nby != 2
    scratch = [pltpu.VMEM((n_off, own, lanes), F32)]
    if not stacked:
        scratch += [
            pltpu.VMEM((nby, n_map, own, lanes), F32),
            pltpu.VMEM((nby, n_off, own, lanes), F32),
        ]
    warp = run(
        functools.partial(finish_kernel, rows=rows, nj=nj, count=nby, stacked=stacked),
        jax.ShapeDtypeStruct((3, own * nj, lanes), F32),
        [v, rate, *all_maps, *all_offs],
        scratch,
    )
    return (product, warp.reshape(3, own, nj, lanes))


def solution(mesh):
    return jax.shard_map(
        on_device,
        mesh=mesh,
        in_specs=(
            P(None, "bx", "by", None),
            P(None, "bx", "by", None),
            P(None, None, "bx", "by", None),
            P("bx", "by", None),
            P("bx", "by", None),
        ),
        out_specs=(P(None, "bx", "by", None), P(None, "bx", "by", None)),
        check_vma=False,
    )
```

```python
import functools
import math

import jax
import jax.numpy as jnp
from jax import lax
from jax.experimental import pallas as pl
from jax.experimental.pallas import tpu as pltpu
from jax.sharding import PartitionSpec as P

SWEEPS = 4
KAPPA = 0.15
GAS = 0.4

F32 = jnp.float32

REACH = [[(0, 0)]]
for _ in range(SWEEPS - 1):
    REACH.append(
        sorted({(i + a, k + b) for i, k in REACH[-1] for a, b in ((1, 0), (-1, 0), (0, 1), (0, -1))})
    )


def matching(axis, first):
    count = lax.axis_size(axis)
    pairs = [(i, i + 1) for i in range(first, count - 1, 2)]
    return pairs + [(b, a) for a, b in pairs]


def swap(x, axis, first):
    return lax.ppermute(x, axis, matching(axis, first))


def ends(x, dim, width, even):
    size = x.shape[dim]
    to_first = lax.dynamic_slice_in_dim(x, jnp.where(even, size - width, 0), width, dim)
    to_second = lax.dynamic_slice_in_dim(x, jnp.where(even, 0, size - width), width, dim)
    return to_first, to_second


def flip(x, axis, mask):
    count = lax.axis_size(axis)
    return lax.ppermute(x, axis, [(i, i ^ mask) for i in range(count)])


def collect(x, axis):
    count = lax.axis_size(axis)
    if count not in (2, 4, 8):
        return [lax.all_gather(x, axis)]
    far = {m: flip(x, axis, m) for m in range(2, count, 2)}
    peers = {1: flip(x, axis, 1)}
    for m, value in far.items():
        peers[m] = value
        peers[m + 1] = flip(value, axis, 1)
    return [peers[m] for m in sorted(peers)]


def shift_i(x, step):
    rows = x.shape[0]
    return pltpu.roll(x, (-step) % rows, 0)


def shift_k(x, step):
    lanes = x.shape[1]
    return pltpu.roll(x, (-step) % lanes, 1)


def edge_k(x, step):
    lane = lax.broadcasted_iota(jnp.int32, x.shape, 1)
    edge = x.shape[1] - 1 if step > 0 else 0
    return jnp.where(lane == edge, 0.0, shift_k(x, step))


def move(x, step):
    return shift_i(x, step[0]) if step[0] else edge_k(x, step[1])


def couple(x):
    return (shift_i(x, 1) + shift_i(x, -1)) + (edge_k(x, 1) + edge_k(x, -1))


def row_valid(rows, lanes):
    own = rows - 2 * SWEEPS
    place = lax.axis_index("bx")
    above = jnp.where(place < lax.axis_size("bx") - 1, SWEEPS - 1, 0)
    below = jnp.where(place > 0, SWEEPS - 1, 0)
    row = lax.broadcasted_iota(jnp.int32, (rows, lanes), 0)
    inside = (row < own + above) | (row >= rows - below)
    return jnp.where(inside, 1.0, 0.0).astype(F32)


def maps_kernel(decay_ref, mask_ref, first_ref, second_ref, rate_ref, map_ref, *, rows, nj):
    lanes = decay_ref.shape[-1]
    own = rows - 2 * SWEEPS
    wide = SWEEPS - 1
    rate_ref[0 : own * nj, :] = (
        (1 - mask_ref[...]).astype(F32) * decay_ref[...]
    ).reshape(own * nj, lanes)
    even = lax.axis_index("bx") % 2 == 0
    first = first_ref[...].reshape(wide * nj, lanes)
    second = second_ref[...].reshape(wide * nj, lanes)
    rate_ref[own * nj : (own + wide) * nj, :] = jnp.where(even, first, second)
    rate_ref[(own + wide) * nj : (rows - wide) * nj, :] = jnp.zeros((2 * nj, lanes), F32)
    rate_ref[(rows - wide) * nj : rows * nj, :] = jnp.where(even, second, first)

    valid = row_valid(rows, lanes)
    coef = [{o: None for o in REACH[d]} for d in range(SWEEPS)]
    for j in range(nj - 1, -1, -1):
        rate = rate_ref[pl.ds(j, rows, stride=nj), :]
        gain = KAPPA * (valid - rate)
        old = coef[0][(0, 0)]
        coef[0][(0, 0)] = rate if old is None else rate * old
        for d in range(1, SWEEPS):
            n = own if d == SWEEPS - 1 else rows
            total = {o: None for o in REACH[d]}
            for o, c in coef[d - 1].items():
                for step in ((1, 0), (-1, 0), (0, 1), (0, -1)):
                    moved = move(c, step)[:n]
                    goal = (o[0] + step[0], o[1] + step[1])
                    total[goal] = moved if total[goal] is None else total[goal] + moved
            for o in REACH[d]:
                fresh = gain[:n] * total[o]
                old = coef[d][o]
                coef[d][o] = fresh if old is None else rate[:n] * old + fresh
    at = 0
    for d in range(SWEEPS):
        for o in REACH[d]:
            c = coef[d][o]
            for part in range(c.shape[0] // own):
                map_ref[at] = c[part * own : (part + 1) * own]
                at += 1


def map_slots(rows, own):
    slots, at = {}, 0
    for d in range(SWEEPS):
        n = 1 if d == SWEEPS - 1 else rows // own
        for o in REACH[d]:
            slots[d, o] = (at, n)
            at += n
    return slots, at


def sweeps(v_ref, rate_ref, valid, state, rows, own, nj, emit):
    comps = v_ref.shape[0]
    for j in range(nj - 1, -1, -1):
        rate = rate_ref[pl.ds(j, rows, stride=nj), :]
        rest = valid - rate
        base = [v_ref[c, pl.ds(j, rows, stride=nj), :] for c in range(comps)]
        before = base
        for s in range(SWEEPS):
            n = own if s == SWEEPS - 1 else rows
            now = []
            for c in range(comps):
                source = base[c][:n] + KAPPA * couple(before[c])[:n]
                new = rest[:n] * source
                if state[s][c] is not None:
                    new = new + rate[:n] * state[s][c]
                now.append(new)
            state[s] = now
            before = now
        if emit is not None:
            emit(j, state[SWEEPS - 1])
    return state


def offsets_kernel(
    flow_ref, adj_ref, first_ref, second_ref, jfirst_ref, jsecond_ref, cfirst_ref, csecond_ref,
    rate_ref, v_ref, off_ref, halo_ref, line_ref, *, rows, nj,
):
    lanes = flow_ref.shape[-1]
    own = rows - 2 * SWEEPS
    w = SWEEPS
    even = lax.axis_index("bx") % 2 == 0
    jeven = lax.axis_index("by") % 2 == 0
    place, count = lax.axis_index("bx"), lax.axis_size("bx")
    one, two = first_ref[...], second_ref[...]
    halo_ref[0] = jnp.where(even, one, two)
    halo_ref[1] = jnp.where(even, two, one)
    a, b = jfirst_ref[...], jsecond_ref[...]
    c, d = cfirst_ref[...], csecond_ref[...]
    line_ref[0, :, 0:own, :] = jnp.where(jeven, b, a)
    line_ref[1, :, 0:own, :] = jnp.where(jeven, a, b)
    line_ref[:, :, own : own + w, :] = jnp.where(even, c, d)
    line_ref[:, :, own + w : rows, :] = jnp.where(even, d, c)

    sub = lax.broadcasted_iota(jnp.int32, (nj, lanes), 0)

    def adjoint_at(comp, i):
        if 0 <= i < own:
            return adj_ref[comp, i]
        if i >= own:
            return halo_ref[0, comp * (w + 1) + i - own]
        return halo_ref[1, comp * (w + 1) + (w + 1) + i]

    def flow_at(comp, i):
        if 0 <= i < own:
            return flow_ref[comp, i]
        base = 5 * (w + 1) + comp * w
        if i >= own:
            return halo_ref[0, base + i - own]
        return halo_ref[1, base + w + i]

    for row in range(rows):
        i = row if row < own + w else row - rows
        jump = []
        for comp in range(5):
            here = adjoint_at(comp, i)
            diff = adjoint_at(comp, i - 1) - adjoint_at(comp, i + 1)
            back = jnp.where(sub == 0, line_ref[0, comp, row : row + 1, :], pltpu.roll(here, 1, 0))
            ahead = jnp.where(
                sub == nj - 1, line_ref[1, comp, row : row + 1, :], pltpu.roll(here, nj - 1, 0)
            )
            jump.append(diff + (back - ahead) + (edge_k(here, -1) - edge_k(here, 1)))
        rho = flow_at(0, i)
        m = [flow_at(comp, i) for comp in (1, 2, 3)]
        energy = flow_at(4, i)
        inv = 1.0 / rho
        u = [x * inv for x in m]
        mu = m[0] * u[0] + m[1] * u[1] + m[2] * u[2]
        pressure = GAS * (energy - 0.5 * mu)
        q = (
            rho * jump[0]
            + (m[0] * jump[1] + m[1] * jump[2] + m[2] * jump[3])
            + (energy + pressure) * jump[4]
        )
        for comp in range(3):
            value = 0.5 * (u[comp] * q + pressure * jump[comp + 1])
            if i >= own:
                value = jnp.where(place < count - 1, value, 0.0)
            elif i < 0:
                value = jnp.where(place > 0, value, 0.0)
            v_ref[comp, row * nj : (row + 1) * nj, :] = value

    valid = row_valid(rows, lanes)
    state = [[None] * 3 for _ in range(SWEEPS)]
    state = sweeps(v_ref, rate_ref, valid, state, rows, own, nj, None)
    at = 0
    for s in range(SWEEPS):
        for comp in range(3):
            x = state[s][comp]
            for part in range(x.shape[0] // own):
                off_ref[at] = x[part * own : (part + 1) * own]
                at += 1


def finish_kernel(*refs, rows, nj, count, stacked):
    own = rows - 2 * SWEEPS
    if stacked:
        v_ref, rate_ref, map_ref, off_ref, out_ref, x_ref = refs
    else:
        v_ref, rate_ref = refs[:2]
        maps = refs[2 : 2 + count - 1]
        offs = refs[1 + count : 2 * count]
        out_ref, x_ref, map_ref, off_ref = refs[2 * count :]
    lanes = v_ref.shape[-1]
    me = lax.axis_index("by")
    if not stacked:
        for mask in range(1, count):
            map_ref[me ^ mask] = maps[mask - 1][...]
            off_ref[me ^ mask] = offs[mask - 1][...]
    slots, _ = map_slots(rows, own)

    def load(ref, block, at, n):
        if n == 1:
            return ref[block, at]
        return jnp.concatenate([ref[block, at + part] for part in range(n)], axis=0)

    sizes = [rows // own] * (SWEEPS - 1) + [1]
    starts, at = {}, 0
    for s in range(SWEEPS):
        for comp in range(3):
            starts[s, comp] = at
            at += sizes[s]
    x_ref[...] = jnp.zeros(x_ref.shape, F32)

    def get(s, comp):
        a = starts[s, comp]
        return jnp.concatenate([x_ref[a + part] for part in range(sizes[s])], axis=0)

    def put(s, comp, value):
        for part in range(sizes[s]):
            x_ref[starts[s, comp] + part] = value[part * own : (part + 1) * own]

    def through(hop, carry):
        block = count - 1 - hop
        coef = {key: load(map_ref, block, *slot) for key, slot in slots.items()}
        fresh = {}
        for comp in range(3):
            x = [get(s, comp) for s in range(SWEEPS)]
            total = [load(off_ref, block, starts[s, comp], sizes[s]) for s in range(SWEEPS)]
            for s in range(SWEEPS):
                for o in sorted({o for d in range(SWEEPS - s) for o in REACH[d]}):
                    moved = x[s]
                    if o[0]:
                        moved = shift_i(moved, o[0])
                    if o[1]:
                        moved = shift_k(moved, o[1])
                    for d in range(SWEEPS - s):
                        if o in REACH[d]:
                            n = sizes[s + d] * own
                            total[s + d] = total[s + d] + coef[d, o][:n] * moved[:n]
            for s in range(SWEEPS):
                fresh[s, comp] = total[s]
        for (s, comp), value in fresh.items():
            put(s, comp, value)
        return carry

    lax.fori_loop(0, count - 1 - me, through, 0)

    valid = row_valid(rows, lanes)
    state = [[get(s, comp) for comp in range(3)] for s in range(SWEEPS)]

    def emit(j, values):
        for comp in range(3):
            out_ref[comp, pl.ds(j, own, stride=nj), :] = values[comp]

    sweeps(v_ref, rate_ref, valid, state, rows, own, nj, emit)


def product_kernel(
    flow_ref, adj_ref, faces_ref, first_ref, second_ref, jfirst_ref, jsecond_ref, out_ref, *, nj,
):
    own, lanes = flow_ref.shape[1], flow_ref.shape[-1]
    w = SWEEPS
    even = lax.axis_index("bx") % 2 == 0
    jeven = lax.axis_index("by") % 2 == 0
    sub = lax.broadcasted_iota(jnp.int32, (nj, lanes), 0)
    for i in range(own):
        here = [adj_ref[comp, i] for comp in range(5)]

        def beside(comp, face):
            if face == 0:
                if i + 1 < own:
                    return adj_ref[comp, i + 1]
                at = comp * (w + 1)
                return jnp.where(even, first_ref[at], second_ref[at])
            if face == 1:
                if i > 0:
                    return adj_ref[comp, i - 1]
                at = comp * (w + 1) + w
                return jnp.where(even, second_ref[at], first_ref[at])
            if face in (2, 3):
                one = jfirst_ref[comp, i : i + 1, :]
                two = jsecond_ref[comp, i : i + 1, :]
                if face == 2:
                    line = jnp.where(jeven, one, two)
                    return jnp.where(sub == nj - 1, line, pltpu.roll(here[comp], nj - 1, 0))
                line = jnp.where(jeven, two, one)
                return jnp.where(sub == 0, line, pltpu.roll(here[comp], 1, 0))
            return edge_k(here[comp], 1 if face == 4 else -1)

        rho = flow_ref[0, i]
        m = [flow_ref[comp, i] for comp in (1, 2, 3)]
        energy = flow_ref[4, i]
        inv = 1.0 / rho
        u = [x * inv for x in m]
        uu = u[0] * u[0] + u[1] * u[1] + u[2] * u[2]
        pressure = GAS * (energy - 0.5 * (rho * uu))
        enthalpy = (energy + pressure) * inv
        sound = jnp.sqrt((1.0 + GAS) * pressure * inv)
        total = None
        for face in range(6):
            s = [faces_ref[face, axis, i] for axis in range(3)]
            h = [0.5 * (here[comp] - beside(comp, face)) for comp in range(5)]
            speed = u[0] * s[0] + u[1] * s[1] + u[2] * s[2]
            area = jnp.sqrt(s[0] * s[0] + s[1] * s[1] + s[2] * s[2])
            wave = jnp.abs(speed) + sound * area
            bulk = (u[0] * h[1] + u[1] * h[2] + u[2] * h[3]) + enthalpy * h[4]
            press = (s[0] * h[1] + s[1] * h[2] + s[2] * h[3]) + speed * h[4]
            full = h[0] + bulk
            term = [
                0.5 * GAS * (uu * press) - speed * bulk + wave * h[0],
                s[0] * full - GAS * (u[0] * press) + (speed + wave) * h[1],
                s[1] * full - GAS * (u[1] * press) + (speed + wave) * h[2],
                s[2] * full - GAS * (u[2] * press) + (speed + wave) * h[3],
                GAS * press + (speed + wave) * h[4],
            ]
            total = term if total is None else [a + b for a, b in zip(total, term)]
        for comp in range(5):
            out_ref[comp, i] = total[comp]


def call(kernel, out_shape, args, scratch=(), interpret=False):
    vmem = pl.BlockSpec(memory_space=pltpu.VMEM)
    single = not isinstance(out_shape, (list, tuple))
    held = [*args, *([out_shape] if single else out_shape), *scratch]
    need = sum(4 * math.prod(a.shape) for a in held)
    return pl.pallas_call(
        kernel,
        out_shape=out_shape,
        in_specs=[vmem] * len(args),
        out_specs=vmem if single else [vmem] * len(out_shape),
        scratch_shapes=list(scratch),
        interpret=interpret,
        compiler_params=pltpu.CompilerParams(vmem_limit_bytes=need + (2 << 20)),
    )(*args)


INTERPRET = False


def on_device(flow, adjoint, faces, decay, surface_mask):
    own, nj, lanes = decay.shape
    w = SWEEPS
    rows = own + 2 * w
    nby = lax.axis_size("by")
    bx, by = lax.axis_index("bx"), lax.axis_index("by")
    even, jeven = bx % 2 == 0, by % 2 == 0

    def run(*args):
        return call(*args, interpret=INTERPRET)


    retention = (1 - surface_mask).astype(F32) * decay
    r1, r2 = ends(retention, 0, w - 1, even)
    r1, r2 = swap(r1, "bx", 0), swap(r2, "bx", 1)
    a1, a2 = ends(adjoint, 1, w + 1, even)
    f1, f2 = ends(flow, 1, w, even)

    def pack(a, f):
        return jnp.concatenate(
            [a.reshape(5 * (w + 1), nj, lanes), f.reshape(5 * w, nj, lanes)], axis=0
        )

    m1, m2 = swap(pack(a1, f1), "bx", 0), swap(pack(a2, f2), "bx", 1)
    l1, l2 = ends(adjoint, 2, 1, jeven)
    l1 = swap(l1.reshape(5, own, lanes), "by", 0)
    l2 = swap(l2.reshape(5, own, lanes), "by", 1)
    below, above = jnp.where(jeven, l2, l1), jnp.where(jeven, l1, l2)
    c1, c2 = ends(jnp.stack([below, above]), 2, w, even)
    c1, c2 = swap(c1, "bx", 0), swap(c2, "bx", 1)

    _, n_map = map_slots(rows, own)
    rate, maps = run(
        functools.partial(maps_kernel, rows=rows, nj=nj),
        [
            jax.ShapeDtypeStruct((rows * nj, lanes), F32),
            jax.ShapeDtypeStruct((n_map, own, lanes), F32),
        ],
        [decay, surface_mask, r1, r2],
    )
    all_maps = collect(maps, "by")

    n_off = 3 * ((SWEEPS - 1) * (rows // own) + 1)
    v, offs = run(
        functools.partial(offsets_kernel, rows=rows, nj=nj),
        [
            jax.ShapeDtypeStruct((3, rows * nj, lanes), F32),
            jax.ShapeDtypeStruct((n_off, own, lanes), F32),
        ],
        [flow, adjoint, m1, m2, l1, l2, c1, c2, rate],
        [
            pltpu.VMEM((2, 5 * (2 * w + 1), nj, lanes), F32),
            pltpu.VMEM((2, 5, rows, lanes), F32),
        ],
    )
    all_offs = collect(offs, "by")

    product = run(
        functools.partial(product_kernel, nj=nj),
        jax.ShapeDtypeStruct(flow.shape, F32),
        [flow, adjoint, faces, m1, m2, l1, l2],
    )

    stacked = len(all_maps) == 1 and nby != 2
    scratch = [pltpu.VMEM((n_off, own, lanes), F32)]
    if not stacked:
        scratch += [
            pltpu.VMEM((nby, n_map, own, lanes), F32),
            pltpu.VMEM((nby, n_off, own, lanes), F32),
        ]
    warp = run(
        functools.partial(finish_kernel, rows=rows, nj=nj, count=nby, stacked=stacked),
        jax.ShapeDtypeStruct((3, own * nj, lanes), F32),
        [v, rate, *all_maps, *all_offs],
        scratch,
    )
    return (product, warp.reshape(3, own, nj, lanes))


def solution(mesh):
    return jax.shard_map(
        on_device,
        mesh=mesh,
        in_specs=(
            P(None, "bx", "by", None),
            P(None, "bx", "by", None),
            P(None, None, "bx", "by", None),
            P("bx", "by", None),
            P("bx", "by", None),
        ),
        out_specs=(P(None, "bx", "by", None), P(None, "bx", "by", None)),
        check_vma=False,
    )
```

```python
import functools
import math

import jax
import jax.numpy as jnp
from jax import lax
from jax.experimental import pallas as pl
from jax.experimental.pallas import tpu as pltpu
from jax.sharding import PartitionSpec as P

SWEEPS = 4
KAPPA = 0.15
GAS = 0.4

F32 = jnp.float32

REACH = [[(0, 0)]]
for _ in range(SWEEPS - 1):
    REACH.append(
        sorted({(i + a, k + b) for i, k in REACH[-1] for a, b in ((1, 0), (-1, 0), (0, 1), (0, -1))})
    )


def matching(axis, first):
    count = lax.axis_size(axis)
    pairs = [(i, i + 1) for i in range(first, count - 1, 2)]
    return pairs + [(b, a) for a, b in pairs]


def swap(x, axis, first):
    return lax.ppermute(x, axis, matching(axis, first))


def ends(x, dim, width, even):
    size = x.shape[dim]
    to_first = lax.dynamic_slice_in_dim(x, jnp.where(even, size - width, 0), width, dim)
    to_second = lax.dynamic_slice_in_dim(x, jnp.where(even, 0, size - width), width, dim)
    return to_first, to_second


def flip(x, axis, mask):
    count = lax.axis_size(axis)
    return lax.ppermute(x, axis, [(i, i ^ mask) for i in range(count)])


def collect(x, axis):
    count = lax.axis_size(axis)
    if count not in (2, 4, 8):
        return [lax.all_gather(x, axis)]
    far = {m: flip(x, axis, m) for m in range(2, count, 2)}
    peers = {1: flip(x, axis, 1)}
    for m, value in far.items():
        peers[m] = value
        peers[m + 1] = flip(value, axis, 1)
    return [peers[m] for m in sorted(peers)]


def shift_i(x, step):
    rows = x.shape[0]
    return pltpu.roll(x, (-step) % rows, 0)


def shift_k(x, step):
    lanes = x.shape[1]
    return pltpu.roll(x, (-step) % lanes, 1)


def edge_k(x, step):
    lane = lax.broadcasted_iota(jnp.int32, x.shape, 1)
    edge = x.shape[1] - 1 if step > 0 else 0
    return jnp.where(lane == edge, 0.0, shift_k(x, step))


def move(x, step):
    return shift_i(x, step[0]) if step[0] else edge_k(x, step[1])


def couple(x):
    return (shift_i(x, 1) + shift_i(x, -1)) + (edge_k(x, 1) + edge_k(x, -1))


def row_valid(rows, lanes):
    own = rows - 2 * SWEEPS
    place = lax.axis_index("bx")
    above = jnp.where(place < lax.axis_size("bx") - 1, SWEEPS - 1, 0)
    below = jnp.where(place > 0, SWEEPS - 1, 0)
    row = lax.broadcasted_iota(jnp.int32, (rows, lanes), 0)
    inside = (row < own + above) | (row >= rows - below)
    return jnp.where(inside, 1.0, 0.0).astype(F32)


def maps_kernel(decay_ref, mask_ref, first_ref, second_ref, rate_ref, map_ref, *, rows, nj):
    lanes = decay_ref.shape[-1]
    own = rows - 2 * SWEEPS
    wide = SWEEPS - 1
    rate_ref[0 : own * nj, :] = (
        (1 - mask_ref[...]).astype(F32) * decay_ref[...]
    ).reshape(own * nj, lanes)
    even = lax.axis_index("bx") % 2 == 0
    first = first_ref[5 : 5 + wide].reshape(wide * nj, lanes)
    second = second_ref[5 : 5 + wide].reshape(wide * nj, lanes)
    rate_ref[own * nj : (own + wide) * nj, :] = jnp.where(even, first, second)
    rate_ref[(own + wide) * nj : (rows - wide) * nj, :] = jnp.zeros((2 * nj, lanes), F32)
    rate_ref[(rows - wide) * nj : rows * nj, :] = jnp.where(even, second, first)

    valid = row_valid(rows, lanes)
    coef = [{o: None for o in REACH[d]} for d in range(SWEEPS)]
    for j in range(nj - 1, -1, -1):
        rate = rate_ref[pl.ds(j, rows, stride=nj), :]
        gain = KAPPA * (valid - rate)
        old = coef[0][(0, 0)]
        coef[0][(0, 0)] = rate if old is None else rate * old
        for d in range(1, SWEEPS):
            n = own if d == SWEEPS - 1 else rows
            total = {o: None for o in REACH[d]}
            for o, c in coef[d - 1].items():
                for step in ((1, 0), (-1, 0), (0, 1), (0, -1)):
                    moved = move(c, step)[:n]
                    goal = (o[0] + step[0], o[1] + step[1])
                    total[goal] = moved if total[goal] is None else total[goal] + moved
            for o in REACH[d]:
                fresh = gain[:n] * total[o]
                old = coef[d][o]
                coef[d][o] = fresh if old is None else rate[:n] * old + fresh
    at = 0
    for d in range(SWEEPS):
        for o in REACH[d]:
            c = coef[d][o]
            for part in range(c.shape[0] // own):
                map_ref[at] = c[part * own : (part + 1) * own]
                at += 1


def map_slots(rows, own):
    slots, at = {}, 0
    for d in range(SWEEPS):
        n = 1 if d == SWEEPS - 1 else rows // own
        for o in REACH[d]:
            slots[d, o] = (at, n)
            at += n
    return slots, at


def sweeps(v_ref, rate_ref, valid, state, rows, own, nj, emit):
    comps = v_ref.shape[0]
    for j in range(nj - 1, -1, -1):
        rate = rate_ref[pl.ds(j, rows, stride=nj), :]
        rest = valid - rate
        base = [v_ref[c, pl.ds(j, rows, stride=nj), :] for c in range(comps)]
        before = base
        for s in range(SWEEPS):
            n = own if s == SWEEPS - 1 else rows
            now = []
            for c in range(comps):
                source = base[c][:n] + KAPPA * couple(before[c])[:n]
                new = rest[:n] * source
                if state[s][c] is not None:
                    new = new + rate[:n] * state[s][c]
                now.append(new)
            state[s] = now
            before = now
        if emit is not None:
            emit(j, state[SWEEPS - 1])
    return state


def volume_kernel(
    flow_ref, adj_ref, first_ref, second_ref, jfirst_ref, jsecond_ref,
    v_ref, out1_ref, out2_ref, *, nj,
):
    own, lanes = flow_ref.shape[1], flow_ref.shape[-1]
    w = SWEEPS
    even = lax.axis_index("bx") % 2 == 0
    jeven = lax.axis_index("by") % 2 == 0
    sub = lax.broadcasted_iota(jnp.int32, (nj, lanes), 0)

    def adjoint_at(comp, i):
        if 0 <= i < own:
            return adj_ref[comp, i]
        if i >= own:
            return jnp.where(even, first_ref[comp], second_ref[comp])
        return jnp.where(even, second_ref[comp], first_ref[comp])

    for i in range(own):
        jump = []
        for comp in range(5):
            here = adjoint_at(comp, i)
            diff = adjoint_at(comp, i - 1) - adjoint_at(comp, i + 1)
            one, two = jfirst_ref[comp, i : i + 1, :], jsecond_ref[comp, i : i + 1, :]
            back = jnp.where(sub == 0, jnp.where(jeven, two, one), pltpu.roll(here, 1, 0))
            ahead = jnp.where(
                sub == nj - 1, jnp.where(jeven, one, two), pltpu.roll(here, nj - 1, 0)
            )
            jump.append(diff + (back - ahead) + (edge_k(here, -1) - edge_k(here, 1)))
        rho = flow_ref[0, i]
        m = [flow_ref[comp, i] for comp in (1, 2, 3)]
        energy = flow_ref[4, i]
        inv = 1.0 / rho
        u = [x * inv for x in m]
        mu = m[0] * u[0] + m[1] * u[1] + m[2] * u[2]
        pressure = GAS * (energy - 0.5 * mu)
        q = (
            rho * jump[0]
            + (m[0] * jump[1] + m[1] * jump[2] + m[2] * jump[3])
            + (energy + pressure) * jump[4]
        )
        for comp in range(3):
            v_ref[comp, i] = 0.5 * (u[comp] * q + pressure * jump[comp + 1])
    low, high = v_ref[:, 0:w], v_ref[:, own - w : own]
    out1_ref[...] = jnp.where(even, high, low)
    out2_ref[...] = jnp.where(even, low, high)


def offsets_kernel(own_ref, first_ref, second_ref, rate_ref, v_ref, off_ref, *, rows, nj):
    lanes = own_ref.shape[-1]
    own = rows - 2 * SWEEPS
    w = SWEEPS
    even = lax.axis_index("bx") % 2 == 0
    for comp in range(3):
        v_ref[comp, 0 : own * nj, :] = own_ref[comp].reshape(own * nj, lanes)
        one = first_ref[comp].reshape(w * nj, lanes)
        two = second_ref[comp].reshape(w * nj, lanes)
        v_ref[comp, own * nj : (own + w) * nj, :] = jnp.where(even, one, two)
        v_ref[comp, (own + w) * nj : rows * nj, :] = jnp.where(even, two, one)

    valid = row_valid(rows, lanes)
    state = [[None] * 3 for _ in range(SWEEPS)]
    state = sweeps(v_ref, rate_ref, valid, state, rows, own, nj, None)
    at = 0
    for s in range(SWEEPS):
        for comp in range(3):
            x = state[s][comp]
            for part in range(x.shape[0] // own):
                off_ref[at] = x[part * own : (part + 1) * own]
                at += 1


def finish_kernel(*refs, rows, nj, count, stacked):
    own = rows - 2 * SWEEPS
    if stacked:
        v_ref, rate_ref, map_ref, off_ref, out_ref, x_ref = refs
    else:
        v_ref, rate_ref = refs[:2]
        maps = refs[2 : 2 + count - 1]
        offs = refs[1 + count : 2 * count]
        out_ref, x_ref, map_ref, off_ref = refs[2 * count :]
    lanes = v_ref.shape[-1]
    me = lax.axis_index("by")
    if not stacked:
        for mask in range(1, count):
            map_ref[me ^ mask] = maps[mask - 1][...]
            off_ref[me ^ mask] = offs[mask - 1][...]
    slots, _ = map_slots(rows, own)

    def load(ref, block, at, n):
        if n == 1:
            return ref[block, at]
        return jnp.concatenate([ref[block, at + part] for part in range(n)], axis=0)

    sizes = [rows // own] * (SWEEPS - 1) + [1]
    starts, at = {}, 0
    for s in range(SWEEPS):
        for comp in range(3):
            starts[s, comp] = at
            at += sizes[s]
    x_ref[...] = jnp.zeros(x_ref.shape, F32)

    def get(s, comp):
        a = starts[s, comp]
        return jnp.concatenate([x_ref[a + part] for part in range(sizes[s])], axis=0)

    def put(s, comp, value):
        for part in range(sizes[s]):
            x_ref[starts[s, comp] + part] = value[part * own : (part + 1) * own]

    def through(hop, carry):
        block = count - 1 - hop
        coef = {key: load(map_ref, block, *slot) for key, slot in slots.items()}
        fresh = {}
        for comp in range(3):
            x = [get(s, comp) for s in range(SWEEPS)]
            total = [load(off_ref, block, starts[s, comp], sizes[s]) for s in range(SWEEPS)]
            for s in range(SWEEPS):
                for o in sorted({o for d in range(SWEEPS - s) for o in REACH[d]}):
                    moved = x[s]
                    if o[0]:
                        moved = shift_i(moved, o[0])
                    if o[1]:
                        moved = shift_k(moved, o[1])
                    for d in range(SWEEPS - s):
                        if o in REACH[d]:
                            n = sizes[s + d] * own
                            total[s + d] = total[s + d] + coef[d, o][:n] * moved[:n]
            for s in range(SWEEPS):
                fresh[s, comp] = total[s]
        for (s, comp), value in fresh.items():
            put(s, comp, value)
        return carry

    lax.fori_loop(0, count - 1 - me, through, 0)

    valid = row_valid(rows, lanes)
    state = [[get(s, comp) for comp in range(3)] for s in range(SWEEPS)]

    def emit(j, values):
        for comp in range(3):
            out_ref[comp, pl.ds(j, own, stride=nj), :] = values[comp]

    sweeps(v_ref, rate_ref, valid, state, rows, own, nj, emit)


def product_kernel(
    flow_ref, adj_ref, faces_ref, first_ref, second_ref, jfirst_ref, jsecond_ref, out_ref, *, nj,
):
    own, lanes = flow_ref.shape[1], flow_ref.shape[-1]
    even = lax.axis_index("bx") % 2 == 0
    jeven = lax.axis_index("by") % 2 == 0
    sub = lax.broadcasted_iota(jnp.int32, (nj, lanes), 0)
    for i in range(own):
        here = [adj_ref[comp, i] for comp in range(5)]

        def beside(comp, face):
            if face == 0:
                if i + 1 < own:
                    return adj_ref[comp, i + 1]
                return jnp.where(even, first_ref[comp], second_ref[comp])
            if face == 1:
                if i > 0:
                    return adj_ref[comp, i - 1]
                return jnp.where(even, second_ref[comp], first_ref[comp])
            if face in (2, 3):
                one = jfirst_ref[comp, i : i + 1, :]
                two = jsecond_ref[comp, i : i + 1, :]
                if face == 2:
                    line = jnp.where(jeven, one, two)
                    return jnp.where(sub == nj - 1, line, pltpu.roll(here[comp], nj - 1, 0))
                line = jnp.where(jeven, two, one)
                return jnp.where(sub == 0, line, pltpu.roll(here[comp], 1, 0))
            return edge_k(here[comp], 1 if face == 4 else -1)

        rho = flow_ref[0, i]
        m = [flow_ref[comp, i] for comp in (1, 2, 3)]
        energy = flow_ref[4, i]
        inv = 1.0 / rho
        u = [x * inv for x in m]
        uu = u[0] * u[0] + u[1] * u[1] + u[2] * u[2]
        pressure = GAS * (energy - 0.5 * (rho * uu))
        enthalpy = (energy + pressure) * inv
        sound = jnp.sqrt((1.0 + GAS) * pressure * inv)
        total = None
        for face in range(6):
            s = [faces_ref[face, axis, i] for axis in range(3)]
            h = [0.5 * (here[comp] - beside(comp, face)) for comp in range(5)]
            speed = u[0] * s[0] + u[1] * s[1] + u[2] * s[2]
            area = jnp.sqrt(s[0] * s[0] + s[1] * s[1] + s[2] * s[2])
            wave = jnp.abs(speed) + sound * area
            bulk = (u[0] * h[1] + u[1] * h[2] + u[2] * h[3]) + enthalpy * h[4]
            press = (s[0] * h[1] + s[1] * h[2] + s[2] * h[3]) + speed * h[4]
            full = h[0] + bulk
            term = [
                0.5 * GAS * (uu * press) - speed * bulk + wave * h[0],
                s[0] * full - GAS * (u[0] * press) + (speed + wave) * h[1],
                s[1] * full - GAS * (u[1] * press) + (speed + wave) * h[2],
                s[2] * full - GAS * (u[2] * press) + (speed + wave) * h[3],
                GAS * press + (speed + wave) * h[4],
            ]
            total = term if total is None else [a + b for a, b in zip(total, term)]
        for comp in range(5):
            out_ref[comp, i] = total[comp]


def call(kernel, out_shape, args, scratch=(), interpret=False):
    vmem = pl.BlockSpec(memory_space=pltpu.VMEM)
    single = not isinstance(out_shape, (list, tuple))
    held = [*args, *([out_shape] if single else out_shape), *scratch]
    need = sum(4 * math.prod(a.shape) for a in held)
    return pl.pallas_call(
        kernel,
        out_shape=out_shape,
        in_specs=[vmem] * len(args),
        out_specs=vmem if single else [vmem] * len(out_shape),
        scratch_shapes=list(scratch),
        interpret=interpret,
        compiler_params=pltpu.CompilerParams(vmem_limit_bytes=need + (2 << 20)),
    )(*args)


INTERPRET = False


def on_device(flow, adjoint, faces, decay, surface_mask):
    own, nj, lanes = decay.shape
    w = SWEEPS
    rows = own + 2 * w
    nby = lax.axis_size("by")
    bx, by = lax.axis_index("bx"), lax.axis_index("by")
    even, jeven = bx % 2 == 0, by % 2 == 0

    def run(*args):
        return call(*args, interpret=INTERPRET)


    l1, l2 = ends(adjoint, 2, 1, jeven)
    l1 = swap(l1.reshape(5, own, lanes), "by", 0)
    l2 = swap(l2.reshape(5, own, lanes), "by", 1)
    retention = (1 - surface_mask).astype(F32) * decay
    r1, r2 = ends(retention, 0, w - 1, even)
    a1, a2 = ends(adjoint, 1, 1, even)
    m1 = jnp.concatenate([a1.reshape(5, nj, lanes), r1], axis=0)
    m2 = jnp.concatenate([a2.reshape(5, nj, lanes), r2], axis=0)
    m1, m2 = swap(m1, "bx", 0), swap(m2, "bx", 1)

    halo = jax.ShapeDtypeStruct((3, w, nj, lanes), F32)
    inner, h1, h2 = run(
        functools.partial(volume_kernel, nj=nj),
        [jax.ShapeDtypeStruct((3, own, nj, lanes), F32), halo, halo],
        [flow, adjoint, m1, m2, l1, l2],
    )
    h1, h2 = swap(h1, "bx", 0), swap(h2, "bx", 1)

    _, n_map = map_slots(rows, own)
    rate, maps = run(
        functools.partial(maps_kernel, rows=rows, nj=nj),
        [
            jax.ShapeDtypeStruct((rows * nj, lanes), F32),
            jax.ShapeDtypeStruct((n_map, own, lanes), F32),
        ],
        [decay, surface_mask, m1, m2],
    )
    all_maps = collect(maps, "by")

    n_off = 3 * ((SWEEPS - 1) * (rows // own) + 1)
    v, offs = run(
        functools.partial(offsets_kernel, rows=rows, nj=nj),
        [
            jax.ShapeDtypeStruct((3, rows * nj, lanes), F32),
            jax.ShapeDtypeStruct((n_off, own, lanes), F32),
        ],
        [inner, h1, h2, rate],
    )
    all_offs = collect(offs, "by")

    product = run(
        functools.partial(product_kernel, nj=nj),
        jax.ShapeDtypeStruct(flow.shape, F32),
        [flow, adjoint, faces, m1, m2, l1, l2],
    )

    stacked = len(all_maps) == 1 and nby != 2
    scratch = [pltpu.VMEM((n_off, own, lanes), F32)]
    if not stacked:
        scratch += [
            pltpu.VMEM((nby, n_map, own, lanes), F32),
            pltpu.VMEM((nby, n_off, own, lanes), F32),
        ]
    warp = run(
        functools.partial(finish_kernel, rows=rows, nj=nj, count=nby, stacked=stacked),
        jax.ShapeDtypeStruct((3, own * nj, lanes), F32),
        [v, rate, *all_maps, *all_offs],
        scratch,
    )
    return (product, warp.reshape(3, own, nj, lanes))


def solution(mesh):
    return jax.shard_map(
        on_device,
        mesh=mesh,
        in_specs=(
            P(None, "bx", "by", None),
            P(None, "bx", "by", None),
            P(None, None, "bx", "by", None),
            P("bx", "by", None),
            P("bx", "by", None),
        ),
        out_specs=(P(None, "bx", "by", None), P(None, "bx", "by", None)),
        check_vma=False,
    )
```

```python
import functools
import math

import jax
import jax.numpy as jnp
from jax import lax
from jax.experimental import pallas as pl
from jax.experimental.pallas import tpu as pltpu
from jax.sharding import PartitionSpec as P

SWEEPS = 4
KAPPA = 0.15
GAS = 0.4

F32 = jnp.float32

REACH = [[(0, 0)]]
for _ in range(SWEEPS - 1):
    REACH.append(
        sorted({(i + a, k + b) for i, k in REACH[-1] for a, b in ((1, 0), (-1, 0), (0, 1), (0, -1))})
    )


def matching(axis, first):
    count = lax.axis_size(axis)
    pairs = [(i, i + 1) for i in range(first, count - 1, 2)]
    return pairs + [(b, a) for a, b in pairs]


def swap(x, axis, first):
    return lax.ppermute(x, axis, matching(axis, first))


def flip(x, axis, mask):
    count = lax.axis_size(axis)
    return lax.ppermute(x, axis, [(i, i ^ mask) for i in range(count)])


def direct(count):
    return count in (2, 4, 8)


def collect(x, axis):
    count = lax.axis_size(axis)
    if not direct(count):
        return [lax.all_gather(x, axis)]
    near = flip(x, axis, 1)[None]
    far = [flip(x, axis, m) for m in range(2, count, 2)]
    if not far:
        return [near]
    far = jnp.stack(far)
    return [near, far, flip(far, axis, 1)]


def sources(count):
    far = list(range(2, count, 2))
    return [[1], far, [m + 1 for m in far]] if far else [[1]]


def shift_i(x, step):
    rows = x.shape[0]
    return pltpu.roll(x, (-step) % rows, 0)


def shift_k(x, step):
    lanes = x.shape[1]
    return pltpu.roll(x, (-step) % lanes, 1)


def edge_k(x, step):
    lane = lax.broadcasted_iota(jnp.int32, x.shape, 1)
    edge = x.shape[1] - 1 if step > 0 else 0
    return jnp.where(lane == edge, 0.0, shift_k(x, step))


def move(x, step):
    return shift_i(x, step[0]) if step[0] else edge_k(x, step[1])


def couple(x):
    return (shift_i(x, 1) + shift_i(x, -1)) + (edge_k(x, 1) + edge_k(x, -1))


def row_valid(rows, lanes):
    own = rows - 2 * SWEEPS
    place = lax.axis_index("bx")
    above = jnp.where(place < lax.axis_size("bx") - 1, SWEEPS - 1, 0)
    below = jnp.where(place > 0, SWEEPS - 1, 0)
    row = lax.broadcasted_iota(jnp.int32, (rows, lanes), 0)
    inside = (row < own + above) | (row >= rows - below)
    return jnp.where(inside, 1.0, 0.0).astype(F32)


def pack_kernel(
    flow_hbm, adj_hbm, decay_hbm, mask_hbm,
    flow_ref, adj_ref, rate_ref, line1_ref, line2_ref, rim1_ref, rim2_ref,
    decay_ref, mask_ref, sems, *, own, nj,
):
    pairs = [(adj_hbm, adj_ref), (decay_hbm, decay_ref), (mask_hbm, mask_ref), (flow_hbm, flow_ref)]
    copies = [pltpu.make_async_copy(a, b, sems.at[n]) for n, (a, b) in enumerate(pairs)]
    for copy in copies:
        copy.start()
    even = lax.axis_index("bx") % 2 == 0
    jeven = lax.axis_index("by") % 2 == 0
    copies[0].wait()
    for comp in range(5):
        bottom = adj_ref[comp, pl.ds(0, own, stride=nj), :]
        top = adj_ref[comp, pl.ds(nj - 1, own, stride=nj), :]
        line1_ref[comp] = jnp.where(jeven, top, bottom)
        line2_ref[comp] = jnp.where(jeven, bottom, top)
        low = adj_ref[comp, 0:nj, :]
        high = adj_ref[comp, (own - 1) * nj : own * nj, :]
        rim1_ref[comp] = jnp.where(even, high, low)
        rim2_ref[comp] = jnp.where(even, low, high)
    copies[1].wait()
    copies[2].wait()
    rate_ref[...] = (1 - mask_ref[...]).astype(F32) * decay_ref[...]
    for row in range(SWEEPS - 1):
        low = rate_ref[row * nj : (row + 1) * nj, :]
        at = own - (SWEEPS - 1) + row
        high = rate_ref[at * nj : (at + 1) * nj, :]
        rim1_ref[5 + row] = jnp.where(even, high, low)
        rim2_ref[5 + row] = jnp.where(even, low, high)
    copies[3].wait()


def pack_rows(parts, width):
    total = parts[0]
    row = lax.broadcasted_iota(jnp.int32, total.shape, 0)
    size = total.shape[0]
    for n, part in enumerate(parts[1:], 1):
        moved = pltpu.roll(part, 2 * width * n, 0)
        place = (row - 2 * width * n + width + size) % size
        total = jnp.where(place < 2 * width, moved, total)
    return total


def unpack_rows(tile, n, width):
    return pltpu.roll(tile, (-2 * width * n) % tile.shape[0], 0) if n else tile


def layout(groups, own):
    places, at = {}, 0
    for keys, width in groups:
        for key in keys:
            places[key] = [at, None, 0, width]
            at += 1
        if width:
            share = max(1, own // (2 * width))
            for n, key in enumerate(keys):
                places[key][1] = at + n // share
                places[key][2] = n % share
            at += -(-len(keys) // share)
    return places, at


def map_layout(own):
    return layout([([(d, o) for o in REACH[d]], SWEEPS - 1 - d) for d in range(SWEEPS)], own)


def off_layout(own):
    return layout([([(s, c) for c in range(3)], SWEEPS - 1 - s) for s in range(SWEEPS)], own)


def store_tiles(ref, places, values, own):
    halos = {}
    for key, (main, halo, position, width) in places.items():
        ref[main] = values[key][0:own]
        if halo is not None:
            halos.setdefault((halo, width), []).append(values[key][own : 2 * own])
    for (halo, width), parts in halos.items():
        ref[halo] = pack_rows(parts, width)


def load_tiles(ref, block, place):
    main, halo, position, width = place
    tile = ref[block, main]
    if halo is None:
        return tile
    return jnp.concatenate([tile, unpack_rows(ref[block, halo], position, width)], axis=0)


def maps_kernel(own_ref, first_ref, second_ref, ext_ref, map_ref, all_ref, *, rows, nj):
    lanes = own_ref.shape[-1]
    own = rows - 2 * SWEEPS
    wide = SWEEPS - 1
    rate_ref = ext_ref
    rate_ref[0 : own * nj, :] = own_ref[...]
    even = lax.axis_index("bx") % 2 == 0
    first = first_ref[5 : 5 + wide].reshape(wide * nj, lanes)
    second = second_ref[5 : 5 + wide].reshape(wide * nj, lanes)
    rate_ref[own * nj : (own + wide) * nj, :] = jnp.where(even, first, second)
    rate_ref[(own + wide) * nj : (rows - wide) * nj, :] = jnp.zeros((2 * nj, lanes), F32)
    rate_ref[(rows - wide) * nj : rows * nj, :] = jnp.where(even, second, first)

    valid = row_valid(rows, lanes)
    coef = [{o: None for o in REACH[d]} for d in range(SWEEPS)]
    for j in range(nj - 1, -1, -1):
        rate = rate_ref[pl.ds(j, rows, stride=nj), :]
        gain = KAPPA * (valid - rate)
        old = coef[0][(0, 0)]
        coef[0][(0, 0)] = rate if old is None else rate * old
        for d in range(1, SWEEPS):
            n = own if d == SWEEPS - 1 else rows
            total = {o: None for o in REACH[d]}
            for o, c in coef[d - 1].items():
                for step in ((1, 0), (-1, 0), (0, 1), (0, -1)):
                    moved = move(c, step)[:n]
                    goal = (o[0] + step[0], o[1] + step[1])
                    total[goal] = moved if total[goal] is None else total[goal] + moved
            for o in REACH[d]:
                fresh = gain[:n] * total[o]
                old = coef[d][o]
                coef[d][o] = fresh if old is None else rate[:n] * old + fresh
        at = 0
        for d in range(SWEEPS):
            for o in REACH[d]:
                all_ref[at, j] = coef[d][o][:own]
                at += 1
    places, _ = map_layout(own)
    store_tiles(map_ref, places, {(d, o): coef[d][o] for d, o in places}, own)


def sweeps(v_ref, rate_ref, valid, state, rows, own, nj, emit):
    comps = v_ref.shape[0]
    for j in range(nj - 1, -1, -1):
        rate = rate_ref[pl.ds(j, rows, stride=nj), :]
        rest = valid - rate
        base = [v_ref[c, pl.ds(j, rows, stride=nj), :] for c in range(comps)]
        before = base
        for s in range(SWEEPS):
            n = own if s == SWEEPS - 1 else rows
            now = []
            for c in range(comps):
                source = base[c][:n] + KAPPA * couple(before[c])[:n]
                new = rest[:n] * source
                if state[s][c] is not None:
                    new = new + rate[:n] * state[s][c]
                now.append(new)
            state[s] = now
            before = now
        if emit is not None:
            emit(j, state[SWEEPS - 1])
    return state


def volume_kernel(
    flow_ref, adj_ref, first_ref, second_ref, jfirst_ref, jsecond_ref,
    v_ref, out1_ref, out2_ref, *, nj,
):
    own, lanes = flow_ref.shape[1], flow_ref.shape[-1]
    w = SWEEPS
    even = lax.axis_index("bx") % 2 == 0
    jeven = lax.axis_index("by") % 2 == 0
    sub = lax.broadcasted_iota(jnp.int32, (nj, lanes), 0)

    def adjoint_at(comp, i):
        if 0 <= i < own:
            return adj_ref[comp, i]
        if i >= own:
            return jnp.where(even, first_ref[comp], second_ref[comp])
        return jnp.where(even, second_ref[comp], first_ref[comp])

    for i in range(own):
        jump = []
        for comp in range(5):
            here = adjoint_at(comp, i)
            diff = adjoint_at(comp, i - 1) - adjoint_at(comp, i + 1)
            one, two = jfirst_ref[comp, i : i + 1, :], jsecond_ref[comp, i : i + 1, :]
            back = jnp.where(sub == 0, jnp.where(jeven, two, one), pltpu.roll(here, 1, 0))
            ahead = jnp.where(
                sub == nj - 1, jnp.where(jeven, one, two), pltpu.roll(here, nj - 1, 0)
            )
            jump.append(diff + (back - ahead) + (edge_k(here, -1) - edge_k(here, 1)))
        rho = flow_ref[0, i]
        m = [flow_ref[comp, i] for comp in (1, 2, 3)]
        energy = flow_ref[4, i]
        inv = 1.0 / rho
        u = [x * inv for x in m]
        mu = m[0] * u[0] + m[1] * u[1] + m[2] * u[2]
        pressure = GAS * (energy - 0.5 * mu)
        q = (
            rho * jump[0]
            + (m[0] * jump[1] + m[1] * jump[2] + m[2] * jump[3])
            + (energy + pressure) * jump[4]
        )
        for comp in range(3):
            v_ref[comp, i] = 0.5 * (u[comp] * q + pressure * jump[comp + 1])
    low, high = v_ref[:, 0:w], v_ref[:, own - w : own]
    out1_ref[...] = jnp.where(even, high, low)
    out2_ref[...] = jnp.where(even, low, high)


def offsets_kernel(own_ref, first_ref, second_ref, rate_ref, off_ref, last_ref, v_ref, *, rows, nj):
    lanes = own_ref.shape[-1]
    own = rows - 2 * SWEEPS
    w = SWEEPS
    even = lax.axis_index("bx") % 2 == 0
    for comp in range(3):
        v_ref[comp, 0 : own * nj, :] = own_ref[comp].reshape(own * nj, lanes)
        one = first_ref[comp].reshape(w * nj, lanes)
        two = second_ref[comp].reshape(w * nj, lanes)
        v_ref[comp, own * nj : (own + w) * nj, :] = jnp.where(even, one, two)
        v_ref[comp, (own + w) * nj : rows * nj, :] = jnp.where(even, two, one)

    valid = row_valid(rows, lanes)
    state = [[None] * 3 for _ in range(SWEEPS)]

    def emit(j, values):
        for comp in range(3):
            last_ref[comp, j] = values[comp]

    state = sweeps(v_ref, rate_ref, valid, state, rows, own, nj, emit)
    places, _ = off_layout(own)
    store_tiles(off_ref, places, {(s, c): state[s][c] for s, c in places}, own)


def finish_kernel(*refs, own, nj, count):
    last_ref, all_ref = refs[:2]
    if direct(count):
        groups = sources(count)
        n = len(groups)
        maps, offs = refs[2 : 2 + n], refs[2 + n : 2 + 2 * n]
        out_ref, x_ref, map_ref, off_ref = refs[2 + 2 * n :]
    else:
        map_ref, off_ref, out_ref, x_ref = refs[2:]
    me = lax.axis_index("by")
    if direct(count):
        for group, mask_list in enumerate(groups):
            for n, mask in enumerate(mask_list):
                map_ref[me ^ mask] = maps[group][n]
                off_ref[me ^ mask] = offs[group][n]
    map_places, _ = map_layout(own)
    off_places, _ = off_layout(own)

    def size(s):
        return own if s == SWEEPS - 1 else 2 * own

    def get(s, comp):
        return x_ref[s, comp, 0 : size(s), :]

    def offset_of(x, o):
        if o[0]:
            x = shift_i(x, o[0])
        return shift_k(x, o[1]) if o[1] else x

    x_ref[...] = jnp.zeros(x_ref.shape, F32)

    def through(hop, carry):
        block = count - 1 - hop
        coef = {key: load_tiles(map_ref, block, place) for key, place in map_places.items()}
        fresh = {}
        for comp in range(3):
            total = [load_tiles(off_ref, block, off_places[s, comp]) for s in range(SWEEPS)]
            for s in range(SWEEPS):
                x = get(s, comp)
                for o in sorted({o for d in range(SWEEPS - s) for o in REACH[d]}):
                    moved = offset_of(x, o)
                    for d in range(SWEEPS - s):
                        if o in REACH[d]:
                            n = size(s + d)
                            total[s + d] = total[s + d] + coef[d, o][:n] * moved[:n]
            for s in range(SWEEPS):
                fresh[s, comp] = total[s]
        for (s, comp), value in fresh.items():
            x_ref[s, comp, 0 : size(s), :] = value
        return carry

    lax.fori_loop(0, count - 1 - me, through, 0)

    total = [[last_ref[comp, j] for j in range(nj)] for comp in range(3)]
    at = 0
    for d in range(SWEEPS):
        x = [get(SWEEPS - 1 - d, comp) for comp in range(3)]
        for o in REACH[d]:
            moved = [offset_of(x[comp], o)[:own] for comp in range(3)]
            for j in range(nj):
                c = all_ref[at, j]
                for comp in range(3):
                    total[comp][j] = total[comp][j] + c * moved[comp]
            at += 1
    for comp in range(3):
        for j in range(nj):
            out_ref[comp, pl.ds(j, own, stride=nj), :] = total[comp][j]


def product_kernel(
    flow_ref, adj_ref, faces_ref, first_ref, second_ref, jfirst_ref, jsecond_ref, out_ref, *, nj,
):
    own, lanes = flow_ref.shape[1], flow_ref.shape[-1]
    even = lax.axis_index("bx") % 2 == 0
    jeven = lax.axis_index("by") % 2 == 0
    sub = lax.broadcasted_iota(jnp.int32, (nj, lanes), 0)
    for i in range(own):
        here = [adj_ref[comp, i] for comp in range(5)]

        def beside(comp, face):
            if face == 0:
                if i + 1 < own:
                    return adj_ref[comp, i + 1]
                return jnp.where(even, first_ref[comp], second_ref[comp])
            if face == 1:
                if i > 0:
                    return adj_ref[comp, i - 1]
                return jnp.where(even, second_ref[comp], first_ref[comp])
            if face in (2, 3):
                one = jfirst_ref[comp, i : i + 1, :]
                two = jsecond_ref[comp, i : i + 1, :]
                if face == 2:
                    line = jnp.where(jeven, one, two)
                    return jnp.where(sub == nj - 1, line, pltpu.roll(here[comp], nj - 1, 0))
                line = jnp.where(jeven, two, one)
                return jnp.where(sub == 0, line, pltpu.roll(here[comp], 1, 0))
            return edge_k(here[comp], 1 if face == 4 else -1)

        rho = flow_ref[0, i]
        m = [flow_ref[comp, i] for comp in (1, 2, 3)]
        energy = flow_ref[4, i]
        inv = 1.0 / rho
        u = [x * inv for x in m]
        uu = u[0] * u[0] + u[1] * u[1] + u[2] * u[2]
        pressure = GAS * (energy - 0.5 * (rho * uu))
        enthalpy = (energy + pressure) * inv
        sound = jnp.sqrt((1.0 + GAS) * pressure * inv)
        total = None
        for face in range(6):
            s = [faces_ref[face, axis, i] for axis in range(3)]
            h = [0.5 * (here[comp] - beside(comp, face)) for comp in range(5)]
            speed = u[0] * s[0] + u[1] * s[1] + u[2] * s[2]
            area = jnp.sqrt(s[0] * s[0] + s[1] * s[1] + s[2] * s[2])
            wave = jnp.abs(speed) + sound * area
            bulk = (u[0] * h[1] + u[1] * h[2] + u[2] * h[3]) + enthalpy * h[4]
            press = (s[0] * h[1] + s[1] * h[2] + s[2] * h[3]) + speed * h[4]
            full = h[0] + bulk
            term = [
                0.5 * GAS * (uu * press) - speed * bulk + wave * h[0],
                s[0] * full - GAS * (u[0] * press) + (speed + wave) * h[1],
                s[1] * full - GAS * (u[1] * press) + (speed + wave) * h[2],
                s[2] * full - GAS * (u[2] * press) + (speed + wave) * h[3],
                GAS * press + (speed + wave) * h[4],
            ]
            total = term if total is None else [a + b for a, b in zip(total, term)]
        for comp in range(5):
            out_ref[comp, i] = total[comp]


def call(kernel, out_shape, args, scratch=(), space=pltpu.VMEM, interpret=False):
    vmem = pl.BlockSpec(memory_space=pltpu.VMEM)
    single = not isinstance(out_shape, (list, tuple))
    held = [*args, *([out_shape] if single else out_shape), *scratch]
    need = sum(4 * math.prod(a.shape) for a in held)
    return pl.pallas_call(
        kernel,
        out_shape=out_shape,
        in_specs=[pl.BlockSpec(memory_space=space)] * len(args),
        out_specs=vmem if single else [vmem] * len(out_shape),
        scratch_shapes=list(scratch),
        interpret=interpret,
        compiler_params=pltpu.CompilerParams(vmem_limit_bytes=need + (2 << 20)),
    )(*args)


INTERPRET = False


def on_device(flow, adjoint, faces, decay, surface_mask):
    own, nj, lanes = decay.shape
    w = SWEEPS
    rows = own + 2 * w
    nby = lax.axis_size("by")

    def run(*args):
        return call(*args, interpret=INTERPRET)


    def shape(*dims):
        return jax.ShapeDtypeStruct(dims, F32)

    flat = [flow.reshape(5, own * nj, lanes), adjoint.reshape(5, own * nj, lanes)]
    flat += [decay.reshape(own * nj, lanes), surface_mask.reshape(own * nj, lanes)]
    rim = shape(5 + w - 1, nj, lanes)
    flow, adjoint, retention, l1, l2, m1, m2 = run(
        functools.partial(pack_kernel, own=own, nj=nj),
        [shape(5, own * nj, lanes)] * 2
        + [shape(own * nj, lanes)]
        + [shape(5, own, lanes)] * 2
        + [rim] * 2,
        flat,
        [
            pltpu.VMEM((own * nj, lanes), F32),
            pltpu.VMEM((own * nj, lanes), jnp.int32),
            pltpu.SemaphoreType.DMA((4,)),
        ],
        pltpu.HBM,
    )
    flow, adjoint = flow.reshape(5, own, nj, lanes), adjoint.reshape(5, own, nj, lanes)
    l1, l2 = swap(l1, "by", 0), swap(l2, "by", 1)
    m1, m2 = swap(m1, "bx", 0), swap(m2, "bx", 1)

    halo = shape(3, w, nj, lanes)
    inner, h1, h2 = run(
        functools.partial(volume_kernel, nj=nj),
        [shape(3, own, nj, lanes), halo, halo],
        [flow, adjoint, m1, m2, l1, l2],
    )
    h1, h2 = swap(h1, "bx", 0), swap(h2, "bx", 1)

    _, n_map = map_layout(own)
    _, n_off = off_layout(own)
    rate, maps, all_coef = run(
        functools.partial(maps_kernel, rows=rows, nj=nj),
        [
            shape(rows * nj, lanes),
            shape(n_map, own, lanes),
            shape(sum(map(len, REACH)), nj, own, lanes),
        ],
        [retention, m1, m2],
    )
    all_maps = collect(maps, "by")

    offs, last = run(
        functools.partial(offsets_kernel, rows=rows, nj=nj),
        [shape(n_off, own, lanes), shape(3, nj, own, lanes)],
        [inner, h1, h2, rate],
        [pltpu.VMEM((3, rows * nj, lanes), F32)],
    )
    all_offs = collect(offs, "by")

    product = run(
        functools.partial(product_kernel, nj=nj),
        jax.ShapeDtypeStruct(flow.shape, F32),
        [flow, adjoint, faces, m1, m2, l1, l2],
    )

    scratch = [pltpu.VMEM((SWEEPS, 3, 2 * own, lanes), F32)]
    if direct(nby):
        scratch += [
            pltpu.VMEM((nby, n_map, own, lanes), F32),
            pltpu.VMEM((nby, n_off, own, lanes), F32),
        ]
    warp = run(
        functools.partial(finish_kernel, own=own, nj=nj, count=nby),
        shape(3, own * nj, lanes),
        [last, all_coef, *all_maps, *all_offs],
        scratch,
    )
    return (product, warp.reshape(3, own, nj, lanes))


def solution(mesh):
    return jax.shard_map(
        on_device,
        mesh=mesh,
        in_specs=(
            P(None, "bx", "by", None),
            P(None, "bx", "by", None),
            P(None, None, "bx", "by", None),
            P("bx", "by", None),
            P("bx", "by", None),
        ),
        out_specs=(P(None, "bx", "by", None), P(None, "bx", "by", None)),
        check_vma=False,
    )
```

```python
import functools
import math

import jax
import jax.numpy as jnp
from jax import lax
from jax.experimental import pallas as pl
from jax.experimental.pallas import tpu as pltpu
from jax.sharding import PartitionSpec as P

SWEEPS = 4
KAPPA = 0.15
GAS = 0.4

F32 = jnp.float32

REACH = [[(0, 0)]]
for _ in range(SWEEPS - 1):
    REACH.append(
        sorted({(i + a, k + b) for i, k in REACH[-1] for a, b in ((1, 0), (-1, 0), (0, 1), (0, -1))})
    )


def matching(axis, first):
    count = lax.axis_size(axis)
    pairs = [(i, i + 1) for i in range(first, count - 1, 2)]
    return pairs + [(b, a) for a, b in pairs]


def swap(x, axis, first):
    return lax.ppermute(x, axis, matching(axis, first))


def flip(x, axis, mask):
    count = lax.axis_size(axis)
    return lax.ppermute(x, axis, [(i, i ^ mask) for i in range(count)])


def direct(count):
    return count in (2, 4, 8)


def collect(x, axis):
    count = lax.axis_size(axis)
    if not direct(count):
        return [lax.all_gather(x, axis)]
    near = flip(x, axis, 1)[None]
    far = [flip(x, axis, m) for m in range(2, count, 2)]
    if not far:
        return [near]
    far = jnp.stack(far)
    return [near, far, flip(far, axis, 1)]


def sources(count):
    far = list(range(2, count, 2))
    return [[1], far, [m + 1 for m in far]] if far else [[1]]


def shift_i(x, step, n):
    size = x[0].shape[0]
    turned = [pltpu.roll(tile, (-step) % size, 0) for tile in x]
    row = lax.broadcasted_iota(jnp.int32, x[0].shape, 0)
    edge = row == (size - 1 if step > 0 else 0)
    return [jnp.where(edge, turned[1 - t], turned[t]) for t in range(n)]


def roll_k(tile, step):
    return pltpu.roll(tile, (-step) % tile.shape[1], 1)


def edge_k(tile, step):
    lane = lax.broadcasted_iota(jnp.int32, tile.shape, 1)
    edge = tile.shape[1] - 1 if step > 0 else 0
    return jnp.where(lane == edge, 0.0, roll_k(tile, step))


def move(x, step, n):
    return shift_i(x, step[0], n) if step[0] else [edge_k(tile, step[1]) for tile in x[:n]]


def couple(x, n):
    up, down = shift_i(x, 1, n), shift_i(x, -1, n)
    return [(up[t] + down[t]) + (edge_k(x[t], 1) + edge_k(x[t], -1)) for t in range(n)]


def at_j(ref, j, rows, nj, tiles):
    size = rows // tiles
    return [ref[pl.ds(j + t * size * nj, size, stride=nj), :] for t in range(tiles)]


def row_valid(rows, lanes):
    own = rows - 2 * SWEEPS
    place = lax.axis_index("bx")
    above = jnp.where(place < lax.axis_size("bx") - 1, SWEEPS - 1, 0)
    below = jnp.where(place > 0, SWEEPS - 1, 0)
    row = lax.broadcasted_iota(jnp.int32, (rows, lanes), 0)
    inside = (row < own + above) | (row >= rows - below)
    valid = jnp.where(inside, 1.0, 0.0).astype(F32)
    return [valid[t * own : (t + 1) * own] for t in range(rows // own)]


def pack_kernel(
    flow_hbm, adj_hbm, decay_hbm, mask_hbm,
    flow_ref, adj_ref, rate_ref, line1_ref, line2_ref, rim1_ref, rim2_ref,
    decay_ref, mask_ref, sems, *, own, nj,
):
    pairs = [(adj_hbm, adj_ref), (decay_hbm, decay_ref), (mask_hbm, mask_ref), (flow_hbm, flow_ref)]
    copies = [pltpu.make_async_copy(a, b, sems.at[n]) for n, (a, b) in enumerate(pairs)]
    for copy in copies:
        copy.start()
    even = lax.axis_index("bx") % 2 == 0
    jeven = lax.axis_index("by") % 2 == 0
    copies[0].wait()
    for comp in range(5):
        bottom = adj_ref[comp, pl.ds(0, own, stride=nj), :]
        top = adj_ref[comp, pl.ds(nj - 1, own, stride=nj), :]
        line1_ref[comp] = jnp.where(jeven, top, bottom)
        line2_ref[comp] = jnp.where(jeven, bottom, top)
        low = adj_ref[comp, 0:nj, :]
        high = adj_ref[comp, (own - 1) * nj : own * nj, :]
        rim1_ref[comp] = jnp.where(even, high, low)
        rim2_ref[comp] = jnp.where(even, low, high)
    copies[1].wait()
    copies[2].wait()
    rate_ref[...] = (1 - mask_ref[...]).astype(F32) * decay_ref[...]
    for row in range(SWEEPS - 1):
        low = rate_ref[row * nj : (row + 1) * nj, :]
        at = own - (SWEEPS - 1) + row
        high = rate_ref[at * nj : (at + 1) * nj, :]
        rim1_ref[5 + row] = jnp.where(even, high, low)
        rim2_ref[5 + row] = jnp.where(even, low, high)
    copies[3].wait()


def pack_rows(parts, width):
    total = parts[0]
    row = lax.broadcasted_iota(jnp.int32, total.shape, 0)
    size = total.shape[0]
    for n, part in enumerate(parts[1:], 1):
        moved = pltpu.roll(part, 2 * width * n, 0)
        place = (row - 2 * width * n + width + size) % size
        total = jnp.where(place < 2 * width, moved, total)
    return total


def unpack_rows(tile, n, width):
    return pltpu.roll(tile, (-2 * width * n) % tile.shape[0], 0) if n else tile


def layout(groups, own):
    places, at = {}, 0
    for keys, width in groups:
        for key in keys:
            places[key] = [at, None, 0, width]
            at += 1
        if width:
            share = max(1, own // (2 * width))
            for n, key in enumerate(keys):
                places[key][1] = at + n // share
                places[key][2] = n % share
            at += -(-len(keys) // share)
    return places, at


def map_layout(own):
    return layout([([(d, o) for o in REACH[d]], SWEEPS - 1 - d) for d in range(SWEEPS)], own)


def off_layout(own):
    return layout([([(s, c) for c in range(3)], SWEEPS - 1 - s) for s in range(SWEEPS)], own)


def store_tiles(ref, places, values):
    halos = {}
    for key, (main, halo, position, width) in places.items():
        ref[main] = values[key][0]
        if halo is not None:
            halos.setdefault((halo, width), []).append(values[key][1])
    for (halo, width), parts in halos.items():
        ref[halo] = pack_rows(parts, width)


def load_tiles(ref, block, place):
    main, halo, position, width = place
    tile = ref[block, main]
    if halo is None:
        return [tile]
    return [tile, unpack_rows(ref[block, halo], position, width)]


def maps_kernel(
    own_ref, first_ref, second_ref, rate_t, gain_t, map_ref, all_ref, ext_ref, side_ref, *, rows, nj,
):
    lanes = own_ref.shape[-1]
    own = rows - 2 * SWEEPS
    wide = SWEEPS - 1
    rate_ref = ext_ref
    rate_ref[0 : own * nj, :] = own_ref[...]
    even = lax.axis_index("bx") % 2 == 0
    first = first_ref[5 : 5 + wide].reshape(wide * nj, lanes)
    second = second_ref[5 : 5 + wide].reshape(wide * nj, lanes)
    rate_ref[own * nj : (own + wide) * nj, :] = jnp.where(even, first, second)
    rate_ref[(own + wide) * nj : (rows - wide) * nj, :] = jnp.zeros((2 * nj, lanes), F32)
    rate_ref[(rows - wide) * nj : rows * nj, :] = jnp.where(even, second, first)

    valid = row_valid(rows, lanes)
    for j in range(nj):
        rate = at_j(rate_ref, j, rows, nj, 2)
        for t in range(2):
            rate_t[j, t] = rate[t]
            gain_t[j, t] = KAPPA * (valid[t] - rate[t])
    places, _ = map_layout(own)
    final, at, begin = {}, 0, 0
    for d in range(SWEEPS):
        n = 1 if d == SWEEPS - 1 else 2
        index = {o: at + i for i, o in enumerate(REACH[d])}
        before = {o: begin + i for i, o in enumerate(REACH[d - 1])} if d else {}
        coef = {o: None for o in REACH[d]}
        for j in range(nj - 1, -1, -1):
            rate = [rate_t[j, t] for t in range(n)]
            if d == 0:
                old = coef[0, 0]
                coef[0, 0] = rate if old is None else [r * c for r, c in zip(rate, old)]
            else:
                total = {o: None for o in REACH[d]}
                for o, i in before.items():
                    c = [all_ref[i, j], side_ref[i, j]]
                    for step in ((1, 0), (-1, 0), (0, 1), (0, -1)):
                        moved = move(c, step, n)
                        goal = (o[0] + step[0], o[1] + step[1])
                        held = total[goal]
                        total[goal] = moved if held is None else [p + q for p, q in zip(held, moved)]
                gain = [gain_t[j, t] for t in range(n)]
                for o in REACH[d]:
                    fresh = [gain[t] * total[o][t] for t in range(n)]
                    old = coef[o]
                    if old is not None:
                        fresh = [rate[t] * old[t] + fresh[t] for t in range(n)]
                    coef[o] = fresh
            for o in REACH[d]:
                all_ref[index[o], j] = coef[o][0]
                if n == 2:
                    side_ref[index[o], j] = coef[o][1]
        final.update({(d, o): coef[o] for o in REACH[d]})
        begin, at = at, at + len(REACH[d])
    store_tiles(map_ref, places, final)


def sweeps(v_ref, rate_t, gain_t, warp_ref, rows, nj, last_ref):
    comps = v_ref.shape[0]
    ends_at = {}
    for s in range(SWEEPS):
        n = 1 if s == SWEEPS - 1 else 2
        state = [None] * comps
        for j in range(nj - 1, -1, -1):
            rate = [rate_t[j, t] for t in range(n)]
            gain = [gain_t[j, t] for t in range(n)]
            for c in range(comps):
                if s == 0:
                    before = at_j(v_ref.at[c], j, rows, nj, 2)
                    base = [gain[t] * (before[t] * (1.0 / KAPPA)) for t in range(n)]
                    for t in range(n):
                        warp_ref[SWEEPS - 1, c, j, t] = base[t]
                else:
                    before = [warp_ref[s - 1, c, j, t] for t in range(2)]
                    base = [warp_ref[SWEEPS - 1, c, j, t] for t in range(n)]
                near = couple(before, n)
                new = [base[t] + gain[t] * near[t] for t in range(n)]
                if state[c] is not None:
                    new = [new[t] + rate[t] * state[c][t] for t in range(n)]
                state[c] = new
                if s == SWEEPS - 1:
                    last_ref[c, j] = new[0]
                else:
                    for t in range(n):
                        warp_ref[s, c, j, t] = new[t]
        for c in range(comps):
            ends_at[s, c] = state[c]
    return ends_at


def volume_kernel(
    flow_ref, adj_ref, first_ref, second_ref, jfirst_ref, jsecond_ref,
    v_ref, out1_ref, out2_ref, *, nj,
):
    own, lanes = flow_ref.shape[1], flow_ref.shape[-1]
    w = SWEEPS
    even = lax.axis_index("bx") % 2 == 0
    jeven = lax.axis_index("by") % 2 == 0
    sub = lax.broadcasted_iota(jnp.int32, (nj, lanes), 0)

    def adjoint_at(comp, i):
        if 0 <= i < own:
            return adj_ref[comp, i]
        if i >= own:
            return jnp.where(even, first_ref[comp], second_ref[comp])
        return jnp.where(even, second_ref[comp], first_ref[comp])

    for i in range(own):
        jump = []
        for comp in range(5):
            here = adjoint_at(comp, i)
            diff = adjoint_at(comp, i - 1) - adjoint_at(comp, i + 1)
            one, two = jfirst_ref[comp, i : i + 1, :], jsecond_ref[comp, i : i + 1, :]
            back = jnp.where(sub == 0, jnp.where(jeven, two, one), pltpu.roll(here, 1, 0))
            ahead = jnp.where(
                sub == nj - 1, jnp.where(jeven, one, two), pltpu.roll(here, nj - 1, 0)
            )
            jump.append(diff + (back - ahead) + (edge_k(here, -1) - edge_k(here, 1)))
        rho = flow_ref[0, i]
        m = [flow_ref[comp, i] for comp in (1, 2, 3)]
        energy = flow_ref[4, i]
        inv = 1.0 / rho
        u = [x * inv for x in m]
        mu = m[0] * u[0] + m[1] * u[1] + m[2] * u[2]
        pressure = GAS * (energy - 0.5 * mu)
        q = (
            rho * jump[0]
            + (m[0] * jump[1] + m[1] * jump[2] + m[2] * jump[3])
            + (energy + pressure) * jump[4]
        )
        for comp in range(3):
            v_ref[comp, i] = 0.5 * (u[comp] * q + pressure * jump[comp + 1])
    low, high = v_ref[:, 0:w], v_ref[:, own - w : own]
    out1_ref[...] = jnp.where(even, high, low)
    out2_ref[...] = jnp.where(even, low, high)


def offsets_kernel(
    own_ref, first_ref, second_ref, rate_t, gain_t, off_ref, last_ref, v_ref, warp_ref, *, rows, nj,
):
    lanes = own_ref.shape[-1]
    own = rows - 2 * SWEEPS
    w = SWEEPS
    even = lax.axis_index("bx") % 2 == 0
    for comp in range(3):
        v_ref[comp, 0 : own * nj, :] = own_ref[comp].reshape(own * nj, lanes)
        one = first_ref[comp].reshape(w * nj, lanes)
        two = second_ref[comp].reshape(w * nj, lanes)
        v_ref[comp, own * nj : (own + w) * nj, :] = jnp.where(even, one, two)
        v_ref[comp, (own + w) * nj : rows * nj, :] = jnp.where(even, two, one)

    ends_at = sweeps(v_ref, rate_t, gain_t, warp_ref, rows, nj, last_ref)
    places, _ = off_layout(own)
    store_tiles(off_ref, places, ends_at)


def finish_kernel(*refs, own, nj, count):
    last_ref, all_ref = refs[:2]
    if direct(count):
        groups = sources(count)
        n = len(groups)
        maps, offs = refs[2 : 2 + n], refs[2 + n : 2 + 2 * n]
        out_ref, x_ref, near_ref, map_ref, off_ref = refs[2 + 2 * n :]
    else:
        map_ref, off_ref, out_ref, x_ref, near_ref = refs[2:]
    me = lax.axis_index("by")
    if direct(count):
        for group, mask_list in enumerate(groups):
            for n, mask in enumerate(mask_list):
                map_ref[me ^ mask] = maps[group][n]
                off_ref[me ^ mask] = offs[group][n]
    map_places, _ = map_layout(own)
    off_places, _ = off_layout(own)

    def tiles(s):
        return 1 if s == SWEEPS - 1 else 2

    def get(s, comp):
        return [x_ref[s, comp, t] for t in range(tiles(s))]

    x_ref[...] = jnp.zeros(x_ref.shape, F32)

    def shifted(x, reach, n):
        deep = max(abs(o[0]) for o in reach)
        by_row = {0: x}
        for step in range(1, deep + 1):
            count_out = 2 if step < deep else n
            by_row[step] = shift_i(by_row[step - 1], 1, count_out)
            by_row[-step] = shift_i(by_row[1 - step], -1, count_out)
        out = {}
        for i, k in reach:
            out[i, k] = [roll_k(tile, k) if k else tile for tile in by_row[i][:n]]
        return out

    def through(hop, carry):
        block = count - 1 - hop
        coef = {key: load_tiles(map_ref, block, place) for key, place in map_places.items()}
        fresh = {}
        for comp in range(3):
            total = [load_tiles(off_ref, block, off_places[s, comp]) for s in range(SWEEPS)]
            for s in range(SWEEPS):
                x = get(s, comp)
                for d in range(SWEEPS - s):
                    n = tiles(s + d)
                    moved = shifted(x, REACH[d], n)
                    for o in REACH[d]:
                        for t in range(n):
                            total[s + d][t] = total[s + d][t] + coef[d, o][t] * moved[o][t]
            for s in range(SWEEPS):
                fresh[s, comp] = total[s]
        for (s, comp), value in fresh.items():
            for t, tile in enumerate(value):
                x_ref[s, comp, t] = tile
        return carry

    lax.fori_loop(0, count - 1 - me, through, 0)

    for comp in range(3):
        at = 0
        for d in range(SWEEPS):
            moved = shifted(get(SWEEPS - 1 - d, comp), REACH[d], 1)
            for o in REACH[d]:
                near_ref[at, comp] = moved[o][0]
                at += 1
    part = nj // 2 if nj % 2 == 0 else nj
    for begin in range(0, nj, part):
        span = range(begin, begin + part)
        total = [[last_ref[comp, j] for j in span] for comp in range(3)]
        for at in range(near_ref.shape[0]):
            moved = [near_ref[at, comp] for comp in range(3)]
            for n, j in enumerate(span):
                c = all_ref[at, j]
                for comp in range(3):
                    total[comp][n] = total[comp][n] + c * moved[comp]
        for comp in range(3):
            for n, j in enumerate(span):
                out_ref[comp, pl.ds(j, own, stride=nj), :] = total[comp][n]


def product_kernel(
    flow_ref, adj_ref, faces_ref, first_ref, second_ref, jfirst_ref, jsecond_ref, out_ref, *, nj,
):
    own, lanes = flow_ref.shape[1], flow_ref.shape[-1]
    even = lax.axis_index("bx") % 2 == 0
    jeven = lax.axis_index("by") % 2 == 0
    sub = lax.broadcasted_iota(jnp.int32, (nj, lanes), 0)
    for i in range(own):
        here = [adj_ref[comp, i] for comp in range(5)]

        def beside(comp, face):
            if face == 0:
                if i + 1 < own:
                    return adj_ref[comp, i + 1]
                return jnp.where(even, first_ref[comp], second_ref[comp])
            if face == 1:
                if i > 0:
                    return adj_ref[comp, i - 1]
                return jnp.where(even, second_ref[comp], first_ref[comp])
            if face in (2, 3):
                one = jfirst_ref[comp, i : i + 1, :]
                two = jsecond_ref[comp, i : i + 1, :]
                if face == 2:
                    line = jnp.where(jeven, one, two)
                    return jnp.where(sub == nj - 1, line, pltpu.roll(here[comp], nj - 1, 0))
                line = jnp.where(jeven, two, one)
                return jnp.where(sub == 0, line, pltpu.roll(here[comp], 1, 0))
            return edge_k(here[comp], 1 if face == 4 else -1)

        rho = flow_ref[0, i]
        m = [flow_ref[comp, i] for comp in (1, 2, 3)]
        energy = flow_ref[4, i]
        inv = 1.0 / rho
        u = [x * inv for x in m]
        uu = u[0] * u[0] + u[1] * u[1] + u[2] * u[2]
        pressure = GAS * (energy - 0.5 * (rho * uu))
        enthalpy = (energy + pressure) * inv
        sound = jnp.sqrt((1.0 + GAS) * pressure * inv)
        total = None
        for face in range(6):
            s = [faces_ref[face, axis, i] for axis in range(3)]
            h = [0.5 * (here[comp] - beside(comp, face)) for comp in range(5)]
            speed = u[0] * s[0] + u[1] * s[1] + u[2] * s[2]
            area = jnp.sqrt(s[0] * s[0] + s[1] * s[1] + s[2] * s[2])
            wave = jnp.abs(speed) + sound * area
            bulk = (u[0] * h[1] + u[1] * h[2] + u[2] * h[3]) + enthalpy * h[4]
            press = (s[0] * h[1] + s[1] * h[2] + s[2] * h[3]) + speed * h[4]
            full = h[0] + bulk
            term = [
                0.5 * GAS * (uu * press) - speed * bulk + wave * h[0],
                s[0] * full - GAS * (u[0] * press) + (speed + wave) * h[1],
                s[1] * full - GAS * (u[1] * press) + (speed + wave) * h[2],
                s[2] * full - GAS * (u[2] * press) + (speed + wave) * h[3],
                GAS * press + (speed + wave) * h[4],
            ]
            total = term if total is None else [a + b for a, b in zip(total, term)]
        for comp in range(5):
            out_ref[comp, i] = total[comp]


def call(kernel, out_shape, args, scratch=(), space=pltpu.VMEM, interpret=False):
    vmem = pl.BlockSpec(memory_space=pltpu.VMEM)
    single = not isinstance(out_shape, (list, tuple))
    held = [*args, *([out_shape] if single else out_shape), *scratch]
    need = sum(4 * math.prod(a.shape) for a in held)
    return pl.pallas_call(
        kernel,
        out_shape=out_shape,
        in_specs=[pl.BlockSpec(memory_space=space)] * len(args),
        out_specs=vmem if single else [vmem] * len(out_shape),
        scratch_shapes=list(scratch),
        interpret=interpret,
        compiler_params=pltpu.CompilerParams(vmem_limit_bytes=need + (2 << 20)),
    )(*args)


INTERPRET = False


def on_device(flow, adjoint, faces, decay, surface_mask):
    own, nj, lanes = decay.shape
    w = SWEEPS
    rows = own + 2 * w
    nby = lax.axis_size("by")

    def run(*args):
        return call(*args, interpret=INTERPRET)


    def shape(*dims):
        return jax.ShapeDtypeStruct(dims, F32)

    flat = [flow.reshape(5, own * nj, lanes), adjoint.reshape(5, own * nj, lanes)]
    flat += [decay.reshape(own * nj, lanes), surface_mask.reshape(own * nj, lanes)]
    flat = [pltpu.with_memory_space_constraint(x, pltpu.HBM) for x in flat]
    rim = shape(5 + w - 1, nj, lanes)
    flow, adjoint, retention, l1, l2, m1, m2 = run(
        functools.partial(pack_kernel, own=own, nj=nj),
        [shape(5, own * nj, lanes)] * 2
        + [shape(own * nj, lanes)]
        + [shape(5, own, lanes)] * 2
        + [rim] * 2,
        flat,
        [
            pltpu.VMEM((own * nj, lanes), F32),
            pltpu.VMEM((own * nj, lanes), jnp.int32),
            pltpu.SemaphoreType.DMA((4,)),
        ],
        pltpu.HBM,
    )
    flow, adjoint = flow.reshape(5, own, nj, lanes), adjoint.reshape(5, own, nj, lanes)
    l1, l2 = swap(l1, "by", 0), swap(l2, "by", 1)
    m1, m2 = swap(m1, "bx", 0), swap(m2, "bx", 1)

    halo = shape(3, w, nj, lanes)
    inner, h1, h2 = run(
        functools.partial(volume_kernel, nj=nj),
        [shape(3, own, nj, lanes), halo, halo],
        [flow, adjoint, m1, m2, l1, l2],
    )
    h1, h2 = swap(h1, "bx", 0), swap(h2, "bx", 1)

    _, n_map = map_layout(own)
    _, n_off = off_layout(own)
    rate, gain, maps, all_coef = run(
        functools.partial(maps_kernel, rows=rows, nj=nj),
        [
            shape(nj, 2, own, lanes),
            shape(nj, 2, own, lanes),
            shape(n_map, own, lanes),
            shape(sum(map(len, REACH)), nj, own, lanes),
        ],
        [retention, m1, m2],
        [
            pltpu.VMEM((rows * nj, lanes), F32),
            pltpu.VMEM((sum(map(len, REACH[:-1])), nj, own, lanes), F32),
        ],
    )
    all_maps = collect(maps, "by")

    offs, last = run(
        functools.partial(offsets_kernel, rows=rows, nj=nj),
        [shape(n_off, own, lanes), shape(3, nj, own, lanes)],
        [inner, h1, h2, rate, gain],
        [pltpu.VMEM((3, rows * nj, lanes), F32), pltpu.VMEM((SWEEPS, 3, nj, 2, own, lanes), F32)],
    )
    all_offs = collect(offs, "by")

    product = run(
        functools.partial(product_kernel, nj=nj),
        jax.ShapeDtypeStruct(flow.shape, F32),
        [flow, adjoint, faces, m1, m2, l1, l2],
    )

    scratch = [
        pltpu.VMEM((SWEEPS, 3, 2, own, lanes), F32),
        pltpu.VMEM((sum(map(len, REACH)), 3, own, lanes), F32),
    ]
    if direct(nby):
        scratch += [
            pltpu.VMEM((nby, n_map, own, lanes), F32),
            pltpu.VMEM((nby, n_off, own, lanes), F32),
        ]
    warp = run(
        functools.partial(finish_kernel, own=own, nj=nj, count=nby),
        shape(3, own * nj, lanes),
        [last, all_coef, *all_maps, *all_offs],
        scratch,
    )
    return (product, warp.reshape(3, own, nj, lanes))


def solution(mesh):
    return jax.shard_map(
        on_device,
        mesh=mesh,
        in_specs=(
            P(None, "bx", "by", None),
            P(None, "bx", "by", None),
            P(None, None, "bx", "by", None),
            P("bx", "by", None),
            P("bx", "by", None),
        ),
        out_specs=(P(None, "bx", "by", None), P(None, "bx", "by", None)),
        check_vma=False,
    )
```

```python
import functools
import math

import jax
import jax.numpy as jnp
from jax import lax
from jax.experimental import pallas as pl
from jax.experimental.pallas import tpu as pltpu
from jax.sharding import PartitionSpec as P

SWEEPS = 4
KAPPA = 0.15
GAS = 0.4

F32 = jnp.float32

REACH = [[(0, 0)]]
for _ in range(SWEEPS - 1):
    REACH.append(
        sorted({(i + a, k + b) for i, k in REACH[-1] for a, b in ((1, 0), (-1, 0), (0, 1), (0, -1))})
    )


def matching(axis, first):
    count = lax.axis_size(axis)
    pairs = [(i, i + 1) for i in range(first, count - 1, 2)]
    return pairs + [(b, a) for a, b in pairs]


def swap(x, axis, first):
    return lax.ppermute(x, axis, matching(axis, first))


def flip(x, axis, mask):
    count = lax.axis_size(axis)
    return lax.ppermute(x, axis, [(i, i ^ mask) for i in range(count)])


def direct(count):
    return count in (2, 4, 8)


def collect(x, axis):
    count = lax.axis_size(axis)
    if not direct(count):
        return [lax.all_gather(x, axis)]
    near = flip(x, axis, 1)[None]
    far = [flip(x, axis, m) for m in range(2, count, 2)]
    if not far:
        return [near]
    far = jnp.stack(far)
    return [near, far, flip(far, axis, 1)]


def sources(count):
    far = list(range(2, count, 2))
    return [[1], far, [m + 1 for m in far]] if far else [[1]]


def shift_i(x, step, n):
    size = x[0].shape[0]
    turned = [pltpu.roll(tile, (-step) % size, 0) for tile in x]
    row = lax.broadcasted_iota(jnp.int32, x[0].shape, 0)
    edge = row == (size - 1 if step > 0 else 0)
    return [jnp.where(edge, turned[1 - t], turned[t]) for t in range(n)]


def roll_k(tile, step):
    return pltpu.roll(tile, (-step) % tile.shape[1], 1)


def edge_k(tile, step):
    lane = lax.broadcasted_iota(jnp.int32, tile.shape, 1)
    edge = tile.shape[1] - 1 if step > 0 else 0
    return jnp.where(lane == edge, 0.0, roll_k(tile, step))


def move(x, step, n):
    return shift_i(x, step[0], n) if step[0] else [edge_k(tile, step[1]) for tile in x[:n]]


def couple(x, n):
    up, down = shift_i(x, 1, n), shift_i(x, -1, n)
    return [(up[t] + down[t]) + (edge_k(x[t], 1) + edge_k(x[t], -1)) for t in range(n)]


def at_j(ref, j, rows, nj, tiles):
    size = rows // tiles
    return [ref[pl.ds(j + t * size * nj, size, stride=nj), :] for t in range(tiles)]


def row_valid(rows, lanes):
    own = rows - 2 * SWEEPS
    place = lax.axis_index("bx")
    above = jnp.where(place < lax.axis_size("bx") - 1, SWEEPS - 1, 0)
    below = jnp.where(place > 0, SWEEPS - 1, 0)
    row = lax.broadcasted_iota(jnp.int32, (rows, lanes), 0)
    inside = (row < own + above) | (row >= rows - below)
    valid = jnp.where(inside, 1.0, 0.0).astype(F32)
    return [valid[t * own : (t + 1) * own] for t in range(rows // own)]


def pack_kernel(
    flow_hbm, adj_hbm, decay_hbm, mask_hbm,
    flow_ref, adj_ref, rate_ref, line1_ref, line2_ref, rim1_ref, rim2_ref,
    decay_ref, mask_ref, sems, *, own, nj,
):
    pairs = [(adj_hbm, adj_ref), (decay_hbm, decay_ref), (mask_hbm, mask_ref), (flow_hbm, flow_ref)]
    copies = [pltpu.make_async_copy(a, b, sems.at[n]) for n, (a, b) in enumerate(pairs)]
    for copy in copies:
        copy.start()
    even = lax.axis_index("bx") % 2 == 0
    jeven = lax.axis_index("by") % 2 == 0
    copies[0].wait()
    for comp in range(5):
        bottom = adj_ref[comp, pl.ds(0, own, stride=nj), :]
        top = adj_ref[comp, pl.ds(nj - 1, own, stride=nj), :]
        line1_ref[comp] = jnp.where(jeven, top, bottom)
        line2_ref[comp] = jnp.where(jeven, bottom, top)
        low = adj_ref[comp, 0:nj, :]
        high = adj_ref[comp, (own - 1) * nj : own * nj, :]
        rim1_ref[comp] = jnp.where(even, high, low)
        rim2_ref[comp] = jnp.where(even, low, high)
    copies[1].wait()
    copies[2].wait()
    rate_ref[...] = (1 - mask_ref[...]).astype(F32) * decay_ref[...]
    for row in range(SWEEPS - 1):
        low = rate_ref[row * nj : (row + 1) * nj, :]
        at = own - (SWEEPS - 1) + row
        high = rate_ref[at * nj : (at + 1) * nj, :]
        rim1_ref[5 + row] = jnp.where(even, high, low)
        rim2_ref[5 + row] = jnp.where(even, low, high)
    copies[3].wait()


def pack_rows(parts, width):
    total = parts[0]
    row = lax.broadcasted_iota(jnp.int32, total.shape, 0)
    size = total.shape[0]
    for n, part in enumerate(parts[1:], 1):
        moved = pltpu.roll(part, 2 * width * n, 0)
        place = (row - 2 * width * n + width + size) % size
        total = jnp.where(place < 2 * width, moved, total)
    return total


def unpack_rows(tile, n, width):
    return pltpu.roll(tile, (-2 * width * n) % tile.shape[0], 0) if n else tile


def layout(groups, own):
    places, at = {}, 0
    for keys, width in groups:
        for key in keys:
            places[key] = [at, None, 0, width]
            at += 1
        if width:
            share = max(1, own // (2 * width))
            for n, key in enumerate(keys):
                places[key][1] = at + n // share
                places[key][2] = n % share
            at += -(-len(keys) // share)
    return places, at


def map_layout(own):
    return layout([([(d, o) for o in REACH[d]], SWEEPS - 1 - d) for d in range(SWEEPS)], own)


def off_layout(own):
    return layout([([(s, c) for c in range(3)], SWEEPS - 1 - s) for s in range(SWEEPS)], own)


def store_tiles(ref, places, values):
    halos = {}
    for key, (main, halo, position, width) in places.items():
        ref[main] = values[key][0]
        if halo is not None:
            halos.setdefault((halo, width), []).append(values[key][1])
    for (halo, width), parts in halos.items():
        ref[halo] = pack_rows(parts, width)


def load_tiles(ref, block, place):
    main, halo, position, width = place
    tile = ref[block, main]
    if halo is None:
        return [tile]
    return [tile, unpack_rows(ref[block, halo], position, width)]


def maps_kernel(
    own_ref, first_ref, second_ref, rate_t, gain_t, map_ref, all_ref, ext_ref, side_ref, *, rows, nj,
):
    lanes = own_ref.shape[-1]
    own = rows - 2 * SWEEPS
    wide = SWEEPS - 1
    rate_ref = ext_ref
    rate_ref[0 : own * nj, :] = own_ref[...]
    even = lax.axis_index("bx") % 2 == 0
    first = first_ref[5 : 5 + wide].reshape(wide * nj, lanes)
    second = second_ref[5 : 5 + wide].reshape(wide * nj, lanes)
    rate_ref[own * nj : (own + wide) * nj, :] = jnp.where(even, first, second)
    rate_ref[(own + wide) * nj : (rows - wide) * nj, :] = jnp.zeros((2 * nj, lanes), F32)
    rate_ref[(rows - wide) * nj : rows * nj, :] = jnp.where(even, second, first)

    valid = row_valid(rows, lanes)
    for j in range(nj):
        rate = at_j(rate_ref, j, rows, nj, 2)
        for t in range(2):
            rate_t[j, t] = rate[t]
            gain_t[j, t] = KAPPA * (valid[t] - rate[t])
    places, _ = map_layout(own)
    final, at, begin = {}, 0, 0
    for d in range(SWEEPS):
        n = 1 if d == SWEEPS - 1 else 2
        index = {o: at + i for i, o in enumerate(REACH[d])}
        before = {o: begin + i for i, o in enumerate(REACH[d - 1])} if d else {}
        coef = {o: None for o in REACH[d]}
        for j in range(nj - 1, -1, -1):
            rate = [rate_t[j, t] for t in range(n)]
            if d == 0:
                old = coef[0, 0]
                coef[0, 0] = rate if old is None else [r * c for r, c in zip(rate, old)]
            else:
                total = {o: None for o in REACH[d]}
                for o, i in before.items():
                    c = [all_ref[i, j], side_ref[i, j]]
                    for step in ((1, 0), (-1, 0), (0, 1), (0, -1)):
                        moved = move(c, step, n)
                        goal = (o[0] + step[0], o[1] + step[1])
                        held = total[goal]
                        total[goal] = moved if held is None else [p + q for p, q in zip(held, moved)]
                gain = [gain_t[j, t] for t in range(n)]
                for o in REACH[d]:
                    fresh = [gain[t] * total[o][t] for t in range(n)]
                    old = coef[o]
                    if old is not None:
                        fresh = [rate[t] * old[t] + fresh[t] for t in range(n)]
                    coef[o] = fresh
            for o in REACH[d]:
                all_ref[index[o], j] = coef[o][0]
                if n == 2:
                    side_ref[index[o], j] = coef[o][1]
        final.update({(d, o): coef[o] for o in REACH[d]})
        begin, at = at, at + len(REACH[d])
    store_tiles(map_ref, places, final)


def sweeps(v_ref, rate_t, gain_t, warp_ref, rows, nj, last_ref):
    comps = v_ref.shape[0]
    ends_at = {}
    for s in range(SWEEPS):
        n = 1 if s == SWEEPS - 1 else 2
        state = [None] * comps
        for j in range(nj - 1, -1, -1):
            rate = [rate_t[j, t] for t in range(n)]
            gain = [gain_t[j, t] for t in range(n)]
            for c in range(comps):
                if s == 0:
                    before = at_j(v_ref.at[c], j, rows, nj, 2)
                    base = [gain[t] * (before[t] * (1.0 / KAPPA)) for t in range(n)]
                    for t in range(n):
                        warp_ref[SWEEPS - 1, c, j, t] = base[t]
                else:
                    before = [warp_ref[s - 1, c, j, t] for t in range(2)]
                    base = [warp_ref[SWEEPS - 1, c, j, t] for t in range(n)]
                near = couple(before, n)
                new = [base[t] + gain[t] * near[t] for t in range(n)]
                if state[c] is not None:
                    new = [new[t] + rate[t] * state[c][t] for t in range(n)]
                state[c] = new
                if s == SWEEPS - 1:
                    last_ref[c, j] = new[0]
                else:
                    for t in range(n):
                        warp_ref[s, c, j, t] = new[t]
        for c in range(comps):
            ends_at[s, c] = state[c]
    return ends_at


def volume_part(flow, jump):
    rho, m, energy = flow[0], flow[1:4], flow[4]
    inv = 1.0 / rho
    u = [x * inv for x in m]
    mu = m[0] * u[0] + m[1] * u[1] + m[2] * u[2]
    pressure = GAS * (energy - 0.5 * mu)
    q = (
        rho * jump[0]
        + (m[0] * jump[1] + m[1] * jump[2] + m[2] * jump[3])
        + (energy + pressure) * jump[4]
    )
    return [0.5 * (u[comp] * q + pressure * jump[comp + 1]) for comp in range(3)]


def volume_kernel(flow_ref, adj_ref, jfirst_ref, jsecond_ref, v_ref, out1_ref, out2_ref, *, nj):
    own, lanes = flow_ref.shape[1], flow_ref.shape[-1]
    w = SWEEPS
    even = lax.axis_index("bx") % 2 == 0
    jeven = lax.axis_index("by") % 2 == 0
    sub = lax.broadcasted_iota(jnp.int32, (nj, lanes), 0)
    for i in range(own):
        jump = []
        for comp in range(5):
            here = adj_ref[comp, i]
            if i == 0:
                diff = -adj_ref[comp, 1]
            elif i == own - 1:
                diff = adj_ref[comp, own - 2]
            else:
                diff = adj_ref[comp, i - 1] - adj_ref[comp, i + 1]
            one, two = jfirst_ref[comp, i : i + 1, :], jsecond_ref[comp, i : i + 1, :]
            back = jnp.where(sub == 0, jnp.where(jeven, two, one), pltpu.roll(here, 1, 0))
            ahead = jnp.where(
                sub == nj - 1, jnp.where(jeven, one, two), pltpu.roll(here, nj - 1, 0)
            )
            jump.append(diff + (back - ahead) + (edge_k(here, -1) - edge_k(here, 1)))
        part = volume_part([flow_ref[comp, i] for comp in range(5)], jump)
        for comp in range(3):
            v_ref[comp, i] = part[comp]
    for comp in range(3):
        low, high = v_ref[comp, 0:w], v_ref[comp, own - w : own]
        out1_ref[comp * w : (comp + 1) * w] = jnp.where(even, high, low)
        out2_ref[comp * w : (comp + 1) * w] = jnp.where(even, low, high)
    for comp in range(5):
        low, high = flow_ref[comp, 0], flow_ref[comp, own - 1]
        out1_ref[3 * w + comp] = jnp.where(even, high, low)
        out2_ref[3 * w + comp] = jnp.where(even, low, high)


def offsets_kernel(
    own_ref, first_ref, second_ref, flow_ref, adj_ref, rim1_ref, rim2_ref, rate_t, gain_t,
    off_ref, last_ref, v_ref, warp_ref, *, rows, nj,
):
    lanes = own_ref.shape[-1]
    own = rows - 2 * SWEEPS
    w = SWEEPS
    even = lax.axis_index("bx") % 2 == 0
    for comp in range(3):
        v_ref[comp, 0 : own * nj, :] = own_ref[comp].reshape(own * nj, lanes)
        one = first_ref[comp * w : (comp + 1) * w].reshape(w * nj, lanes)
        two = second_ref[comp * w : (comp + 1) * w].reshape(w * nj, lanes)
        v_ref[comp, own * nj : (own + w) * nj, :] = jnp.where(even, one, two)
        v_ref[comp, (own + w) * nj : rows * nj, :] = jnp.where(even, two, one)

    place, count = lax.axis_index("bx"), lax.axis_size("bx")
    reach = range(5)
    rim_up = [jnp.where(even, rim1_ref[c], rim2_ref[c]) for c in reach]
    rim_low = [jnp.where(even, rim2_ref[c], rim1_ref[c]) for c in reach]
    at = 3 * w
    flow_up = [jnp.where(even, first_ref[at + c], second_ref[at + c]) for c in reach]
    flow_low = [jnp.where(even, second_ref[at + c], first_ref[at + c]) for c in reach]

    def add(row, flow, adjoint, sign, inside):
        part = volume_part(flow, adjoint)
        for comp in range(3):
            lines = slice(row * nj, (row + 1) * nj)
            term = part[comp] if inside is None else jnp.where(inside, part[comp], 0.0)
            v_ref[comp, lines, :] = v_ref[comp, lines, :] + sign * term

    add(0, [flow_ref[c, 0] for c in reach], rim_low, 1.0, None)
    add(own - 1, [flow_ref[c, own - 1] for c in reach], rim_up, -1.0, None)
    add(own, flow_up, [adj_ref[c, own - 1] for c in reach], 1.0, place < count - 1)
    add(rows - 1, flow_low, [adj_ref[c, 0] for c in reach], -1.0, place > 0)

    ends_at = sweeps(v_ref, rate_t, gain_t, warp_ref, rows, nj, last_ref)
    places, _ = off_layout(own)
    store_tiles(off_ref, places, ends_at)


def finish_kernel(*refs, own, nj, count):
    last_ref, all_ref = refs[:2]
    if direct(count):
        groups = sources(count)
        n = len(groups)
        maps, offs = refs[2 : 2 + n], refs[2 + n : 2 + 2 * n]
        out_ref, x_ref, near_ref, map_ref, off_ref = refs[2 + 2 * n :]
    else:
        map_ref, off_ref, out_ref, x_ref, near_ref = refs[2:]
    me = lax.axis_index("by")
    if direct(count):
        for group, mask_list in enumerate(groups):
            for n, mask in enumerate(mask_list):
                map_ref[me ^ mask] = maps[group][n]
                off_ref[me ^ mask] = offs[group][n]
    map_places, _ = map_layout(own)
    off_places, _ = off_layout(own)

    def tiles(s):
        return 1 if s == SWEEPS - 1 else 2

    def get(s, comp):
        return [x_ref[s, comp, t] for t in range(tiles(s))]

    x_ref[...] = jnp.zeros(x_ref.shape, F32)

    def shifted(x, reach, n):
        deep = max(abs(o[0]) for o in reach)
        by_row = {0: x}
        for step in range(1, deep + 1):
            count_out = 2 if step < deep else n
            by_row[step] = shift_i(by_row[step - 1], 1, count_out)
            by_row[-step] = shift_i(by_row[1 - step], -1, count_out)
        out = {}
        for i, k in reach:
            out[i, k] = [roll_k(tile, k) if k else tile for tile in by_row[i][:n]]
        return out

    def through(hop, carry):
        block = count - 1 - hop
        coef = {key: load_tiles(map_ref, block, place) for key, place in map_places.items()}
        fresh = {}
        for comp in range(3):
            total = [load_tiles(off_ref, block, off_places[s, comp]) for s in range(SWEEPS)]
            for s in range(SWEEPS):
                x = get(s, comp)
                for d in range(SWEEPS - s):
                    n = tiles(s + d)
                    moved = shifted(x, REACH[d], n)
                    for o in REACH[d]:
                        for t in range(n):
                            total[s + d][t] = total[s + d][t] + coef[d, o][t] * moved[o][t]
            for s in range(SWEEPS):
                fresh[s, comp] = total[s]
        for (s, comp), value in fresh.items():
            for t, tile in enumerate(value):
                x_ref[s, comp, t] = tile
        return carry

    lax.fori_loop(0, count - 1 - me, through, 0)

    for comp in range(3):
        at = 0
        for d in range(SWEEPS):
            moved = shifted(get(SWEEPS - 1 - d, comp), REACH[d], 1)
            for o in REACH[d]:
                near_ref[at, comp] = moved[o][0]
                at += 1
    part = nj // 2 if nj % 2 == 0 else nj
    for begin in range(0, nj, part):
        span = range(begin, begin + part)
        total = [[last_ref[comp, j] for j in span] for comp in range(3)]
        for at in range(near_ref.shape[0]):
            moved = [near_ref[at, comp] for comp in range(3)]
            for n, j in enumerate(span):
                c = all_ref[at, j]
                for comp in range(3):
                    total[comp][n] = total[comp][n] + c * moved[comp]
        for comp in range(3):
            for n, j in enumerate(span):
                out_ref[comp, pl.ds(j, own, stride=nj), :] = total[comp][n]


def product_kernel(
    flow_ref, adj_ref, faces_ref, first_ref, second_ref, jfirst_ref, jsecond_ref, out_ref, *, nj,
):
    own, lanes = flow_ref.shape[1], flow_ref.shape[-1]
    even = lax.axis_index("bx") % 2 == 0
    jeven = lax.axis_index("by") % 2 == 0
    sub = lax.broadcasted_iota(jnp.int32, (nj, lanes), 0)
    for i in range(own):
        here = [adj_ref[comp, i] for comp in range(5)]

        def beside(comp, face):
            if face == 0:
                if i + 1 < own:
                    return adj_ref[comp, i + 1]
                return jnp.where(even, first_ref[comp], second_ref[comp])
            if face == 1:
                if i > 0:
                    return adj_ref[comp, i - 1]
                return jnp.where(even, second_ref[comp], first_ref[comp])
            if face in (2, 3):
                one = jfirst_ref[comp, i : i + 1, :]
                two = jsecond_ref[comp, i : i + 1, :]
                if face == 2:
                    line = jnp.where(jeven, one, two)
                    return jnp.where(sub == nj - 1, line, pltpu.roll(here[comp], nj - 1, 0))
                line = jnp.where(jeven, two, one)
                return jnp.where(sub == 0, line, pltpu.roll(here[comp], 1, 0))
            return edge_k(here[comp], 1 if face == 4 else -1)

        rho = flow_ref[0, i]
        m = [flow_ref[comp, i] for comp in (1, 2, 3)]
        energy = flow_ref[4, i]
        inv = 1.0 / rho
        u = [x * inv for x in m]
        uu = u[0] * u[0] + u[1] * u[1] + u[2] * u[2]
        pressure = GAS * (energy - 0.5 * (rho * uu))
        enthalpy = (energy + pressure) * inv
        sound = jnp.sqrt((1.0 + GAS) * pressure * inv)
        total = None
        for face in range(6):
            s = [faces_ref[face, axis, i] for axis in range(3)]
            h = [0.5 * (here[comp] - beside(comp, face)) for comp in range(5)]
            speed = u[0] * s[0] + u[1] * s[1] + u[2] * s[2]
            area = jnp.sqrt(s[0] * s[0] + s[1] * s[1] + s[2] * s[2])
            wave = jnp.abs(speed) + sound * area
            bulk = (u[0] * h[1] + u[1] * h[2] + u[2] * h[3]) + enthalpy * h[4]
            press = (s[0] * h[1] + s[1] * h[2] + s[2] * h[3]) + speed * h[4]
            full = h[0] + bulk
            term = [
                0.5 * GAS * (uu * press) - speed * bulk + wave * h[0],
                s[0] * full - GAS * (u[0] * press) + (speed + wave) * h[1],
                s[1] * full - GAS * (u[1] * press) + (speed + wave) * h[2],
                s[2] * full - GAS * (u[2] * press) + (speed + wave) * h[3],
                GAS * press + (speed + wave) * h[4],
            ]
            total = term if total is None else [a + b for a, b in zip(total, term)]
        for comp in range(5):
            out_ref[comp, i] = total[comp]


def call(kernel, out_shape, args, scratch=(), space=pltpu.VMEM, interpret=False):
    vmem = pl.BlockSpec(memory_space=pltpu.VMEM)
    single = not isinstance(out_shape, (list, tuple))
    held = [*args, *([out_shape] if single else out_shape), *scratch]
    need = sum(4 * math.prod(a.shape) for a in held)
    return pl.pallas_call(
        kernel,
        out_shape=out_shape,
        in_specs=[pl.BlockSpec(memory_space=space)] * len(args),
        out_specs=vmem if single else [vmem] * len(out_shape),
        scratch_shapes=list(scratch),
        interpret=interpret,
        compiler_params=pltpu.CompilerParams(vmem_limit_bytes=need + (2 << 20)),
    )(*args)


INTERPRET = False


def on_device(flow, adjoint, faces, decay, surface_mask):
    own, nj, lanes = decay.shape
    w = SWEEPS
    rows = own + 2 * w
    nby = lax.axis_size("by")

    def run(*args):
        return call(*args, interpret=INTERPRET)


    def shape(*dims):
        return jax.ShapeDtypeStruct(dims, F32)

    flat = [flow.reshape(5, own * nj, lanes), adjoint.reshape(5, own * nj, lanes)]
    flat += [decay.reshape(own * nj, lanes), surface_mask.reshape(own * nj, lanes)]
    flat = [pltpu.with_memory_space_constraint(x, pltpu.HBM) for x in flat]
    rim = shape(5 + w - 1, nj, lanes)
    flow, adjoint, retention, l1, l2, m1, m2 = run(
        functools.partial(pack_kernel, own=own, nj=nj),
        [shape(5, own * nj, lanes)] * 2
        + [shape(own * nj, lanes)]
        + [shape(5, own, lanes)] * 2
        + [rim] * 2,
        flat,
        [
            pltpu.VMEM((own * nj, lanes), F32),
            pltpu.VMEM((own * nj, lanes), jnp.int32),
            pltpu.SemaphoreType.DMA((4,)),
        ],
        pltpu.HBM,
    )
    flow, adjoint = flow.reshape(5, own, nj, lanes), adjoint.reshape(5, own, nj, lanes)
    l1, l2 = swap(l1, "by", 0), swap(l2, "by", 1)
    m1, m2 = swap(m1, "bx", 0), swap(m2, "bx", 1)

    halo = shape(3 * w + 5, nj, lanes)
    inner, h1, h2 = run(
        functools.partial(volume_kernel, nj=nj),
        [shape(3, own, nj, lanes), halo, halo],
        [flow, adjoint, l1, l2],
    )
    h1, h2 = swap(h1, "bx", 0), swap(h2, "bx", 1)

    _, n_map = map_layout(own)
    _, n_off = off_layout(own)
    rate, gain, maps, all_coef = run(
        functools.partial(maps_kernel, rows=rows, nj=nj),
        [
            shape(nj, 2, own, lanes),
            shape(nj, 2, own, lanes),
            shape(n_map, own, lanes),
            shape(sum(map(len, REACH)), nj, own, lanes),
        ],
        [retention, m1, m2],
        [
            pltpu.VMEM((rows * nj, lanes), F32),
            pltpu.VMEM((sum(map(len, REACH[:-1])), nj, own, lanes), F32),
        ],
    )
    all_maps = collect(maps, "by")

    offs, last = run(
        functools.partial(offsets_kernel, rows=rows, nj=nj),
        [shape(n_off, own, lanes), shape(3, nj, own, lanes)],
        [inner, h1, h2, flow, adjoint, m1, m2, rate, gain],
        [pltpu.VMEM((3, rows * nj, lanes), F32), pltpu.VMEM((SWEEPS, 3, nj, 2, own, lanes), F32)],
    )
    all_offs = collect(offs, "by")

    product = run(
        functools.partial(product_kernel, nj=nj),
        jax.ShapeDtypeStruct(flow.shape, F32),
        [flow, adjoint, faces, m1, m2, l1, l2],
    )

    scratch = [
        pltpu.VMEM((SWEEPS, 3, 2, own, lanes), F32),
        pltpu.VMEM((sum(map(len, REACH)), 3, own, lanes), F32),
    ]
    if direct(nby):
        scratch += [
            pltpu.VMEM((nby, n_map, own, lanes), F32),
            pltpu.VMEM((nby, n_off, own, lanes), F32),
        ]
    warp = run(
        functools.partial(finish_kernel, own=own, nj=nj, count=nby),
        shape(3, own * nj, lanes),
        [last, all_coef, *all_maps, *all_offs],
        scratch,
    )
    return (product, warp.reshape(3, own, nj, lanes))


def solution(mesh):
    return jax.shard_map(
        on_device,
        mesh=mesh,
        in_specs=(
            P(None, "bx", "by", None),
            P(None, "bx", "by", None),
            P(None, None, "bx", "by", None),
            P("bx", "by", None),
            P("bx", "by", None),
        ),
        out_specs=(P(None, "bx", "by", None), P(None, "bx", "by", None)),
        check_vma=False,
    )
```

```python
import functools
import math

import jax
import jax.numpy as jnp
from jax import lax
from jax.experimental import pallas as pl
from jax.experimental.pallas import tpu as pltpu
from jax.sharding import PartitionSpec as P

SWEEPS = 4
KAPPA = 0.15
GAS = 0.4

F32 = jnp.float32

REACH = [[(0, 0)]]
for _ in range(SWEEPS - 1):
    REACH.append(
        sorted({(i + a, k + b) for i, k in REACH[-1] for a, b in ((1, 0), (-1, 0), (0, 1), (0, -1))})
    )


def matching(axis, first, closed):
    count = lax.axis_size(axis)
    pairs = [(i, i + 1) for i in range(first, count - 1, 2)]
    if closed and first and count % 2 == 0 and count > 2:
        pairs.append((0, count - 1))
    return pairs + [(b, a) for a, b in pairs]


def swap(x, axis, first, closed=False):
    return lax.ppermute(x, axis, matching(axis, first, closed))


def flip(x, axis, mask):
    count = lax.axis_size(axis)
    return lax.ppermute(x, axis, [(i, i ^ mask) for i in range(count)])


def direct(count):
    return count in (2, 4, 8)


def collect(x, axis):
    count = lax.axis_size(axis)
    if not direct(count):
        return [lax.all_gather(x, axis)]
    near = flip(x, axis, 1)[None]
    far = [flip(x, axis, m) for m in range(2, count, 2)]
    if not far:
        return [near]
    far = jnp.stack(far)
    return [near, far, flip(far, axis, 1)]


def sources(count):
    far = list(range(2, count, 2))
    return [[1], far, [m + 1 for m in far]] if far else [[1]]


def shift_i(x, step, n):
    size = x[0].shape[0]
    turned = [pltpu.roll(tile, (-step) % size, 0) for tile in x]
    row = lax.broadcasted_iota(jnp.int32, x[0].shape, 0)
    edge = row == (size - 1 if step > 0 else 0)
    return [jnp.where(edge, turned[1 - t], turned[t]) for t in range(n)]


def roll_k(tile, step):
    return pltpu.roll(tile, (-step) % tile.shape[1], 1)


def edge_k(tile, step):
    lane = lax.broadcasted_iota(jnp.int32, tile.shape, 1)
    edge = tile.shape[1] - 1 if step > 0 else 0
    return jnp.where(lane == edge, 0.0, roll_k(tile, step))


def move(x, step, n):
    return shift_i(x, step[0], n) if step[0] else [edge_k(tile, step[1]) for tile in x[:n]]


def couple(x, n):
    up, down = shift_i(x, 1, n), shift_i(x, -1, n)
    return [(up[t] + down[t]) + (edge_k(x[t], 1) + edge_k(x[t], -1)) for t in range(n)]


def at_j(ref, j, rows, nj, tiles):
    size = rows // tiles
    return [ref[pl.ds(j + t * size * nj, size, stride=nj), :] for t in range(tiles)]


def row_valid(rows, lanes):
    own = rows - 2 * SWEEPS
    place = lax.axis_index("bx")
    above = jnp.where(place < lax.axis_size("bx") - 1, SWEEPS - 1, 0)
    below = jnp.where(place > 0, SWEEPS - 1, 0)
    row = lax.broadcasted_iota(jnp.int32, (rows, lanes), 0)
    inside = (row < own + above) | (row >= rows - below)
    valid = jnp.where(inside, 1.0, 0.0).astype(F32)
    return [valid[t * own : (t + 1) * own] for t in range(rows // own)]


def pack_kernel(
    flow_hbm, adj_hbm, decay_hbm, mask_hbm,
    flow_ref, adj_ref, rate_ref, line1_ref, line2_ref, rim1_ref, rim2_ref,
    decay_ref, mask_ref, sems, *, own, nj,
):
    pairs = [(adj_hbm, adj_ref), (decay_hbm, decay_ref), (mask_hbm, mask_ref), (flow_hbm, flow_ref)]
    copies = [pltpu.make_async_copy(a, b, sems.at[n]) for n, (a, b) in enumerate(pairs)]
    for copy in copies:
        copy.start()
    even = lax.axis_index("bx") % 2 == 0
    jeven = lax.axis_index("by") % 2 == 0
    place = lax.axis_index("by")
    inner = (place > 0) & (place < lax.axis_size("by") - 1)
    copies[0].wait()
    for comp in range(5):
        bottom = adj_ref[comp, pl.ds(0, own, stride=nj), :]
        top = adj_ref[comp, pl.ds(nj - 1, own, stride=nj), :]
        line1_ref[comp] = jnp.where(jeven, top, bottom)
        line2_ref[comp] = jnp.where(inner, jnp.where(jeven, bottom, top), 0.0)
        low = adj_ref[comp, 0:nj, :]
        high = adj_ref[comp, (own - 1) * nj : own * nj, :]
        rim1_ref[comp] = jnp.where(even, high, low)
        rim2_ref[comp] = jnp.where(even, low, high)
    copies[1].wait()
    copies[2].wait()
    rate_ref[...] = (1 - mask_ref[...]).astype(F32) * decay_ref[...]
    for row in range(SWEEPS - 1):
        low = rate_ref[row * nj : (row + 1) * nj, :]
        at = own - (SWEEPS - 1) + row
        high = rate_ref[at * nj : (at + 1) * nj, :]
        rim1_ref[5 + row] = jnp.where(even, high, low)
        rim2_ref[5 + row] = jnp.where(even, low, high)
    copies[3].wait()


def pack_rows(parts, width):
    total = parts[0]
    row = lax.broadcasted_iota(jnp.int32, total.shape, 0)
    size = total.shape[0]
    for n, part in enumerate(parts[1:], 1):
        moved = pltpu.roll(part, 2 * width * n, 0)
        place = (row - 2 * width * n + width + size) % size
        total = jnp.where(place < 2 * width, moved, total)
    return total


def unpack_rows(tile, n, width):
    return pltpu.roll(tile, (-2 * width * n) % tile.shape[0], 0) if n else tile


def layout(groups, own):
    places, at = {}, 0
    for keys, width in groups:
        for key in keys:
            places[key] = [at, None, 0, width]
            at += 1
        if width:
            share = max(1, own // (2 * width))
            for n, key in enumerate(keys):
                places[key][1] = at + n // share
                places[key][2] = n % share
            at += -(-len(keys) // share)
    return places, at


def map_layout(own):
    return layout([([(d, o) for o in REACH[d]], SWEEPS - 1 - d) for d in range(SWEEPS)], own)


def off_layout(own):
    return layout([([(s, c) for c in range(3)], SWEEPS - 1 - s) for s in range(SWEEPS)], own)


def store_tiles(ref, places, values):
    halos = {}
    for key, (main, halo, position, width) in places.items():
        ref[main] = values[key][0]
        if halo is not None:
            halos.setdefault((halo, width), []).append(values[key][1])
    for (halo, width), parts in halos.items():
        ref[halo] = pack_rows(parts, width)


def load_tiles(ref, block, place):
    main, halo, position, width = place
    tile = ref[block, main]
    if halo is None:
        return [tile]
    return [tile, unpack_rows(ref[block, halo], position, width)]


def maps_kernel(
    own_ref, first_ref, second_ref, rate_t, gain_t, map_ref, all_ref, ext_ref, side_ref, *, rows, nj,
):
    lanes = own_ref.shape[-1]
    own = rows - 2 * SWEEPS
    wide = SWEEPS - 1
    rate_ref = ext_ref
    rate_ref[0 : own * nj, :] = own_ref[...]
    even = lax.axis_index("bx") % 2 == 0
    first = first_ref[5 : 5 + wide].reshape(wide * nj, lanes)
    second = second_ref[5 : 5 + wide].reshape(wide * nj, lanes)
    rate_ref[own * nj : (own + wide) * nj, :] = jnp.where(even, first, second)
    rate_ref[(own + wide) * nj : (rows - wide) * nj, :] = jnp.zeros((2 * nj, lanes), F32)
    rate_ref[(rows - wide) * nj : rows * nj, :] = jnp.where(even, second, first)

    valid = row_valid(rows, lanes)
    for j in range(nj):
        rate = at_j(rate_ref, j, rows, nj, 2)
        for t in range(2):
            rate_t[j, t] = rate[t]
            gain_t[j, t] = KAPPA * (valid[t] - rate[t])
    places, _ = map_layout(own)
    final, at, begin = {}, 0, 0
    for d in range(SWEEPS):
        n = 1 if d == SWEEPS - 1 else 2
        index = {o: at + i for i, o in enumerate(REACH[d])}
        before = {o: begin + i for i, o in enumerate(REACH[d - 1])} if d else {}
        coef = {o: None for o in REACH[d]}
        for j in range(nj - 1, -1, -1):
            rate = [rate_t[j, t] for t in range(n)]
            if d == 0:
                old = coef[0, 0]
                coef[0, 0] = rate if old is None else [r * c for r, c in zip(rate, old)]
            else:
                total = {o: None for o in REACH[d]}
                for o, i in before.items():
                    c = [all_ref[i, j], side_ref[i, j]]
                    for step in ((1, 0), (-1, 0), (0, 1), (0, -1)):
                        moved = move(c, step, n)
                        goal = (o[0] + step[0], o[1] + step[1])
                        held = total[goal]
                        total[goal] = moved if held is None else [p + q for p, q in zip(held, moved)]
                gain = [gain_t[j, t] for t in range(n)]
                for o in REACH[d]:
                    fresh = [gain[t] * total[o][t] for t in range(n)]
                    old = coef[o]
                    if old is not None:
                        fresh = [rate[t] * old[t] + fresh[t] for t in range(n)]
                    coef[o] = fresh
            for o in REACH[d]:
                all_ref[index[o], j] = coef[o][0]
                if n == 2:
                    side_ref[index[o], j] = coef[o][1]
        final.update({(d, o): coef[o] for o in REACH[d]})
        begin, at = at, at + len(REACH[d])
    store_tiles(map_ref, places, final)


def sweeps(v_ref, rate_t, gain_t, warp_ref, rows, nj, last_ref):
    comps = v_ref.shape[0]
    ends_at = {}
    for s in range(SWEEPS):
        n = 1 if s == SWEEPS - 1 else 2
        state = [None] * comps
        for j in range(nj - 1, -1, -1):
            rate = [rate_t[j, t] for t in range(n)]
            gain = [gain_t[j, t] for t in range(n)]
            for c in range(comps):
                if s == 0:
                    before = at_j(v_ref.at[c], j, rows, nj, 2)
                    base = [gain[t] * (before[t] * (1.0 / KAPPA)) for t in range(n)]
                    for t in range(n):
                        warp_ref[SWEEPS - 1, c, j, t] = base[t]
                else:
                    before = [warp_ref[s - 1, c, j, t] for t in range(2)]
                    base = [warp_ref[SWEEPS - 1, c, j, t] for t in range(n)]
                near = couple(before, n)
                new = [base[t] + gain[t] * near[t] for t in range(n)]
                if state[c] is not None:
                    new = [new[t] + rate[t] * state[c][t] for t in range(n)]
                state[c] = new
                if s == SWEEPS - 1:
                    last_ref[c, j] = new[0]
                else:
                    for t in range(n):
                        warp_ref[s, c, j, t] = new[t]
        for c in range(comps):
            ends_at[s, c] = state[c]
    return ends_at


def volume_part(flow, jump):
    rho, m, energy = flow[0], flow[1:4], flow[4]
    inv = 1.0 / rho
    u = [x * inv for x in m]
    mu = m[0] * u[0] + m[1] * u[1] + m[2] * u[2]
    pressure = GAS * (energy - 0.5 * mu)
    q = (
        rho * jump[0]
        + (m[0] * jump[1] + m[1] * jump[2] + m[2] * jump[3])
        + (energy + pressure) * jump[4]
    )
    return [0.5 * (u[comp] * q + pressure * jump[comp + 1]) for comp in range(3)]


def volume_kernel(flow_ref, adj_ref, jfirst_ref, jsecond_ref, v_ref, out1_ref, out2_ref, *, nj):
    own, lanes = flow_ref.shape[1], flow_ref.shape[-1]
    w = SWEEPS
    even = lax.axis_index("bx") % 2 == 0
    jeven = lax.axis_index("by") % 2 == 0
    sub = lax.broadcasted_iota(jnp.int32, (nj, lanes), 0)
    for i in range(own):
        jump = []
        for comp in range(5):
            here = adj_ref[comp, i]
            if i == 0:
                diff = -adj_ref[comp, 1]
            elif i == own - 1:
                diff = adj_ref[comp, own - 2]
            else:
                diff = adj_ref[comp, i - 1] - adj_ref[comp, i + 1]
            one, two = jfirst_ref[comp, i : i + 1, :], jsecond_ref[comp, i : i + 1, :]
            back = jnp.where(sub == 0, jnp.where(jeven, two, one), pltpu.roll(here, 1, 0))
            ahead = jnp.where(
                sub == nj - 1, jnp.where(jeven, one, two), pltpu.roll(here, nj - 1, 0)
            )
            jump.append(diff + (back - ahead) + (edge_k(here, -1) - edge_k(here, 1)))
        part = volume_part([flow_ref[comp, i] for comp in range(5)], jump)
        for comp in range(3):
            v_ref[comp, i] = part[comp]
    for comp in range(3):
        low, high = v_ref[comp, 0:w], v_ref[comp, own - w : own]
        out1_ref[comp * w : (comp + 1) * w] = jnp.where(even, high, low)
        out2_ref[comp * w : (comp + 1) * w] = jnp.where(even, low, high)
    for comp in range(5):
        low, high = flow_ref[comp, 0], flow_ref[comp, own - 1]
        out1_ref[3 * w + comp] = jnp.where(even, high, low)
        out2_ref[3 * w + comp] = jnp.where(even, low, high)


def offsets_kernel(
    own_ref, first_ref, second_ref, flow_ref, adj_ref, rim1_ref, rim2_ref, rate_t, gain_t,
    off_ref, last_ref, v_ref, warp_ref, *, rows, nj,
):
    lanes = own_ref.shape[-1]
    own = rows - 2 * SWEEPS
    w = SWEEPS
    even = lax.axis_index("bx") % 2 == 0
    for comp in range(3):
        v_ref[comp, 0 : own * nj, :] = own_ref[comp].reshape(own * nj, lanes)
        one = first_ref[comp * w : (comp + 1) * w].reshape(w * nj, lanes)
        two = second_ref[comp * w : (comp + 1) * w].reshape(w * nj, lanes)
        v_ref[comp, own * nj : (own + w) * nj, :] = jnp.where(even, one, two)
        v_ref[comp, (own + w) * nj : rows * nj, :] = jnp.where(even, two, one)

    place, count = lax.axis_index("bx"), lax.axis_size("bx")
    reach = range(5)
    rim_up = [jnp.where(even, rim1_ref[c], rim2_ref[c]) for c in reach]
    rim_low = [jnp.where(even, rim2_ref[c], rim1_ref[c]) for c in reach]
    at = 3 * w
    flow_up = [jnp.where(even, first_ref[at + c], second_ref[at + c]) for c in reach]
    flow_low = [jnp.where(even, second_ref[at + c], first_ref[at + c]) for c in reach]

    def add(row, flow, adjoint, sign, inside):
        part = volume_part(flow, adjoint)
        for comp in range(3):
            lines = slice(row * nj, (row + 1) * nj)
            term = part[comp] if inside is None else jnp.where(inside, part[comp], 0.0)
            v_ref[comp, lines, :] = v_ref[comp, lines, :] + sign * term

    add(0, [flow_ref[c, 0] for c in reach], rim_low, 1.0, None)
    add(own - 1, [flow_ref[c, own - 1] for c in reach], rim_up, -1.0, None)
    add(own, flow_up, [adj_ref[c, own - 1] for c in reach], 1.0, place < count - 1)
    add(rows - 1, flow_low, [adj_ref[c, 0] for c in reach], -1.0, place > 0)

    ends_at = sweeps(v_ref, rate_t, gain_t, warp_ref, rows, nj, last_ref)
    places, _ = off_layout(own)
    store_tiles(off_ref, places, ends_at)


def finish_kernel(*refs, own, nj, count):
    last_ref, all_ref = refs[:2]
    if direct(count):
        groups = sources(count)
        n = len(groups)
        maps, offs = refs[2 : 2 + n], refs[2 + n : 2 + 2 * n]
        out_ref, x_ref, near_ref, map_ref, off_ref = refs[2 + 2 * n :]
    else:
        map_ref, off_ref, out_ref, x_ref, near_ref = refs[2:]
    me = lax.axis_index("by")
    if direct(count):
        for group, mask_list in enumerate(groups):
            for n, mask in enumerate(mask_list):
                map_ref[me ^ mask] = maps[group][n]
                off_ref[me ^ mask] = offs[group][n]
    map_places, _ = map_layout(own)
    off_places, _ = off_layout(own)

    def tiles(s):
        return 1 if s == SWEEPS - 1 else 2

    def get(s, comp):
        return [x_ref[s, comp, t] for t in range(tiles(s))]

    x_ref[...] = jnp.zeros(x_ref.shape, F32)

    def shifted(x, reach, n):
        deep = max(abs(o[0]) for o in reach)
        by_row = {0: x}
        for step in range(1, deep + 1):
            count_out = 2 if step < deep else n
            by_row[step] = shift_i(by_row[step - 1], 1, count_out)
            by_row[-step] = shift_i(by_row[1 - step], -1, count_out)
        out = {}
        for i, k in reach:
            out[i, k] = [roll_k(tile, k) if k else tile for tile in by_row[i][:n]]
        return out

    def through(hop, carry):
        block = count - 1 - hop
        coef = {key: load_tiles(map_ref, block, place) for key, place in map_places.items()}
        fresh = {}
        for comp in range(3):
            total = [load_tiles(off_ref, block, off_places[s, comp]) for s in range(SWEEPS)]
            for s in range(SWEEPS):
                x = get(s, comp)
                for d in range(SWEEPS - s):
                    n = tiles(s + d)
                    moved = shifted(x, REACH[d], n)
                    for o in REACH[d]:
                        for t in range(n):
                            total[s + d][t] = total[s + d][t] + coef[d, o][t] * moved[o][t]
            for s in range(SWEEPS):
                fresh[s, comp] = total[s]
        for (s, comp), value in fresh.items():
            for t, tile in enumerate(value):
                x_ref[s, comp, t] = tile
        return carry

    lax.fori_loop(0, count - 1 - me, through, 0)

    for comp in range(3):
        at = 0
        for d in range(SWEEPS):
            moved = shifted(get(SWEEPS - 1 - d, comp), REACH[d], 1)
            for o in REACH[d]:
                near_ref[at, comp] = moved[o][0]
                at += 1
    part = nj // 2 if nj % 2 == 0 else nj
    for begin in range(0, nj, part):
        span = range(begin, begin + part)
        total = [[last_ref[comp, j] for j in span] for comp in range(3)]
        for at in range(near_ref.shape[0]):
            moved = [near_ref[at, comp] for comp in range(3)]
            for n, j in enumerate(span):
                c = all_ref[at, j]
                for comp in range(3):
                    total[comp][n] = total[comp][n] + c * moved[comp]
        for comp in range(3):
            for n, j in enumerate(span):
                out_ref[comp, pl.ds(j, own, stride=nj), :] = total[comp][n]


def product_kernel(
    flow_ref, adj_ref, faces_ref, first_ref, second_ref, jfirst_ref, jsecond_ref, out_ref, *, nj,
):
    own, lanes = flow_ref.shape[1], flow_ref.shape[-1]
    even = lax.axis_index("bx") % 2 == 0
    jeven = lax.axis_index("by") % 2 == 0
    sub = lax.broadcasted_iota(jnp.int32, (nj, lanes), 0)
    for i in range(own):
        here = [adj_ref[comp, i] for comp in range(5)]

        def beside(comp, face):
            if face == 0:
                if i + 1 < own:
                    return adj_ref[comp, i + 1]
                return jnp.where(even, first_ref[comp], second_ref[comp])
            if face == 1:
                if i > 0:
                    return adj_ref[comp, i - 1]
                return jnp.where(even, second_ref[comp], first_ref[comp])
            if face in (2, 3):
                one = jfirst_ref[comp, i : i + 1, :]
                two = jsecond_ref[comp, i : i + 1, :]
                if face == 2:
                    line = jnp.where(jeven, one, two)
                    return jnp.where(sub == nj - 1, line, pltpu.roll(here[comp], nj - 1, 0))
                line = jnp.where(jeven, two, one)
                return jnp.where(sub == 0, line, pltpu.roll(here[comp], 1, 0))
            return edge_k(here[comp], 1 if face == 4 else -1)

        rho = flow_ref[0, i]
        m = [flow_ref[comp, i] for comp in (1, 2, 3)]
        energy = flow_ref[4, i]
        inv = 1.0 / rho
        u = [x * inv for x in m]
        uu = u[0] * u[0] + u[1] * u[1] + u[2] * u[2]
        pressure = GAS * (energy - 0.5 * (rho * uu))
        enthalpy = (energy + pressure) * inv
        sound = jnp.sqrt((1.0 + GAS) * pressure * inv)
        total = None
        for face in range(6):
            s = [faces_ref[face, axis, i] for axis in range(3)]
            h = [0.5 * (here[comp] - beside(comp, face)) for comp in range(5)]
            speed = u[0] * s[0] + u[1] * s[1] + u[2] * s[2]
            area = jnp.sqrt(s[0] * s[0] + s[1] * s[1] + s[2] * s[2])
            wave = jnp.abs(speed) + sound * area
            bulk = (u[0] * h[1] + u[1] * h[2] + u[2] * h[3]) + enthalpy * h[4]
            press = (s[0] * h[1] + s[1] * h[2] + s[2] * h[3]) + speed * h[4]
            full = h[0] + bulk
            term = [
                0.5 * GAS * (uu * press) - speed * bulk + wave * h[0],
                s[0] * full - GAS * (u[0] * press) + (speed + wave) * h[1],
                s[1] * full - GAS * (u[1] * press) + (speed + wave) * h[2],
                s[2] * full - GAS * (u[2] * press) + (speed + wave) * h[3],
                GAS * press + (speed + wave) * h[4],
            ]
            total = term if total is None else [a + b for a, b in zip(total, term)]
        for comp in range(5):
            out_ref[comp, i] = total[comp]


def call(kernel, out_shape, args, scratch=(), space=pltpu.VMEM, interpret=False):
    vmem = pl.BlockSpec(memory_space=pltpu.VMEM)
    single = not isinstance(out_shape, (list, tuple))
    held = [*args, *([out_shape] if single else out_shape), *scratch]
    need = sum(4 * math.prod(a.shape) for a in held)
    return pl.pallas_call(
        kernel,
        out_shape=out_shape,
        in_specs=[pl.BlockSpec(memory_space=space)] * len(args),
        out_specs=vmem if single else [vmem] * len(out_shape),
        scratch_shapes=list(scratch),
        interpret=interpret,
        compiler_params=pltpu.CompilerParams(vmem_limit_bytes=need + (2 << 20)),
    )(*args)


INTERPRET = False


def on_device(flow, adjoint, faces, decay, surface_mask):
    own, nj, lanes = decay.shape
    w = SWEEPS
    rows = own + 2 * w
    nby = lax.axis_size("by")

    def run(*args):
        return call(*args, interpret=INTERPRET)


    def shape(*dims):
        return jax.ShapeDtypeStruct(dims, F32)

    flat = [flow.reshape(5, own * nj, lanes), adjoint.reshape(5, own * nj, lanes)]
    flat += [decay.reshape(own * nj, lanes), surface_mask.reshape(own * nj, lanes)]
    flat = [pltpu.with_memory_space_constraint(x, pltpu.HBM) for x in flat]
    rim = shape(5 + w - 1, nj, lanes)
    flow, adjoint, retention, l1, l2, m1, m2 = run(
        functools.partial(pack_kernel, own=own, nj=nj),
        [shape(5, own * nj, lanes)] * 2
        + [shape(own * nj, lanes)]
        + [shape(5, own, lanes)] * 2
        + [rim] * 2,
        flat,
        [
            pltpu.VMEM((own * nj, lanes), F32),
            pltpu.VMEM((own * nj, lanes), jnp.int32),
            pltpu.SemaphoreType.DMA((4,)),
        ],
        pltpu.HBM,
    )
    flow, adjoint = flow.reshape(5, own, nj, lanes), adjoint.reshape(5, own, nj, lanes)
    l1, l2 = swap(l1, "by", 0), swap(l2, "by", 1, closed=True)
    m1, m2 = swap(m1, "bx", 0), swap(m2, "bx", 1)

    halo = shape(3 * w + 5, nj, lanes)
    inner, h1, h2 = run(
        functools.partial(volume_kernel, nj=nj),
        [shape(3, own, nj, lanes), halo, halo],
        [flow, adjoint, l1, l2],
    )
    h1, h2 = swap(h1, "bx", 0), swap(h2, "bx", 1)

    _, n_map = map_layout(own)
    _, n_off = off_layout(own)
    rate, gain, maps, all_coef = run(
        functools.partial(maps_kernel, rows=rows, nj=nj),
        [
            shape(nj, 2, own, lanes),
            shape(nj, 2, own, lanes),
            shape(n_map, own, lanes),
            shape(sum(map(len, REACH)), nj, own, lanes),
        ],
        [retention, m1, m2],
        [
            pltpu.VMEM((rows * nj, lanes), F32),
            pltpu.VMEM((sum(map(len, REACH[:-1])), nj, own, lanes), F32),
        ],
    )
    all_maps = collect(maps, "by")

    offs, last = run(
        functools.partial(offsets_kernel, rows=rows, nj=nj),
        [shape(n_off, own, lanes), shape(3, nj, own, lanes)],
        [inner, h1, h2, flow, adjoint, m1, m2, rate, gain],
        [pltpu.VMEM((3, rows * nj, lanes), F32), pltpu.VMEM((SWEEPS, 3, nj, 2, own, lanes), F32)],
    )
    all_offs = collect(offs, "by")

    product = run(
        functools.partial(product_kernel, nj=nj),
        jax.ShapeDtypeStruct(flow.shape, F32),
        [flow, adjoint, faces, m1, m2, l1, l2],
    )

    scratch = [
        pltpu.VMEM((SWEEPS, 3, 2, own, lanes), F32),
        pltpu.VMEM((sum(map(len, REACH)), 3, own, lanes), F32),
    ]
    if direct(nby):
        scratch += [
            pltpu.VMEM((nby, n_map, own, lanes), F32),
            pltpu.VMEM((nby, n_off, own, lanes), F32),
        ]
    warp = run(
        functools.partial(finish_kernel, own=own, nj=nj, count=nby),
        shape(3, own * nj, lanes),
        [last, all_coef, *all_maps, *all_offs],
        scratch,
    )
    return (product, warp.reshape(3, own, nj, lanes))


def solution(mesh):
    return jax.shard_map(
        on_device,
        mesh=mesh,
        in_specs=(
            P(None, "bx", "by", None),
            P(None, "bx", "by", None),
            P(None, None, "bx", "by", None),
            P("bx", "by", None),
            P("bx", "by", None),
        ),
        out_specs=(P(None, "bx", "by", None), P(None, "bx", "by", None)),
        check_vma=False,
    )
```

```python
import functools
import math

import jax
import jax.numpy as jnp
from jax import lax
from jax.experimental import pallas as pl
from jax.experimental.pallas import tpu as pltpu
from jax.sharding import PartitionSpec as P

SWEEPS = 4
KAPPA = 0.15
GAS = 0.4

F32 = jnp.float32

REACH = [[(0, 0)]]
for _ in range(SWEEPS - 1):
    REACH.append(
        sorted({(i + a, k + b) for i, k in REACH[-1] for a, b in ((1, 0), (-1, 0), (0, 1), (0, -1))})
    )


def matching(axis, first, closed):
    count = lax.axis_size(axis)
    pairs = [(i, i + 1) for i in range(first, count - 1, 2)]
    if closed and first and count % 2 == 0 and count > 2:
        pairs.append((0, count - 1))
    return pairs + [(b, a) for a, b in pairs]


def swap(x, axis, first, closed=False):
    return lax.ppermute(x, axis, matching(axis, first, closed))


def flip(x, axis, mask):
    count = lax.axis_size(axis)
    return lax.ppermute(x, axis, [(i, i ^ mask) for i in range(count)])


def direct(count):
    return count in (2, 4, 8)


def collect(x, axis):
    count = lax.axis_size(axis)
    if not direct(count):
        return [lax.all_gather(x, axis)]
    near = flip(x, axis, 1)[None]
    far = [flip(x, axis, m) for m in range(2, count, 2)]
    if not far:
        return [near]
    far = jnp.stack(far)
    return [near, far, flip(far, axis, 1)]


def sources(count):
    far = list(range(2, count, 2))
    return [[1], far, [m + 1 for m in far]] if far else [[1]]


def shift_i(x, step, n):
    if step == 0:
        return x[:n]
    size = x[0].shape[0]
    turned = [pltpu.roll(tile, (-step) % size, 0) for tile in x]
    row = lax.broadcasted_iota(jnp.int32, x[0].shape, 0)
    edge = row >= size - step if step > 0 else row < -step
    return [jnp.where(edge, turned[1 - t], turned[t]) for t in range(n)]


def roll_k(tile, step):
    return pltpu.roll(tile, (-step) % tile.shape[1], 1)


def edge_k(tile, step):
    lane = lax.broadcasted_iota(jnp.int32, tile.shape, 1)
    edge = tile.shape[1] - 1 if step > 0 else 0
    return jnp.where(lane == edge, 0.0, roll_k(tile, step))


def move(x, step, n):
    return shift_i(x, step[0], n) if step[0] else [edge_k(tile, step[1]) for tile in x[:n]]


def couple(x, n):
    up, down = shift_i(x, 1, n), shift_i(x, -1, n)
    return [(up[t] + down[t]) + (edge_k(x[t], 1) + edge_k(x[t], -1)) for t in range(n)]


def at_j(ref, j, rows, nj, tiles):
    size = rows // tiles
    return [ref[pl.ds(j + t * size * nj, size, stride=nj), :] for t in range(tiles)]


def row_valid(rows, lanes):
    own = rows - 2 * SWEEPS
    place = lax.axis_index("bx")
    above = jnp.where(place < lax.axis_size("bx") - 1, SWEEPS - 1, 0)
    below = jnp.where(place > 0, SWEEPS - 1, 0)
    row = lax.broadcasted_iota(jnp.int32, (rows, lanes), 0)
    inside = (row < own + above) | (row >= rows - below)
    valid = jnp.where(inside, 1.0, 0.0).astype(F32)
    return [valid[t * own : (t + 1) * own] for t in range(rows // own)]


def pack_kernel(
    flow_hbm, adj_hbm, decay_hbm, mask_hbm,
    flow_ref, adj_ref, rate_ref, line1_ref, line2_ref, rim1_ref, rim2_ref,
    decay_ref, mask_ref, sems, *, own, nj,
):
    pairs = [(adj_hbm, adj_ref), (decay_hbm, decay_ref), (mask_hbm, mask_ref), (flow_hbm, flow_ref)]
    copies = [pltpu.make_async_copy(a, b, sems.at[n]) for n, (a, b) in enumerate(pairs)]
    for copy in copies:
        copy.start()
    even = lax.axis_index("bx") % 2 == 0
    jeven = lax.axis_index("by") % 2 == 0
    place = lax.axis_index("by")
    inner = (place > 0) & (place < lax.axis_size("by") - 1)
    copies[0].wait()
    for comp in range(5):
        bottom = adj_ref[comp, pl.ds(0, own, stride=nj), :]
        top = adj_ref[comp, pl.ds(nj - 1, own, stride=nj), :]
        line1_ref[comp] = jnp.where(jeven, top, bottom)
        line2_ref[comp] = jnp.where(inner, jnp.where(jeven, bottom, top), 0.0)
        low = adj_ref[comp, 0:nj, :]
        high = adj_ref[comp, (own - 1) * nj : own * nj, :]
        rim1_ref[comp] = jnp.where(even, high, low)
        rim2_ref[comp] = jnp.where(even, low, high)
    copies[1].wait()
    copies[2].wait()
    rate_ref[...] = (1 - mask_ref[...]).astype(F32) * decay_ref[...]
    for row in range(SWEEPS - 1):
        low = rate_ref[row * nj : (row + 1) * nj, :]
        at = own - (SWEEPS - 1) + row
        high = rate_ref[at * nj : (at + 1) * nj, :]
        rim1_ref[5 + row] = jnp.where(even, high, low)
        rim2_ref[5 + row] = jnp.where(even, low, high)
    copies[3].wait()


def pack_rows(parts, width):
    total = parts[0]
    row = lax.broadcasted_iota(jnp.int32, total.shape, 0)
    size = total.shape[0]
    for n, part in enumerate(parts[1:], 1):
        moved = pltpu.roll(part, 2 * width * n, 0)
        place = (row - 2 * width * n + width + size) % size
        total = jnp.where(place < 2 * width, moved, total)
    return total


def unpack_rows(tile, n, width):
    return pltpu.roll(tile, (-2 * width * n) % tile.shape[0], 0) if n else tile


def layout(groups, own):
    places, at = {}, 0
    for keys, width in groups:
        for key in keys:
            places[key] = [at, None, 0, width]
            at += 1
        if width:
            share = max(1, own // (2 * width))
            for n, key in enumerate(keys):
                places[key][1] = at + n // share
                places[key][2] = n % share
            at += -(-len(keys) // share)
    return places, at


def map_layout(own):
    return layout([([(d, o) for o in REACH[d]], SWEEPS - 1 - d) for d in range(SWEEPS)], own)


def off_layout(own):
    return layout([([(s, c) for c in range(3)], SWEEPS - 1 - s) for s in range(SWEEPS)], own)


def store_tiles(ref, places, values):
    halos = {}
    for key, (main, halo, position, width) in places.items():
        ref[main] = values[key][0]
        if halo is not None:
            halos.setdefault((halo, width), []).append(values[key][1])
    for (halo, width), parts in halos.items():
        ref[halo] = pack_rows(parts, width)


def load_tiles(ref, block, place):
    main, halo, position, width = place
    tile = ref[block, main]
    if halo is None:
        return [tile]
    return [tile, unpack_rows(ref[block, halo], position, width)]


def maps_kernel(
    own_ref, first_ref, second_ref, rate_t, gain_t, map_ref, all_ref, ext_ref, side_ref, *, rows, nj,
):
    lanes = own_ref.shape[-1]
    own = rows - 2 * SWEEPS
    wide = SWEEPS - 1
    rate_ref = ext_ref
    rate_ref[0 : own * nj, :] = own_ref[...]
    even = lax.axis_index("bx") % 2 == 0
    first = first_ref[5 : 5 + wide].reshape(wide * nj, lanes)
    second = second_ref[5 : 5 + wide].reshape(wide * nj, lanes)
    rate_ref[own * nj : (own + wide) * nj, :] = jnp.where(even, first, second)
    rate_ref[(own + wide) * nj : (rows - wide) * nj, :] = jnp.zeros((2 * nj, lanes), F32)
    rate_ref[(rows - wide) * nj : rows * nj, :] = jnp.where(even, second, first)

    valid = row_valid(rows, lanes)
    for j in range(nj):
        rate = at_j(rate_ref, j, rows, nj, 2)
        for t in range(2):
            rate_t[j, t] = rate[t]
            gain_t[j, t] = KAPPA * (valid[t] - rate[t])
    places, _ = map_layout(own)
    final, at, begin = {}, 0, 0
    for d in range(SWEEPS):
        n = 1 if d == SWEEPS - 1 else 2
        index = {o: at + i for i, o in enumerate(REACH[d])}
        before = {o: begin + i for i, o in enumerate(REACH[d - 1])} if d else {}
        coef = {o: None for o in REACH[d]}
        for j in range(nj - 1, -1, -1):
            rate = [rate_t[j, t] for t in range(n)]
            if d == 0:
                old = coef[0, 0]
                coef[0, 0] = rate if old is None else [r * c for r, c in zip(rate, old)]
            else:
                total = {o: None for o in REACH[d]}
                for o, i in before.items():
                    c = [all_ref[i, j], side_ref[i, j]]
                    for step in ((1, 0), (-1, 0), (0, 1), (0, -1)):
                        moved = move(c, step, n)
                        goal = (o[0] + step[0], o[1] + step[1])
                        held = total[goal]
                        total[goal] = moved if held is None else [p + q for p, q in zip(held, moved)]
                gain = [gain_t[j, t] for t in range(n)]
                for o in REACH[d]:
                    fresh = [gain[t] * total[o][t] for t in range(n)]
                    old = coef[o]
                    if old is not None:
                        fresh = [rate[t] * old[t] + fresh[t] for t in range(n)]
                    coef[o] = fresh
            for o in REACH[d]:
                all_ref[index[o], j] = coef[o][0]
                if n == 2:
                    side_ref[index[o], j] = coef[o][1]
        final.update({(d, o): coef[o] for o in REACH[d]})
        begin, at = at, at + len(REACH[d])
    store_tiles(map_ref, places, final)


def sweeps(v_ref, rate_t, gain_t, warp_ref, rows, nj, last_ref):
    comps = v_ref.shape[0]
    ends_at = {}
    for s in range(SWEEPS):
        n = 1 if s == SWEEPS - 1 else 2
        state = [None] * comps
        for j in range(nj - 1, -1, -1):
            rate = [rate_t[j, t] for t in range(n)]
            gain = [gain_t[j, t] for t in range(n)]
            for c in range(comps):
                if s == 0:
                    before = at_j(v_ref.at[c], j, rows, nj, 2)
                    base = [gain[t] * (before[t] * (1.0 / KAPPA)) for t in range(n)]
                    for t in range(n):
                        warp_ref[SWEEPS - 1, c, j, t] = base[t]
                else:
                    before = [warp_ref[s - 1, c, j, t] for t in range(2)]
                    base = [warp_ref[SWEEPS - 1, c, j, t] for t in range(n)]
                near = couple(before, n)
                new = [base[t] + gain[t] * near[t] for t in range(n)]
                if state[c] is not None:
                    new = [new[t] + rate[t] * state[c][t] for t in range(n)]
                state[c] = new
                if s == SWEEPS - 1:
                    last_ref[c, j] = new[0]
                else:
                    for t in range(n):
                        warp_ref[s, c, j, t] = new[t]
        for c in range(comps):
            ends_at[s, c] = state[c]
    return ends_at


def volume_part(flow, jump):
    rho, m, energy = flow[0], flow[1:4], flow[4]
    inv = 1.0 / rho
    u = [x * inv for x in m]
    mu = m[0] * u[0] + m[1] * u[1] + m[2] * u[2]
    pressure = GAS * (energy - 0.5 * mu)
    q = (
        rho * jump[0]
        + (m[0] * jump[1] + m[1] * jump[2] + m[2] * jump[3])
        + (energy + pressure) * jump[4]
    )
    return [0.5 * (u[comp] * q + pressure * jump[comp + 1]) for comp in range(3)]


def volume_kernel(flow_ref, adj_ref, jfirst_ref, jsecond_ref, v_ref, out1_ref, out2_ref, *, nj):
    own, lanes = flow_ref.shape[1], flow_ref.shape[-1]
    w = SWEEPS
    even = lax.axis_index("bx") % 2 == 0
    jeven = lax.axis_index("by") % 2 == 0
    sub = lax.broadcasted_iota(jnp.int32, (nj, lanes), 0)
    for i in range(own):
        jump = []
        for comp in range(5):
            here = adj_ref[comp, i]
            if i == 0:
                diff = -adj_ref[comp, 1]
            elif i == own - 1:
                diff = adj_ref[comp, own - 2]
            else:
                diff = adj_ref[comp, i - 1] - adj_ref[comp, i + 1]
            one, two = jfirst_ref[comp, i : i + 1, :], jsecond_ref[comp, i : i + 1, :]
            back = jnp.where(sub == 0, jnp.where(jeven, two, one), pltpu.roll(here, 1, 0))
            ahead = jnp.where(
                sub == nj - 1, jnp.where(jeven, one, two), pltpu.roll(here, nj - 1, 0)
            )
            jump.append(diff + (back - ahead) + (edge_k(here, -1) - edge_k(here, 1)))
        part = volume_part([flow_ref[comp, i] for comp in range(5)], jump)
        for comp in range(3):
            v_ref[comp, i] = part[comp]
    for comp in range(3):
        low, high = v_ref[comp, 0:w], v_ref[comp, own - w : own]
        out1_ref[comp * w : (comp + 1) * w] = jnp.where(even, high, low)
        out2_ref[comp * w : (comp + 1) * w] = jnp.where(even, low, high)
    for comp in range(5):
        low, high = flow_ref[comp, 0], flow_ref[comp, own - 1]
        out1_ref[3 * w + comp] = jnp.where(even, high, low)
        out2_ref[3 * w + comp] = jnp.where(even, low, high)


def offsets_kernel(
    own_ref, first_ref, second_ref, flow_ref, adj_ref, rim1_ref, rim2_ref, rate_t, gain_t,
    off_ref, last_ref, v_ref, warp_ref, *, rows, nj,
):
    lanes = own_ref.shape[-1]
    own = rows - 2 * SWEEPS
    w = SWEEPS
    even = lax.axis_index("bx") % 2 == 0
    for comp in range(3):
        v_ref[comp, 0 : own * nj, :] = own_ref[comp].reshape(own * nj, lanes)
        one = first_ref[comp * w : (comp + 1) * w].reshape(w * nj, lanes)
        two = second_ref[comp * w : (comp + 1) * w].reshape(w * nj, lanes)
        v_ref[comp, own * nj : (own + w) * nj, :] = jnp.where(even, one, two)
        v_ref[comp, (own + w) * nj : rows * nj, :] = jnp.where(even, two, one)

    place, count = lax.axis_index("bx"), lax.axis_size("bx")
    reach = range(5)
    rim_up = [jnp.where(even, rim1_ref[c], rim2_ref[c]) for c in reach]
    rim_low = [jnp.where(even, rim2_ref[c], rim1_ref[c]) for c in reach]
    at = 3 * w
    flow_up = [jnp.where(even, first_ref[at + c], second_ref[at + c]) for c in reach]
    flow_low = [jnp.where(even, second_ref[at + c], first_ref[at + c]) for c in reach]

    def add(row, flow, adjoint, sign, inside):
        part = volume_part(flow, adjoint)
        for comp in range(3):
            lines = slice(row * nj, (row + 1) * nj)
            term = part[comp] if inside is None else jnp.where(inside, part[comp], 0.0)
            v_ref[comp, lines, :] = v_ref[comp, lines, :] + sign * term

    add(0, [flow_ref[c, 0] for c in reach], rim_low, 1.0, None)
    add(own - 1, [flow_ref[c, own - 1] for c in reach], rim_up, -1.0, None)
    add(own, flow_up, [adj_ref[c, own - 1] for c in reach], 1.0, place < count - 1)
    add(rows - 1, flow_low, [adj_ref[c, 0] for c in reach], -1.0, place > 0)

    ends_at = sweeps(v_ref, rate_t, gain_t, warp_ref, rows, nj, last_ref)
    places, _ = off_layout(own)
    store_tiles(off_ref, places, ends_at)


def finish_kernel(*refs, own, nj, count):
    last_ref, all_ref = refs[:2]
    if direct(count):
        groups = sources(count)
        n = len(groups)
        maps, offs = refs[2 : 2 + n], refs[2 + n : 2 + 2 * n]
        out_ref, x_ref, near_ref, map_ref, off_ref = refs[2 + 2 * n :]
    else:
        map_ref, off_ref, out_ref, x_ref, near_ref = refs[2:]
    me = lax.axis_index("by")
    if direct(count):
        for group, mask_list in enumerate(groups):
            for n, mask in enumerate(mask_list):
                map_ref[me ^ mask] = maps[group][n]
                off_ref[me ^ mask] = offs[group][n]
    map_places, _ = map_layout(own)
    off_places, _ = off_layout(own)

    def tiles(s):
        return 1 if s == SWEEPS - 1 else 2

    def get(s, comp):
        return [x_ref[s, comp, t] for t in range(tiles(s))]

    def shifted(x, reach, n):
        by_row = {i: shift_i(x, i, n) for i in sorted({o[0] for o in reach})}
        out = {}
        for i, k in reach:
            out[i, k] = [roll_k(tile, k) if k else tile for tile in by_row[i][:n]]
        return out

    def through(block, x):
        coef = {key: load_tiles(map_ref, block, place) for key, place in map_places.items()}
        fresh = {}
        for comp in range(3):
            total = [load_tiles(off_ref, block, off_places[s, comp]) for s in range(SWEEPS)]
            if x is not None:
                for s in range(SWEEPS):
                    for d in range(SWEEPS - s):
                        n = tiles(s + d)
                        moved = shifted(x[s, comp], REACH[d], n)
                        for t in range(n):
                            terms = [coef[d, o][t] * moved[o][t] for o in REACH[d]]
                            while len(terms) > 1:
                                pairs = [terms[i : i + 2] for i in range(0, len(terms), 2)]
                                terms = [functools.reduce(jnp.add, pair) for pair in pairs]
                            total[s + d][t] = total[s + d][t] + terms[0]
            for s in range(SWEEPS):
                fresh[s, comp] = total[s]
        return fresh

    if direct(count):
        x = None
        for block in range(count - 1, 0, -1):
            fresh = through(block, x)
            for key, value in fresh.items():
                held = [jnp.zeros_like(tile) for tile in value] if x is None else x[key]
                fresh[key] = [jnp.where(block > me, a, b) for a, b in zip(value, held)]
            x = fresh
        for (s, comp), value in x.items():
            for t, tile in enumerate(value):
                x_ref[s, comp, t] = tile
    else:

        def step(hop, carry):
            x = {(s, comp): get(s, comp) for s in range(SWEEPS) for comp in range(3)}
            for (s, comp), value in through(count - 1 - hop, x).items():
                for t, tile in enumerate(value):
                    x_ref[s, comp, t] = tile
            return carry

        x_ref[...] = jnp.zeros(x_ref.shape, F32)
        lax.fori_loop(0, count - 1 - me, step, 0)

    for comp in range(3):
        at = 0
        for d in range(SWEEPS):
            moved = shifted(get(SWEEPS - 1 - d, comp), REACH[d], 1)
            for o in REACH[d]:
                near_ref[at, comp] = moved[o][0]
                at += 1
    part = nj // 2 if nj % 2 == 0 else nj
    for begin in range(0, nj, part):
        span = range(begin, begin + part)
        total = [[last_ref[comp, j] for j in span] for comp in range(3)]
        for at in range(near_ref.shape[0]):
            moved = [near_ref[at, comp] for comp in range(3)]
            for n, j in enumerate(span):
                c = all_ref[at, j]
                for comp in range(3):
                    total[comp][n] = total[comp][n] + c * moved[comp]
        for comp in range(3):
            for n, j in enumerate(span):
                out_ref[comp, pl.ds(j, own, stride=nj), :] = total[comp][n]


def product_kernel(
    flow_ref, adj_ref, faces_ref, first_ref, second_ref, jfirst_ref, jsecond_ref, out_ref, *, nj,
):
    own, lanes = flow_ref.shape[1], flow_ref.shape[-1]
    even = lax.axis_index("bx") % 2 == 0
    jeven = lax.axis_index("by") % 2 == 0
    sub = lax.broadcasted_iota(jnp.int32, (nj, lanes), 0)
    for i in range(own):
        here = [adj_ref[comp, i] for comp in range(5)]

        def beside(comp, face):
            if face == 0:
                if i + 1 < own:
                    return adj_ref[comp, i + 1]
                return jnp.where(even, first_ref[comp], second_ref[comp])
            if face == 1:
                if i > 0:
                    return adj_ref[comp, i - 1]
                return jnp.where(even, second_ref[comp], first_ref[comp])
            if face in (2, 3):
                one = jfirst_ref[comp, i : i + 1, :]
                two = jsecond_ref[comp, i : i + 1, :]
                if face == 2:
                    line = jnp.where(jeven, one, two)
                    return jnp.where(sub == nj - 1, line, pltpu.roll(here[comp], nj - 1, 0))
                line = jnp.where(jeven, two, one)
                return jnp.where(sub == 0, line, pltpu.roll(here[comp], 1, 0))
            return edge_k(here[comp], 1 if face == 4 else -1)

        rho = flow_ref[0, i]
        m = [flow_ref[comp, i] for comp in (1, 2, 3)]
        energy = flow_ref[4, i]
        inv = 1.0 / rho
        u = [x * inv for x in m]
        uu = u[0] * u[0] + u[1] * u[1] + u[2] * u[2]
        pressure = GAS * (energy - 0.5 * (rho * uu))
        enthalpy = (energy + pressure) * inv
        sound = jnp.sqrt((1.0 + GAS) * pressure * inv)
        total = None
        for face in range(6):
            s = [faces_ref[face, axis, i] for axis in range(3)]
            h = [0.5 * (here[comp] - beside(comp, face)) for comp in range(5)]
            speed = u[0] * s[0] + u[1] * s[1] + u[2] * s[2]
            area = jnp.sqrt(s[0] * s[0] + s[1] * s[1] + s[2] * s[2])
            wave = jnp.abs(speed) + sound * area
            bulk = (u[0] * h[1] + u[1] * h[2] + u[2] * h[3]) + enthalpy * h[4]
            press = (s[0] * h[1] + s[1] * h[2] + s[2] * h[3]) + speed * h[4]
            full = h[0] + bulk
            term = [
                0.5 * GAS * (uu * press) - speed * bulk + wave * h[0],
                s[0] * full - GAS * (u[0] * press) + (speed + wave) * h[1],
                s[1] * full - GAS * (u[1] * press) + (speed + wave) * h[2],
                s[2] * full - GAS * (u[2] * press) + (speed + wave) * h[3],
                GAS * press + (speed + wave) * h[4],
            ]
            total = term if total is None else [a + b for a, b in zip(total, term)]
        for comp in range(5):
            out_ref[comp, i] = total[comp]


def call(kernel, out_shape, args, scratch=(), space=pltpu.VMEM, interpret=False):
    vmem = pl.BlockSpec(memory_space=pltpu.VMEM)
    single = not isinstance(out_shape, (list, tuple))
    held = [*args, *([out_shape] if single else out_shape), *scratch]
    need = sum(4 * math.prod(a.shape) for a in held)
    return pl.pallas_call(
        kernel,
        out_shape=out_shape,
        in_specs=[pl.BlockSpec(memory_space=space)] * len(args),
        out_specs=vmem if single else [vmem] * len(out_shape),
        scratch_shapes=list(scratch),
        interpret=interpret,
        compiler_params=pltpu.CompilerParams(vmem_limit_bytes=need + (2 << 20)),
    )(*args)


INTERPRET = False


def on_device(flow, adjoint, faces, decay, surface_mask):
    own, nj, lanes = decay.shape
    w = SWEEPS
    rows = own + 2 * w
    nby = lax.axis_size("by")

    def run(*args):
        return call(*args, interpret=INTERPRET)


    def shape(*dims):
        return jax.ShapeDtypeStruct(dims, F32)

    flat = [flow.reshape(5, own * nj, lanes), adjoint.reshape(5, own * nj, lanes)]
    flat += [decay.reshape(own * nj, lanes), surface_mask.reshape(own * nj, lanes)]
    flat = [pltpu.with_memory_space_constraint(x, pltpu.HBM) for x in flat]
    rim = shape(5 + w - 1, nj, lanes)
    flow, adjoint, retention, l1, l2, m1, m2 = run(
        functools.partial(pack_kernel, own=own, nj=nj),
        [shape(5, own * nj, lanes)] * 2
        + [shape(own * nj, lanes)]
        + [shape(5, own, lanes)] * 2
        + [rim] * 2,
        flat,
        [
            pltpu.VMEM((own * nj, lanes), F32),
            pltpu.VMEM((own * nj, lanes), jnp.int32),
            pltpu.SemaphoreType.DMA((4,)),
        ],
        pltpu.HBM,
    )
    flow, adjoint = flow.reshape(5, own, nj, lanes), adjoint.reshape(5, own, nj, lanes)
    l1, l2 = swap(l1, "by", 0), swap(l2, "by", 1, closed=True)
    m1, m2 = swap(m1, "bx", 0), swap(m2, "bx", 1)

    halo = shape(3 * w + 5, nj, lanes)
    inner, h1, h2 = run(
        functools.partial(volume_kernel, nj=nj),
        [shape(3, own, nj, lanes), halo, halo],
        [flow, adjoint, l1, l2],
    )
    h1, h2 = swap(h1, "bx", 0), swap(h2, "bx", 1)

    _, n_map = map_layout(own)
    _, n_off = off_layout(own)
    rate, gain, maps, all_coef = run(
        functools.partial(maps_kernel, rows=rows, nj=nj),
        [
            shape(nj, 2, own, lanes),
            shape(nj, 2, own, lanes),
            shape(n_map, own, lanes),
            shape(sum(map(len, REACH)), nj, own, lanes),
        ],
        [retention, m1, m2],
        [
            pltpu.VMEM((rows * nj, lanes), F32),
            pltpu.VMEM((sum(map(len, REACH[:-1])), nj, own, lanes), F32),
        ],
    )
    all_maps = collect(maps, "by")

    offs, last = run(
        functools.partial(offsets_kernel, rows=rows, nj=nj),
        [shape(n_off, own, lanes), shape(3, nj, own, lanes)],
        [inner, h1, h2, flow, adjoint, m1, m2, rate, gain],
        [pltpu.VMEM((3, rows * nj, lanes), F32), pltpu.VMEM((SWEEPS, 3, nj, 2, own, lanes), F32)],
    )
    all_offs = collect(offs, "by")

    product = run(
        functools.partial(product_kernel, nj=nj),
        jax.ShapeDtypeStruct(flow.shape, F32),
        [flow, adjoint, faces, m1, m2, l1, l2],
    )

    scratch = [
        pltpu.VMEM((SWEEPS, 3, 2, own, lanes), F32),
        pltpu.VMEM((sum(map(len, REACH)), 3, own, lanes), F32),
    ]
    if direct(nby):
        scratch += [
            pltpu.VMEM((nby, n_map, own, lanes), F32),
            pltpu.VMEM((nby, n_off, own, lanes), F32),
        ]
    warp = run(
        functools.partial(finish_kernel, own=own, nj=nj, count=nby),
        shape(3, own * nj, lanes),
        [last, all_coef, *all_maps, *all_offs],
        scratch,
    )
    return (product, warp.reshape(3, own, nj, lanes))


def solution(mesh):
    return jax.shard_map(
        on_device,
        mesh=mesh,
        in_specs=(
            P(None, "bx", "by", None),
            P(None, "bx", "by", None),
            P(None, None, "bx", "by", None),
            P("bx", "by", None),
            P("bx", "by", None),
        ),
        out_specs=(P(None, "bx", "by", None), P(None, "bx", "by", None)),
        check_vma=False,
    )
```

```python
import functools
import math

import jax
import jax.numpy as jnp
from jax import lax
from jax.experimental import pallas as pl
from jax.experimental.pallas import tpu as pltpu
from jax.sharding import PartitionSpec as P

SWEEPS = 4
KAPPA = 0.15
GAS = 0.4

F32 = jnp.float32

REACH = [[(0, 0)]]
for _ in range(SWEEPS - 1):
    REACH.append(
        sorted({(i + a, k + b) for i, k in REACH[-1] for a, b in ((1, 0), (-1, 0), (0, 1), (0, -1))})
    )


def matching(axis, first, closed):
    count = lax.axis_size(axis)
    pairs = [(i, i + 1) for i in range(first, count - 1, 2)]
    if closed and first and count % 2 == 0 and count > 2:
        pairs.append((0, count - 1))
    return pairs + [(b, a) for a, b in pairs]


def swap(x, axis, first, closed=False):
    return lax.ppermute(x, axis, matching(axis, first, closed))


def flip(x, axis, mask):
    count = lax.axis_size(axis)
    return lax.ppermute(x, axis, [(i, i ^ mask) for i in range(count)])


def direct(count):
    return count in (2, 4, 8)


def collect(x, axis):
    count = lax.axis_size(axis)
    if not direct(count):
        return [lax.all_gather(x, axis)]
    near = flip(x, axis, 1)[None]
    far = [flip(x, axis, m) for m in range(2, count, 2)]
    if not far:
        return [near]
    far = jnp.stack(far)
    return [near, far, flip(far, axis, 1)]


def sources(count):
    far = list(range(2, count, 2))
    return [[1], far, [m + 1 for m in far]] if far else [[1]]


def shift_i(x, step, n):
    if step == 0:
        return x[:n]
    size = x[0].shape[0]
    turned = [pltpu.roll(tile, (-step) % size, 0) for tile in x]
    row = lax.broadcasted_iota(jnp.int32, x[0].shape, 0)
    edge = row >= size - step if step > 0 else row < -step
    return [jnp.where(edge, turned[1 - t], turned[t]) for t in range(n)]


def roll_k(tile, step):
    return pltpu.roll(tile, (-step) % tile.shape[1], 1)


def edge_k(tile, step):
    lane = lax.broadcasted_iota(jnp.int32, tile.shape, 1)
    edge = tile.shape[1] - 1 if step > 0 else 0
    return jnp.where(lane == edge, 0.0, roll_k(tile, step))


def move(x, step, n):
    return shift_i(x, step[0], n) if step[0] else [edge_k(tile, step[1]) for tile in x[:n]]


def couple(x, n):
    up, down = shift_i(x, 1, n), shift_i(x, -1, n)
    return [(up[t] + down[t]) + (edge_k(x[t], 1) + edge_k(x[t], -1)) for t in range(n)]


def at_j(ref, j, rows, nj, tiles):
    size = rows // tiles
    return [ref[pl.ds(j + t * size * nj, size, stride=nj), :] for t in range(tiles)]


def row_valid(rows, lanes):
    own = rows - 2 * SWEEPS
    place = lax.axis_index("bx")
    above = jnp.where(place < lax.axis_size("bx") - 1, SWEEPS - 1, 0)
    below = jnp.where(place > 0, SWEEPS - 1, 0)
    row = lax.broadcasted_iota(jnp.int32, (rows, lanes), 0)
    inside = (row < own + above) | (row >= rows - below)
    valid = jnp.where(inside, 1.0, 0.0).astype(F32)
    return [valid[t * own : (t + 1) * own] for t in range(rows // own)]


def pack_kernel(
    flow_hbm, adj_hbm, decay_hbm, mask_hbm,
    flow_ref, adj_ref, rate_ref, line1_ref, line2_ref, rim1_ref, rim2_ref,
    decay_ref, mask_ref, sems, *, own, nj,
):
    pairs = [(adj_hbm, adj_ref), (decay_hbm, decay_ref), (mask_hbm, mask_ref), (flow_hbm, flow_ref)]
    copies = [pltpu.make_async_copy(a, b, sems.at[n]) for n, (a, b) in enumerate(pairs)]
    for copy in copies:
        copy.start()
    even = lax.axis_index("bx") % 2 == 0
    jeven = lax.axis_index("by") % 2 == 0
    place = lax.axis_index("by")
    inner = (place > 0) & (place < lax.axis_size("by") - 1)
    copies[0].wait()
    for comp in range(5):
        bottom = adj_ref[comp, pl.ds(0, own, stride=nj), :]
        top = adj_ref[comp, pl.ds(nj - 1, own, stride=nj), :]
        line1_ref[comp] = jnp.where(jeven, top, bottom)
        line2_ref[comp] = jnp.where(inner, jnp.where(jeven, bottom, top), 0.0)
        low = adj_ref[comp, 0:nj, :]
        high = adj_ref[comp, (own - 1) * nj : own * nj, :]
        rim1_ref[comp] = jnp.where(even, high, low)
        rim2_ref[comp] = jnp.where(even, low, high)
    copies[1].wait()
    copies[2].wait()
    rate_ref[...] = (1 - mask_ref[...]).astype(F32) * decay_ref[...]
    for row in range(SWEEPS - 1):
        low = rate_ref[row * nj : (row + 1) * nj, :]
        at = own - (SWEEPS - 1) + row
        high = rate_ref[at * nj : (at + 1) * nj, :]
        rim1_ref[5 + row] = jnp.where(even, high, low)
        rim2_ref[5 + row] = jnp.where(even, low, high)
    copies[3].wait()


def pack_rows(parts, width):
    total = parts[0]
    row = lax.broadcasted_iota(jnp.int32, total.shape, 0)
    size = total.shape[0]
    for n, part in enumerate(parts[1:], 1):
        moved = pltpu.roll(part, 2 * width * n, 0)
        place = (row - 2 * width * n + width + size) % size
        total = jnp.where(place < 2 * width, moved, total)
    return total


def unpack_rows(tile, n, width):
    return pltpu.roll(tile, (-2 * width * n) % tile.shape[0], 0) if n else tile


def layout(groups, own):
    places, at = {}, 0
    for keys, width in groups:
        for key in keys:
            places[key] = [at, None, 0, width]
            at += 1
        if width:
            share = max(1, own // (2 * width))
            for n, key in enumerate(keys):
                places[key][1] = at + n // share
                places[key][2] = n % share
            at += -(-len(keys) // share)
    return places, at


def map_layout(own):
    return layout([([(d, o) for o in REACH[d]], SWEEPS - 1 - d) for d in range(SWEEPS)], own)


def off_layout(own):
    return layout([([(s, c) for c in range(3)], SWEEPS - 1 - s) for s in range(SWEEPS)], own)


def store_tiles(ref, places, values):
    halos = {}
    for key, (main, halo, position, width) in places.items():
        ref[main] = values[key][0]
        if halo is not None:
            halos.setdefault((halo, width), []).append(values[key][1])
    for (halo, width), parts in halos.items():
        ref[halo] = pack_rows(parts, width)


def load_tiles(ref, block, place):
    main, halo, position, width = place
    tile = ref[block, main]
    if halo is None:
        return [tile]
    return [tile, unpack_rows(ref[block, halo], position, width)]


def maps_kernel(
    own_ref, first_ref, second_ref, rate_t, gain_t, map_ref, all_ref, ext_ref, side_ref, *, rows, nj,
):
    lanes = own_ref.shape[-1]
    own = rows - 2 * SWEEPS
    wide = SWEEPS - 1
    rate_ref = ext_ref
    rate_ref[0 : own * nj, :] = own_ref[...]
    even = lax.axis_index("bx") % 2 == 0
    first = first_ref[5 : 5 + wide].reshape(wide * nj, lanes)
    second = second_ref[5 : 5 + wide].reshape(wide * nj, lanes)
    rate_ref[own * nj : (own + wide) * nj, :] = jnp.where(even, first, second)
    rate_ref[(own + wide) * nj : (rows - wide) * nj, :] = jnp.zeros((2 * nj, lanes), F32)
    rate_ref[(rows - wide) * nj : rows * nj, :] = jnp.where(even, second, first)

    valid = row_valid(rows, lanes)
    for j in range(nj):
        rate = at_j(rate_ref, j, rows, nj, 2)
        for t in range(2):
            rate_t[j, t] = rate[t]
            gain_t[j, t] = KAPPA * (valid[t] - rate[t])
    places, _ = map_layout(own)
    final, at, begin = {}, 0, 0
    for d in range(SWEEPS):
        n = 1 if d == SWEEPS - 1 else 2
        index = {o: at + i for i, o in enumerate(REACH[d])}
        before = {o: begin + i for i, o in enumerate(REACH[d - 1])} if d else {}
        coef = {o: None for o in REACH[d]}
        for j in range(nj - 1, -1, -1):
            rate = [rate_t[j, t] for t in range(n)]
            if d == 0:
                old = coef[0, 0]
                coef[0, 0] = rate if old is None else [r * c for r, c in zip(rate, old)]
            else:
                total = {o: None for o in REACH[d]}
                for o, i in before.items():
                    c = [all_ref[i, j], side_ref[i, j]]
                    for step in ((1, 0), (-1, 0), (0, 1), (0, -1)):
                        moved = move(c, step, n)
                        goal = (o[0] + step[0], o[1] + step[1])
                        held = total[goal]
                        total[goal] = moved if held is None else [p + q for p, q in zip(held, moved)]
                gain = [gain_t[j, t] for t in range(n)]
                for o in REACH[d]:
                    fresh = [gain[t] * total[o][t] for t in range(n)]
                    old = coef[o]
                    if old is not None:
                        fresh = [rate[t] * old[t] + fresh[t] for t in range(n)]
                    coef[o] = fresh
            for o in REACH[d]:
                all_ref[index[o], j] = coef[o][0]
                if n == 2:
                    side_ref[index[o], j] = coef[o][1]
        final.update({(d, o): coef[o] for o in REACH[d]})
        begin, at = at, at + len(REACH[d])
    turned = {(d, o): [roll_k(t, -o[1]) if o[1] else t for t in c] for (d, o), c in final.items()}
    store_tiles(map_ref, places, turned)


def sweeps(v_ref, rate_t, gain_t, warp_ref, rows, nj, last_ref):
    comps = v_ref.shape[0]
    ends_at = {}
    for s in range(SWEEPS):
        n = 1 if s == SWEEPS - 1 else 2
        state = [None] * comps
        for j in range(nj - 1, -1, -1):
            rate = [rate_t[j, t] for t in range(n)]
            gain = [gain_t[j, t] for t in range(n)]
            for c in range(comps):
                if s == 0:
                    before = at_j(v_ref.at[c], j, rows, nj, 2)
                    base = [gain[t] * (before[t] * (1.0 / KAPPA)) for t in range(n)]
                    for t in range(n):
                        warp_ref[SWEEPS - 1, c, j, t] = base[t]
                else:
                    before = [warp_ref[s - 1, c, j, t] for t in range(2)]
                    base = [warp_ref[SWEEPS - 1, c, j, t] for t in range(n)]
                near = couple(before, n)
                new = [base[t] + gain[t] * near[t] for t in range(n)]
                if state[c] is not None:
                    new = [new[t] + rate[t] * state[c][t] for t in range(n)]
                state[c] = new
                if s == SWEEPS - 1:
                    last_ref[c, j] = new[0]
                else:
                    for t in range(n):
                        warp_ref[s, c, j, t] = new[t]
        for c in range(comps):
            ends_at[s, c] = state[c]
    return ends_at


def volume_part(flow, jump):
    rho, m, energy = flow[0], flow[1:4], flow[4]
    inv = 1.0 / rho
    u = [x * inv for x in m]
    mu = m[0] * u[0] + m[1] * u[1] + m[2] * u[2]
    pressure = GAS * (energy - 0.5 * mu)
    q = (
        rho * jump[0]
        + (m[0] * jump[1] + m[1] * jump[2] + m[2] * jump[3])
        + (energy + pressure) * jump[4]
    )
    return [0.5 * (u[comp] * q + pressure * jump[comp + 1]) for comp in range(3)]


def volume_kernel(flow_ref, adj_ref, jfirst_ref, jsecond_ref, v_ref, out1_ref, out2_ref, *, nj):
    own, lanes = flow_ref.shape[1], flow_ref.shape[-1]
    w = SWEEPS
    even = lax.axis_index("bx") % 2 == 0
    jeven = lax.axis_index("by") % 2 == 0
    sub = lax.broadcasted_iota(jnp.int32, (nj, lanes), 0)
    for i in range(own):
        jump = []
        for comp in range(5):
            here = adj_ref[comp, i]
            if i == 0:
                diff = -adj_ref[comp, 1]
            elif i == own - 1:
                diff = adj_ref[comp, own - 2]
            else:
                diff = adj_ref[comp, i - 1] - adj_ref[comp, i + 1]
            one, two = jfirst_ref[comp, i : i + 1, :], jsecond_ref[comp, i : i + 1, :]
            back = jnp.where(sub == 0, jnp.where(jeven, two, one), pltpu.roll(here, 1, 0))
            ahead = jnp.where(
                sub == nj - 1, jnp.where(jeven, one, two), pltpu.roll(here, nj - 1, 0)
            )
            jump.append(diff + (back - ahead) + (edge_k(here, -1) - edge_k(here, 1)))
        part = volume_part([flow_ref[comp, i] for comp in range(5)], jump)
        for comp in range(3):
            v_ref[comp, i] = part[comp]
    for comp in range(3):
        low, high = v_ref[comp, 0:w], v_ref[comp, own - w : own]
        out1_ref[comp * w : (comp + 1) * w] = jnp.where(even, high, low)
        out2_ref[comp * w : (comp + 1) * w] = jnp.where(even, low, high)
    for comp in range(5):
        low, high = flow_ref[comp, 0], flow_ref[comp, own - 1]
        out1_ref[3 * w + comp] = jnp.where(even, high, low)
        out2_ref[3 * w + comp] = jnp.where(even, low, high)


def offsets_kernel(
    own_ref, first_ref, second_ref, flow_ref, adj_ref, rim1_ref, rim2_ref, rate_t, gain_t,
    off_ref, last_ref, v_ref, warp_ref, *, rows, nj,
):
    lanes = own_ref.shape[-1]
    own = rows - 2 * SWEEPS
    w = SWEEPS
    even = lax.axis_index("bx") % 2 == 0
    for comp in range(3):
        v_ref[comp, 0 : own * nj, :] = own_ref[comp].reshape(own * nj, lanes)
        one = first_ref[comp * w : (comp + 1) * w].reshape(w * nj, lanes)
        two = second_ref[comp * w : (comp + 1) * w].reshape(w * nj, lanes)
        v_ref[comp, own * nj : (own + w) * nj, :] = jnp.where(even, one, two)
        v_ref[comp, (own + w) * nj : rows * nj, :] = jnp.where(even, two, one)

    place, count = lax.axis_index("bx"), lax.axis_size("bx")
    reach = range(5)
    rim_up = [jnp.where(even, rim1_ref[c], rim2_ref[c]) for c in reach]
    rim_low = [jnp.where(even, rim2_ref[c], rim1_ref[c]) for c in reach]
    at = 3 * w
    flow_up = [jnp.where(even, first_ref[at + c], second_ref[at + c]) for c in reach]
    flow_low = [jnp.where(even, second_ref[at + c], first_ref[at + c]) for c in reach]

    def add(row, flow, adjoint, sign, inside):
        part = volume_part(flow, adjoint)
        for comp in range(3):
            lines = slice(row * nj, (row + 1) * nj)
            term = part[comp] if inside is None else jnp.where(inside, part[comp], 0.0)
            v_ref[comp, lines, :] = v_ref[comp, lines, :] + sign * term

    add(0, [flow_ref[c, 0] for c in reach], rim_low, 1.0, None)
    add(own - 1, [flow_ref[c, own - 1] for c in reach], rim_up, -1.0, None)
    add(own, flow_up, [adj_ref[c, own - 1] for c in reach], 1.0, place < count - 1)
    add(rows - 1, flow_low, [adj_ref[c, 0] for c in reach], -1.0, place > 0)

    ends_at = sweeps(v_ref, rate_t, gain_t, warp_ref, rows, nj, last_ref)
    places, _ = off_layout(own)
    store_tiles(off_ref, places, ends_at)


def finish_kernel(*refs, own, nj, count):
    last_ref, all_ref = refs[:2]
    if direct(count):
        groups = sources(count)
        n = len(groups)
        maps, offs = refs[2 : 2 + n], refs[2 + n : 2 + 2 * n]
        out_ref, x_ref, near_ref, map_ref, off_ref = refs[2 + 2 * n :]
    else:
        map_ref, off_ref, out_ref, x_ref, near_ref = refs[2:]
    me = lax.axis_index("by")
    if direct(count):
        for group, mask_list in enumerate(groups):
            for n, mask in enumerate(mask_list):
                map_ref[me ^ mask] = maps[group][n]
                off_ref[me ^ mask] = offs[group][n]
    map_places, _ = map_layout(own)
    off_places, _ = off_layout(own)

    def tiles(s):
        return 1 if s == SWEEPS - 1 else 2

    def get(s, comp):
        return [x_ref[s, comp, t] for t in range(tiles(s))]

    def shifted(x, reach, n):
        by_row = {i: shift_i(x, i, n) for i in sorted({o[0] for o in reach})}
        out = {}
        for i, k in reach:
            out[i, k] = [roll_k(tile, k) if k else tile for tile in by_row[i][:n]]
        return out

    def through(block, x):
        coef = {key: load_tiles(map_ref, block, place) for key, place in map_places.items()}
        fresh = {}
        for comp in range(3):
            total = [load_tiles(off_ref, block, off_places[s, comp]) for s in range(SWEEPS)]
            if x is not None:
                sums = {}
                for s in range(SWEEPS):
                    for d in range(SWEEPS - s):
                        n = tiles(s + d)
                        for i in sorted({o[0] for o in REACH[d]}):
                            moved = shift_i(x[s, comp], i, n)
                            for k in (o[1] for o in REACH[d] if o[0] == i):
                                for t in range(n):
                                    term = coef[d, (i, k)][t] * moved[t]
                                    sums.setdefault((s + d, t, k), []).append(term)
                for (s, t, k), terms in sums.items():
                    while len(terms) > 1:
                        pairs = [terms[i : i + 2] for i in range(0, len(terms), 2)]
                        terms = [functools.reduce(jnp.add, pair) for pair in pairs]
                    total[s][t] = total[s][t] + (roll_k(terms[0], k) if k else terms[0])
            for s in range(SWEEPS):
                fresh[s, comp] = total[s]
        return fresh

    if direct(count):
        x = None
        for block in range(count - 1, 0, -1):
            fresh = through(block, x)
            for key, value in fresh.items():
                held = [jnp.zeros_like(tile) for tile in value] if x is None else x[key]
                fresh[key] = [jnp.where(block > me, a, b) for a, b in zip(value, held)]
            x = fresh
        for (s, comp), value in x.items():
            for t, tile in enumerate(value):
                x_ref[s, comp, t] = tile
    else:

        def step(hop, carry):
            x = {(s, comp): get(s, comp) for s in range(SWEEPS) for comp in range(3)}
            for (s, comp), value in through(count - 1 - hop, x).items():
                for t, tile in enumerate(value):
                    x_ref[s, comp, t] = tile
            return carry

        x_ref[...] = jnp.zeros(x_ref.shape, F32)
        lax.fori_loop(0, count - 1 - me, step, 0)

    for comp in range(3):
        at = 0
        for d in range(SWEEPS):
            moved = shifted(get(SWEEPS - 1 - d, comp), REACH[d], 1)
            for o in REACH[d]:
                near_ref[at, comp] = moved[o][0]
                at += 1
    part = nj // 2 if nj % 2 == 0 else nj
    for begin in range(0, nj, part):
        span = range(begin, begin + part)
        total = [[last_ref[comp, j] for j in span] for comp in range(3)]
        for at in range(near_ref.shape[0]):
            moved = [near_ref[at, comp] for comp in range(3)]
            for n, j in enumerate(span):
                c = all_ref[at, j]
                for comp in range(3):
                    total[comp][n] = total[comp][n] + c * moved[comp]
        for comp in range(3):
            for n, j in enumerate(span):
                out_ref[comp, pl.ds(j, own, stride=nj), :] = total[comp][n]


def product_kernel(
    flow_ref, adj_ref, faces_ref, first_ref, second_ref, jfirst_ref, jsecond_ref, out_ref, *, nj,
):
    own, lanes = flow_ref.shape[1], flow_ref.shape[-1]
    even = lax.axis_index("bx") % 2 == 0
    jeven = lax.axis_index("by") % 2 == 0
    sub = lax.broadcasted_iota(jnp.int32, (nj, lanes), 0)
    for i in range(own):
        here = [adj_ref[comp, i] for comp in range(5)]

        def beside(comp, face):
            if face == 0:
                if i + 1 < own:
                    return adj_ref[comp, i + 1]
                return jnp.where(even, first_ref[comp], second_ref[comp])
            if face == 1:
                if i > 0:
                    return adj_ref[comp, i - 1]
                return jnp.where(even, second_ref[comp], first_ref[comp])
            if face in (2, 3):
                one = jfirst_ref[comp, i : i + 1, :]
                two = jsecond_ref[comp, i : i + 1, :]
                if face == 2:
                    line = jnp.where(jeven, one, two)
                    return jnp.where(sub == nj - 1, line, pltpu.roll(here[comp], nj - 1, 0))
                line = jnp.where(jeven, two, one)
                return jnp.where(sub == 0, line, pltpu.roll(here[comp], 1, 0))
            return edge_k(here[comp], 1 if face == 4 else -1)

        rho = flow_ref[0, i]
        m = [flow_ref[comp, i] for comp in (1, 2, 3)]
        energy = flow_ref[4, i]
        inv = 1.0 / rho
        u = [x * inv for x in m]
        uu = u[0] * u[0] + u[1] * u[1] + u[2] * u[2]
        pressure = GAS * (energy - 0.5 * (rho * uu))
        enthalpy = (energy + pressure) * inv
        sound = jnp.sqrt((1.0 + GAS) * pressure * inv)
        total = None
        for face in range(6):
            s = [faces_ref[face, axis, i] for axis in range(3)]
            h = [0.5 * (here[comp] - beside(comp, face)) for comp in range(5)]
            speed = u[0] * s[0] + u[1] * s[1] + u[2] * s[2]
            area = jnp.sqrt(s[0] * s[0] + s[1] * s[1] + s[2] * s[2])
            wave = jnp.abs(speed) + sound * area
            bulk = (u[0] * h[1] + u[1] * h[2] + u[2] * h[3]) + enthalpy * h[4]
            press = (s[0] * h[1] + s[1] * h[2] + s[2] * h[3]) + speed * h[4]
            full = h[0] + bulk
            term = [
                0.5 * GAS * (uu * press) - speed * bulk + wave * h[0],
                s[0] * full - GAS * (u[0] * press) + (speed + wave) * h[1],
                s[1] * full - GAS * (u[1] * press) + (speed + wave) * h[2],
                s[2] * full - GAS * (u[2] * press) + (speed + wave) * h[3],
                GAS * press + (speed + wave) * h[4],
            ]
            total = term if total is None else [a + b for a, b in zip(total, term)]
        for comp in range(5):
            out_ref[comp, i] = total[comp]


def call(kernel, out_shape, args, scratch=(), space=pltpu.VMEM, interpret=False):
    vmem = pl.BlockSpec(memory_space=pltpu.VMEM)
    single = not isinstance(out_shape, (list, tuple))
    held = [*args, *([out_shape] if single else out_shape), *scratch]
    need = sum(4 * math.prod(a.shape) for a in held)
    return pl.pallas_call(
        kernel,
        out_shape=out_shape,
        in_specs=[pl.BlockSpec(memory_space=space)] * len(args),
        out_specs=vmem if single else [vmem] * len(out_shape),
        scratch_shapes=list(scratch),
        interpret=interpret,
        compiler_params=pltpu.CompilerParams(vmem_limit_bytes=need + (2 << 20)),
    )(*args)


INTERPRET = False


def on_device(flow, adjoint, faces, decay, surface_mask):
    own, nj, lanes = decay.shape
    w = SWEEPS
    rows = own + 2 * w
    nby = lax.axis_size("by")

    def run(*args):
        return call(*args, interpret=INTERPRET)


    def shape(*dims):
        return jax.ShapeDtypeStruct(dims, F32)

    flat = [flow.reshape(5, own * nj, lanes), adjoint.reshape(5, own * nj, lanes)]
    flat += [decay.reshape(own * nj, lanes), surface_mask.reshape(own * nj, lanes)]
    flat = [pltpu.with_memory_space_constraint(x, pltpu.HBM) for x in flat]
    rim = shape(5 + w - 1, nj, lanes)
    flow, adjoint, retention, l1, l2, m1, m2 = run(
        functools.partial(pack_kernel, own=own, nj=nj),
        [shape(5, own * nj, lanes)] * 2
        + [shape(own * nj, lanes)]
        + [shape(5, own, lanes)] * 2
        + [rim] * 2,
        flat,
        [
            pltpu.VMEM((own * nj, lanes), F32),
            pltpu.VMEM((own * nj, lanes), jnp.int32),
            pltpu.SemaphoreType.DMA((4,)),
        ],
        pltpu.HBM,
    )
    flow, adjoint = flow.reshape(5, own, nj, lanes), adjoint.reshape(5, own, nj, lanes)
    l1, l2 = swap(l1, "by", 0), swap(l2, "by", 1, closed=True)
    m1, m2 = swap(m1, "bx", 0), swap(m2, "bx", 1)

    halo = shape(3 * w + 5, nj, lanes)
    inner, h1, h2 = run(
        functools.partial(volume_kernel, nj=nj),
        [shape(3, own, nj, lanes), halo, halo],
        [flow, adjoint, l1, l2],
    )
    h1, h2 = swap(h1, "bx", 0), swap(h2, "bx", 1)

    _, n_map = map_layout(own)
    _, n_off = off_layout(own)
    rate, gain, maps, all_coef = run(
        functools.partial(maps_kernel, rows=rows, nj=nj),
        [
            shape(nj, 2, own, lanes),
            shape(nj, 2, own, lanes),
            shape(n_map, own, lanes),
            shape(sum(map(len, REACH)), nj, own, lanes),
        ],
        [retention, m1, m2],
        [
            pltpu.VMEM((rows * nj, lanes), F32),
            pltpu.VMEM((sum(map(len, REACH[:-1])), nj, own, lanes), F32),
        ],
    )
    all_maps = collect(maps, "by")

    offs, last = run(
        functools.partial(offsets_kernel, rows=rows, nj=nj),
        [shape(n_off, own, lanes), shape(3, nj, own, lanes)],
        [inner, h1, h2, flow, adjoint, m1, m2, rate, gain],
        [pltpu.VMEM((3, rows * nj, lanes), F32), pltpu.VMEM((SWEEPS, 3, nj, 2, own, lanes), F32)],
    )
    all_offs = collect(offs, "by")

    product = run(
        functools.partial(product_kernel, nj=nj),
        jax.ShapeDtypeStruct(flow.shape, F32),
        [flow, adjoint, faces, m1, m2, l1, l2],
    )

    scratch = [
        pltpu.VMEM((SWEEPS, 3, 2, own, lanes), F32),
        pltpu.VMEM((sum(map(len, REACH)), 3, own, lanes), F32),
    ]
    if direct(nby):
        scratch += [
            pltpu.VMEM((nby, n_map, own, lanes), F32),
            pltpu.VMEM((nby, n_off, own, lanes), F32),
        ]
    warp = run(
        functools.partial(finish_kernel, own=own, nj=nj, count=nby),
        shape(3, own * nj, lanes),
        [last, all_coef, *all_maps, *all_offs],
        scratch,
    )
    return (product, warp.reshape(3, own, nj, lanes))


def solution(mesh):
    return jax.shard_map(
        on_device,
        mesh=mesh,
        in_specs=(
            P(None, "bx", "by", None),
            P(None, "bx", "by", None),
            P(None, None, "bx", "by", None),
            P("bx", "by", None),
            P("bx", "by", None),
        ),
        out_specs=(P(None, "bx", "by", None), P(None, "bx", "by", None)),
        check_vma=False,
    )
```
